32 devices in a mesh: expert: 8 (over z, x), tensor: 4 (over y, core).
Axes of the slice: x: 2, y: 2, z: 4, core: 2. Of those that a mesh axis runs over, the one named last changes fastest.
Arguments:
- tokens: bfloat16 [2048, 1280], P('expert'), may hold values from -6 to 6
- segment_ids: int32 [2048], replicated, may hold values from 0 to 3, never falling along the last dimension, each value on 1 to 1024 neighbouring positions
- expert_ids: int32 [2048, 7], P('expert'), may hold values from 0 to 15, all different within a row; in each aligned block of 256 rows (0 to 255, 256 to 511, ...) at most 224 rows name the same one
- gate_values: float32 [2048, 7], P('expert'), may hold values from 0.1 to 0.3
- expert_slot: int32 [16], replicated, may hold values from 0 to 15, each once
- first_gain: float32 [1280], replicated, may hold values from 0.1 to 1.9
- second_gain: float32 [1280], replicated, may hold values from 0.1 to 1.9
- query_weight: bfloat16 [10, 2, 64, 1280], P(None, None, 'tensor'), may hold values from -0.15625 to 0.15625
- key_weight: bfloat16 [10, 2, 64, 1280], P(None, None, 'tensor'), may hold values from -0.15625 to 0.15625
- value_weight: bfloat16 [10, 2, 64, 1280], P(None, None, 'tensor'), may hold values from -0.15625 to 0.15625
- output_weight: bfloat16 [10, 2, 64, 1280], P(None, None, 'tensor'), may hold values from -2.5 to 2.5
- shared_gate: bfloat16 [896, 1280], P('tensor'), may hold values from -0.15625 to 0.15625
- shared_up: bfloat16 [896, 1280], P('tensor'), may hold values from -0.15625 to 0.15625
- shared_down: bfloat16 [896, 1280], P('tensor'), may hold values from -0.1875 to 0.1875
- routed_gate: bfloat16 [16, 896, 1280], P('expert', 'tensor'), may hold values from -0.15625 to 0.15625
- routed_up: bfloat16 [16, 896, 1280], P('expert', 'tensor'), may hold values from -0.15625 to 0.15625
- routed_down: bfloat16 [16, 896, 1280], P('expert', 'tensor'), may hold values from -0.1875 to 0.1875
- cotangent: bfloat16 [2048, 1280], P('expert'), may hold values from -6 to 6
Outputs:
- output: bfloat16 [2048, 1280], P('expert')
- input_grad: bfloat16 [2048, 1280], P('expert')
- gate_grad: float32 [2048, 7], P('expert')
- first_gain_grad: float32 [1280], P('expert')
- second_gain_grad: float32 [1280], P('expert')
- query_grad: float32 [10, 2, 64, 1280], P(None, None, 'tensor', 'expert')
- key_grad: float32 [10, 2, 64, 1280], P(None, None, 'tensor', 'expert')
- value_grad: float32 [10, 2, 64, 1280], P(None, None, 'tensor', 'expert')
- output_weight_grad: float32 [10, 2, 64, 1280], P(None, None, 'tensor', 'expert')
- shared_gate_grad: float32 [896, 1280], P('tensor', 'expert')
- shared_up_grad: float32 [896, 1280], P('tensor', 'expert')
- shared_down_grad: float32 [896, 1280], P('tensor', 'expert')
- routed_gate_grad: float32 [16, 896, 1280], P('expert', 'tensor')
- routed_up_grad: float32 [16, 896, 1280], P('expert', 'tensor')
- routed_down_grad: float32 [16, 896, 1280], P('expert', 'tensor')
The draws below stay inside these ranges and needn't reach their ends.
Inputs may be any that keep to these rules, and one draw needn't show every extreme that they name: `segment_ids`: segment ids never fall along the stream; every document has at most 1024 tokens and one has exactly 1024. `expert_ids`: A token's 7 experts are different. Within the 256 tokens of one index of expert no expert is named more than 224 times, a bound that some block reaches there. Each slot once: expert e uses the weights of slot expert_slot[e], which index expert_slot[e] // 2 of the expert axis holds.
All inputs are finite; a program needn't handle non-finite values.
Results may differ from the reference program's by a relative error of at most 0.014.
Values may be sent and summed in bfloat16 or wider, within the bound.
No kernel may reach another device: no remote copies, remote signals or barrier semaphores. Data moves between devices by JAX's collectives and lax.ppermute only.
A program may use at most 256 MiB of HBM per device.

```python
import math
import jax
import jax.numpy as jnp
import numpy as np
from jax import lax

D = 1280
HEADS = 10
HD = 128
FF = 896
TOP = 7
TOK_DEV = 256
TOKENS = 2048
EXPERTS = 16
CAP = 224
DOC_MOST = 1024
SEGMENTS = 4
N_EXPERT = 8


def with_spikes(values, rng, source, target, parts, factor):
    owner, partner = [(jnp.arange(values.shape[position]) // (values.shape[position] // parts)).reshape([-1 if axis == position else 1 for axis in range(values.ndim)]) for position in (source, target)]
    chosen = jax.random.permutation(rng, parts)[partner]
    strong = (owner == chosen) | (owner == (partner + parts // 2) % parts)
    return jnp.where(strong, factor * values, values)


def steps_of(key, dims, split, low, high):
    factor_of, own = 1.0, jax.random.fold_in(key, 6)
    for axis_at, shards_of in split:
        heights = jnp.exp(jax.random.uniform(jax.random.fold_in(own, axis_at), (shards_of,), jnp.float32, low / len(split), high / len(split)))
        factor_of = factor_of * jnp.repeat(heights, dims[axis_at] // shards_of).reshape([-1 if axis == axis_at else 1 for axis in range(len(dims))])
    return factor_of


def profile(count, total, most, lean):
    loads = [(1 << 20) // math.isqrt(rank ** lean) + 1 for rank in range(2, count + 1)]
    spare, given = total - most - (count - 1), [1] * (count - 1)
    while spare > 0:
        free = [i for i in range(count - 1) if given[i] < most]
        mass, left = sum([loads[i] for i in free]), spare
        for i in free:
            extra = min(most - given[i], max(1, left * loads[i] // mass), spare)
            given[i] = given[i] + extra
            spare = spare - extra
    return np.array([most] + given)


def ragged_sizes(rng, count, total, bound, slope):
    if count == 2:
        one = jax.random.randint(rng, (), max(1, total - bound), min(bound, total - 1) + 1)
        return jnp.stack([one, total - one])
    lengths = jnp.asarray(profile(count, total, bound, slope), jnp.int32)
    twos = (count - 1) // 2
    source_of, taker = lengths[1:1 + 2 * twos:2], lengths[2:2 + 2 * twos:2]
    slack = jnp.minimum(source_of - 1, bound - taker)
    passed = jax.random.randint(jax.random.fold_in(rng, 1), (twos,), 0, 1 << 20) % (slack + 1)
    lengths = lengths.at[1:1 + 2 * twos:2].set(source_of - passed).at[2:2 + 2 * twos:2].set(taker + passed)
    return lengths[jax.random.permutation(jax.random.fold_in(rng, 2), count)]


def deal_out(key, own, number, rows, amount, top, most, slope):
    order = jax.random.permutation(key, amount)
    crowded, ordinary = portions_of(amount, rows * top, most, slope, True), portions_of(amount, rows * top, most, slope, False)
    places = jnp.arange(amount)

    def named(tallies, turn):
        used = int((tallies > 0).sum())
        fixed = max(1, used // 4)
        moved = fixed + (places - fixed + turn * (used - fixed)) % max(1, amount - fixed)
        return jnp.zeros((amount,), jnp.int32).at[order[jnp.where(places < fixed, places, moved)]].set(jnp.asarray(tallies, jnp.int32))

    tallies = jnp.where(number % 4 == 0, named(crowded, number // 4), named(ordinary, number - number // 4 - 1))
    mixed = jax.random.permutation(jax.random.fold_in(own, 3), amount)
    giver, receiver = mixed[0:amount // 2 * 2:2], mixed[1:amount // 2 * 2:2]
    slack = jnp.minimum(tallies[giver] - 1, most - tallies[receiver]) // 2
    slack = jnp.where((giver == order[0]) | (receiver == order[0]) | (tallies[receiver] == 0), 0, jnp.maximum(slack, 0))
    moved = jax.random.randint(jax.random.fold_in(own, 4), (amount // 2,), 0, 1 << 20) % (slack + 1)
    tallies = tallies.at[giver].add(-moved).at[receiver].add(moved)
    labels = jnp.searchsorted(jnp.cumsum(tallies), jnp.arange(rows * top), side="right").astype(jnp.int32)
    table = labels.reshape(top, rows).T
    table = table[jax.random.permutation(jax.random.fold_in(own, 1), rows)]
    turn = jax.random.randint(jax.random.fold_in(own, 2), (rows, 1), 0, top)
    return jnp.take_along_axis(table, (jnp.arange(top)[None, :] + turn) % top, axis=1)


def portions_of(amount, total, bound, slope, full):
    weights = [(1 << 20) // math.isqrt(rank ** slope) + 1 for rank in range(1, amount + 1)]
    largest = bound if full else min(bound, max(-(-total // amount), total * weights[0] // sum(weights)))
    least = 1 if total - largest >= amount - 1 else 0
    given, spare = [largest] + [least] * (amount - 1), total - largest - least * (amount - 1)
    while spare > 0:
        candidates = [i for i in range(1, amount) if given[i] < largest] or [i for i in range(1, amount) if given[i] < bound]
        whole, budget = sum([weights[i] for i in candidates]), spare
        for i in candidates:
            addition = min(bound - given[i], max(1, budget * weights[i] // whole), spare)
            given[i] = given[i] + addition
            spare = spare - addition
    return np.array(given)


def gaussian(key, dims, width, reach, shards=(), kind=jnp.bfloat16):
    loudness = steps_of(key, dims, shards, -0.22, 0.18) if shards else 1.0
    entries = jax.random.normal(key, dims, jnp.float32) * width * loudness
    return jnp.minimum(jnp.maximum(entries, -reach), reach).astype(kind)


def noise_with(own_key, dims, deviation, most, split, heavy, held_as=jnp.bfloat16):
    values = deviation * jax.random.normal(own_key, dims, jnp.float32)
    if split:
        values = values * steps_of(own_key, dims, split, -0.22, 0.18)
    return jnp.clip(with_spikes(values, jax.random.fold_in(own_key, 3), *heavy), -most, most).astype(held_as)


def setup_inputs(seed: int = 0) -> dict:
    keys = jax.random.split(jax.random.key(seed), 19)
    tokens = gaussian(keys[0], (TOKENS, D), 1.0, 6.0, ((0, 8),))
    segment_ids = jnp.searchsorted(jnp.cumsum(ragged_sizes(keys[1], SEGMENTS, TOKENS, DOC_MOST, 1)), jnp.arange(TOKENS), side="right").astype(jnp.int32)
    expert_ids_keys = jax.random.split(jax.random.fold_in(keys[2], 1), TOKENS // TOK_DEV)
    expert_ids_turns = jax.random.permutation(jax.random.fold_in(keys[2], 3), TOKENS // TOK_DEV)
    expert_ids = jax.vmap(lambda own, number: deal_out(jax.random.fold_in(keys[2], 2), own, number, TOK_DEV, EXPERTS, TOP, CAP, 2))(expert_ids_keys, expert_ids_turns).reshape((TOKENS, TOP))
    gate_values = jnp.clip(0.1 + 0.20000001043081284 * jax.random.uniform(keys[3], (TOKENS, TOP), jnp.float32) ** steps_of(keys[3], (TOKENS, TOP), ((0, 8),), -0.2, 0.2), 0.1, 0.3)
    expert_slot = jax.random.permutation(keys[4], EXPERTS).astype(jnp.int32)
    first_gain = jnp.clip(1.0 + 0.18 * jax.random.normal(keys[5], (D,), jnp.float32), 0.1, 1.9)
    second_gain = jnp.clip(1.0 + 0.18 * jax.random.normal(keys[6], (D,), jnp.float32), 0.1, 1.9)
    query_weight = gaussian(keys[7], (HEADS, 2, HD // 2, D), D ** -0.5, 0.15625, ((2, 4),))
    key_weight = gaussian(keys[8], (HEADS, 2, HD // 2, D), D ** -0.5, 0.15625, ((2, 4),))
    value_weight = gaussian(keys[9], (HEADS, 2, HD // 2, D), D ** -0.5, 0.15625, ((2, 4),))
    output_weight = gaussian(keys[10], (HEADS, 2, HD // 2, D), (max(1, HEADS * HD // 256)) ** -0.5, 2.5, ((2, 4),))
    shared_gate = gaussian(keys[11], (FF, D), D ** -0.5, 0.15625, ((0, 4),))
    shared_up = gaussian(keys[12], (FF, D), D ** -0.5, 0.15625, ((0, 4),))
    shared_down = gaussian(keys[13], (FF, D), FF ** -0.5, 0.1875, ((0, 4),))
    routed_gate = gaussian(keys[14], (EXPERTS, FF, D), D ** -0.5, 0.15625, ((0, 8), (1, 4)))
    routed_up = gaussian(keys[15], (EXPERTS, FF, D), D ** -0.5, 0.15625, ((0, 8), (1, 4)))
    routed_down = gaussian(keys[16], (EXPERTS, FF, D), FF ** -0.5, 0.1875, ((0, 8), (1, 4)))
    cotangent = noise_with(keys[17], (TOKENS, D), 1.0, 6.0, ((0, 8),), (0, 1, 8, 2.0))
    return dict(tokens=tokens, segment_ids=segment_ids, expert_ids=expert_ids, gate_values=gate_values, expert_slot=expert_slot, first_gain=first_gain, second_gain=second_gain, query_weight=query_weight, key_weight=key_weight, value_weight=value_weight, output_weight=output_weight, shared_gate=shared_gate, shared_up=shared_up, shared_down=shared_down, routed_gate=routed_gate, routed_up=routed_up, routed_down=routed_down, cotangent=cotangent)


EPSILON = 1e-06
MASKED = -1e+30
HIGHEST = lax.Precision.HIGHEST

@jax.custom_vjp
def low(v):
    return lax.optimization_barrier(v.astype(jnp.bfloat16)).astype(jnp.float32)

@jax.custom_vjp
def low_back(v):
    return v

def low_keep(v):
    return (low(v), None)

def low_pass(kept, grad):
    return (grad,)

def back_keep(v):
    return (v, None)

def back_low(kept, grad):
    return (low(grad),)
low.defvjp(low_keep, low_pass)
low_back.defvjp(back_keep, back_low)

def rms_scale(values):
    return lax.rsqrt(lax.optimization_barrier(jnp.mean(values * values, axis=-1, keepdims=True)) + EPSILON)

def doc_positions(segment_ids):
    length_all = segment_ids.shape[0]
    places = jnp.arange(length_all, dtype=jnp.int32)
    is_first = jnp.concatenate([jnp.ones((1,), jnp.bool_), segment_ids[1:] != segment_ids[:-1]])
    doc_start = lax.cummax(jnp.where(is_first, places, 0), axis=0)
    return places - doc_start

def rotate(vectors, positions):
    half_size = vectors.shape[-1] // 2
    inverse_freq = 10000.0 ** (-2.0 * jnp.arange(half_size, dtype=jnp.float32) / (2 * half_size))
    angles = positions.astype(jnp.float32)[:, None] * inverse_freq[None, :]
    cosine = jnp.cos(angles)[:, None, :]
    sine_table = jnp.sin(angles)[:, None, :]
    first_half = vectors[..., :half_size]
    second_half = vectors[..., half_size:]
    return jnp.concatenate([first_half * cosine - second_half * sine_table, second_half * cosine + first_half * sine_table], axis=-1)

def attend_block(packed):
    query_block, key_window, value_window, query_seg, key_seg, query_pos, key_pos = packed
    scores = jnp.einsum('qhd,khd->hqk', query_block, key_window, precision=HIGHEST) * HD ** (-0.5)
    scores = low_back(scores)
    allowed = (query_seg[:, None] == key_seg[None, :]) & (key_pos[None, :] <= query_pos[:, None]) & (key_pos[None, :] >= 0)
    scores = jnp.where(allowed[None], scores, MASKED)
    row_max = lax.optimization_barrier(jnp.max(scores, axis=-1, keepdims=True))
    log_total = row_max + jnp.log(lax.optimization_barrier(jnp.sum(jnp.exp(scores - row_max), axis=-1, keepdims=True)))
    probs = low(jnp.exp(scores - log_total))
    return jnp.einsum('hqk,khd->qhd', probs, value_window, precision=HIGHEST)

def run_expert(packed):
    rows, gate_mat, up_mat, down_mat = packed
    gate_pre = low_back(jnp.dot(rows, gate_mat.T, precision=HIGHEST))
    up_pre = low_back(jnp.dot(rows, up_mat.T, precision=HIGHEST))
    active = low(jax.nn.silu(gate_pre) * up_pre)
    return low_back(jnp.dot(active, down_mat, precision=HIGHEST))

def forward(tokens, gate_values, first_gain, second_gain, query_weight, key_weight, value_weight, output_weight, shared_gate, shared_up, shared_down, routed_gate, routed_up, routed_down, segment_ids, expert_ids, expert_slot):
    total = tokens.shape[0]
    normed_one = low(tokens * rms_scale(tokens) * first_gain)
    positions = doc_positions(segment_ids)

    def project(weight):
        return jnp.dot(normed_one, weight.reshape(HEADS * HD, D).T, precision=HIGHEST).reshape(total, HEADS, HD)
    query = low(rotate(low_back(project(query_weight)), positions))
    key = low(rotate(low_back(project(key_weight)), positions))
    value = low(low_back(project(value_weight)))
    block_rows = min(512, total)
    block_count = total // block_rows
    window = DOC_MOST
    key_pad = jnp.concatenate([jnp.zeros((window, HEADS, HD), key.dtype), key])
    value_pad = jnp.concatenate([jnp.zeros((window, HEADS, HD), value.dtype), value])
    seg_pad = jnp.concatenate([jnp.full((window,), -1, jnp.int32), segment_ids])
    starts = jnp.arange(block_count, dtype=jnp.int32) * block_rows
    window_index = starts[:, None] + jnp.arange(window + block_rows, dtype=jnp.int32)[None, :]
    packed = (query.reshape(block_count, block_rows, HEADS, HD), key_pad[window_index], value_pad[window_index], segment_ids.reshape(block_count, block_rows), seg_pad[window_index], jnp.arange(total, dtype=jnp.int32).reshape(block_count, block_rows), window_index - window)
    attended = lax.map(jax.checkpoint(attend_block), packed)
    attended = low(low_back(attended.reshape(total, HEADS * HD)))
    attn_out = low_back(jnp.dot(attended, output_weight.reshape(HEADS * HD, D), precision=HIGHEST))
    hidden = tokens + attn_out
    normed_two = low(hidden * rms_scale(hidden) * second_gain)
    shared_gate_pre = low_back(jnp.dot(normed_two, shared_gate.T, precision=HIGHEST))
    shared_up_pre = low_back(jnp.dot(normed_two, shared_up.T, precision=HIGHEST))
    shared_act = low(jax.nn.silu(shared_gate_pre) * shared_up_pre)
    shared_out = jnp.dot(shared_act, shared_down, precision=HIGHEST)
    experts_total = expert_slot.shape[0]
    flat_ids = expert_ids.reshape(-1)
    onehot = (flat_ids[:, None] == jnp.arange(experts_total, dtype=jnp.int32)[None, :]).astype(jnp.int32)
    rank_row = lax.optimization_barrier(jnp.sum((jnp.cumsum(onehot, axis=0) - 1) * onehot, axis=1))
    room = N_EXPERT * CAP
    target = flat_ids * room + rank_row
    rows = jnp.repeat(normed_two, TOP, axis=0)
    buffer = jnp.zeros((experts_total * room, D), rows.dtype).at[target].set(rows).reshape(experts_total, room, D)
    results = lax.map(jax.checkpoint(run_expert), (buffer, routed_gate[expert_slot], routed_up[expert_slot], routed_down[expert_slot]))
    gathered = results.reshape(experts_total * room, D)[target].reshape(total, TOP, D)
    routed_out = jnp.einsum('tk,tkd->td', gate_values, gathered, precision=HIGHEST)
    return hidden + shared_out + routed_out

def reference(tokens, segment_ids, expert_ids, gate_values, expert_slot, first_gain, second_gain, query_weight, key_weight, value_weight, output_weight, shared_gate, shared_up, shared_down, routed_gate, routed_up, routed_down, cotangent):
    floats = tuple((array.astype(jnp.float32) for array in (tokens, gate_values, first_gain, second_gain, query_weight, key_weight, value_weight, output_weight, shared_gate, shared_up, shared_down, routed_gate, routed_up, routed_down)))

    def wrapped(*values):
        return forward(*values, segment_ids, expert_ids, expert_slot)
    result, pullback = jax.vjp(wrapped, *floats)
    grads = pullback(cotangent.astype(jnp.float32))
    return (result.astype(jnp.bfloat16), grads[0].astype(jnp.bfloat16), grads[1], grads[2], grads[3], grads[4], grads[5], grads[6], grads[7], grads[8], grads[9], grads[10], grads[11], grads[12], grads[13])
```

```python
import jax
import jax.numpy as jnp
from jax import lax
from jax.experimental import pallas as pl
from jax.experimental.pallas import tpu as pltpu
from jax.sharding import PartitionSpec as P

HD = 128
REACH = 4
EPSILON = 1e-06
MASKED = -1e30
BF = jnp.bfloat16
F32 = jnp.float32
BOTH = ("expert", "tensor")
VMEM_LIMIT = 60 * 1024 * 1024


def dot(a, b, ca, cb):
    return lax.dot_general(a, b, (((ca,), (cb,)), ((), ())), preferred_element_type=F32)


def whole(shape):
    zeros = (0,) * len(shape)
    return pl.BlockSpec(shape, lambda *_: zeros)


def query_groups(blocks, groups):
    cost = [min(b, REACH) + 1 for b in range(blocks)]
    most = max(cost)
    while True:
        starts, load = [0], 0
        for b in range(blocks):
            if load + cost[b] > most:
                starts.append(b)
                load = 0
            load += cost[b]
        if len(starts) <= groups:
            break
        most += 1
    return starts + [blocks] * (groups + 2 - len(starts))


def rms_scale(values):
    return lax.rsqrt(jnp.mean(values * values, axis=-1, keepdims=True) + EPSILON)


def norm_backward(grad_out, values, inverse_rms, gain_vector):
    weighted = grad_out * gain_vector
    normal = values * inverse_rms
    gain_grad = jnp.sum(grad_out * normal, axis=0)
    grad_in = inverse_rms * (
        weighted - normal * jnp.mean(normal * weighted, axis=-1, keepdims=True)
    )
    return grad_in, gain_grad


def project(tokens, gain, wq, wk, wv, cosine, sine, units, groups):
    rows, width = tokens.shape
    heads = wq.shape[0]
    hw = wq.shape[1] * wq.shape[2]
    pw = wq.shape[2]

    def body(tok, gain_ref, q_ref, k_ref, v_ref, cos_ref, sin_ref, norm_ref, send_ref):
        x = tok[...].astype(F32)
        normed = (x * rms_scale(x) * gain_ref[...]).astype(BF)
        norm_ref[...] = normed
        cos = cos_ref[...]
        sin = sin_ref[...]
        for part, w_ref in enumerate((q_ref, k_ref, v_ref)):
            pre = dot(w_ref[...], normed, 1, 1)
            for h in range(heads):
                a = pre[h * hw : h * hw + pw]
                b = pre[h * hw + pw : (h + 1) * hw]
                if part < 2:
                    a, b = a * cos - b * sin, b * cos + a * sin
                chunk = jnp.concatenate([a, b], axis=0).astype(BF)
                for unit in range(h, units, heads):
                    send_ref[unit, part * hw : (part + 1) * hw] = chunk

    flat = (heads * hw, width)
    return pl.pallas_call(
        body,
        out_shape=(
            jax.ShapeDtypeStruct((rows, width), BF),
            jax.ShapeDtypeStruct((units, 3 * hw, rows), BF),
        ),
        compiler_params=pltpu.CompilerParams(vmem_limit_bytes=VMEM_LIMIT),
        name="project",
    )(tokens, gain[None], wq.reshape(flat), wk.reshape(flat), wv.reshape(flat), cosine, sine)


def allowed_pairs(seg_col, seg_row, query_block, key_block, rows):
    wide = jnp.concatenate([seg_col] * (rows // seg_col.shape[1]), axis=1)
    same = wide == seg_row
    ahead = lax.broadcasted_iota(jnp.int32, (rows, rows), 0) - lax.broadcasted_iota(
        jnp.int32, (rows, rows), 1
    )
    return same & (ahead + (query_block - key_block) * rows >= 0)


def attend(bounds, arrived, seg_col, seg_row, most):
    blocks, quarters, chunk, rows = arrived.shape
    hw = chunk // 3
    hd = quarters * hw
    scale = HD ** (-0.5)

    def part(ref, block, which):
        return ref[block, :, which * hw : (which + 1) * hw, :].reshape(hd, rows)

    def body(bounds_ref, arr_ref, col_ref, row_ref, out_ref, lse_ref, score_ref):
        query_block = bounds_ref[0] + pl.program_id(0)

        @pl.when(query_block < bounds_ref[1])
        def _():
            query = part(arr_ref, query_block, 0)
            col = col_ref[query_block]
            low = jnp.maximum(query_block - REACH, 0)

            def first(kb, best):
                s = dot(query, part(arr_ref, kb, 1), 0, 0) * scale
                s = jnp.where(allowed_pairs(col, row_ref[kb], query_block, kb, rows), s, MASKED)
                score_ref[kb - low] = s
                return jnp.maximum(best, jnp.max(s, axis=1, keepdims=True))

            best = lax.fori_loop(low, query_block + 1, first, jnp.full((rows, 1), MASKED, F32))

            def second(kb, carry):
                total, out = carry
                p = jnp.exp(score_ref[kb - low] - best)
                total = total + jnp.sum(p, axis=1, keepdims=True)
                return total, out + dot(p.astype(BF), part(arr_ref, kb, 2), 1, 1)

            total, out = lax.fori_loop(
                low, query_block + 1, second, (jnp.zeros((rows, 1), F32), jnp.zeros((rows, hd), F32))
            )
            out_ref[query_block] = (out / total).astype(BF)
            lse_ref[query_block] = jnp.broadcast_to(best + jnp.log(total), (rows, 128))

    grid_spec = pltpu.PrefetchScalarGridSpec(
        num_scalar_prefetch=1,
        grid=(most,),
        in_specs=[whole(arrived.shape), whole(seg_col.shape), whole(seg_row.shape)],
        out_specs=[whole((blocks, rows, hd)), whole((blocks, rows, 128))],
        scratch_shapes=[pltpu.VMEM((REACH + 1, rows, rows), F32)],
    )
    return pl.pallas_call(
        body,
        grid_spec=grid_spec,
        out_shape=(
            jax.ShapeDtypeStruct((blocks, rows, hd), BF),
            jax.ShapeDtypeStruct((blocks, rows, 128), F32),
        ),
        compiler_params=pltpu.CompilerParams(vmem_limit_bytes=VMEM_LIMIT),
        name="attend",
    )(bounds, arrived, seg_col, seg_row)


def attend_back(bounds, arrived, seg_col, seg_row, lse, grad_out, most):
    blocks, quarters, chunk, rows = arrived.shape
    hw = chunk // 3
    hd = quarters * hw
    scale = HD ** (-0.5)

    def part(ref, block, which):
        return ref[block, :, which * hw : (which + 1) * hw, :].reshape(hd, rows)

    def body(bounds_ref, arr_ref, col_ref, row_ref, lse_ref, do_ref, res_ref, prob_ref, dp_ref, dk_ref, dv_ref):
        step = pl.program_id(0)
        query_block = bounds_ref[0] + step

        @pl.when(step == 0)
        def _():
            res_ref[...] = jnp.zeros(res_ref.shape, BF)
            dk_ref[...] = jnp.zeros(dk_ref.shape, F32)
            dv_ref[...] = jnp.zeros(dv_ref.shape, F32)

        @pl.when(query_block < bounds_ref[1])
        def _():
            query = part(arr_ref, query_block, 0)
            col = col_ref[query_block]
            lse_now = jnp.concatenate([lse_ref[query_block]] * (rows // 128), axis=1)
            do = do_ref[query_block]
            low = jnp.maximum(query_block - REACH, 0)

            def first(kb, inner):
                s = dot(query, part(arr_ref, kb, 1), 0, 0) * scale
                ok = allowed_pairs(col, row_ref[kb], query_block, kb, rows)
                p = jnp.where(ok, jnp.exp(jnp.where(ok, s - lse_now, 0.0)), 0.0)
                dp = dot(do, part(arr_ref, kb, 2), 1, 0)
                prob_ref[kb - low] = p
                dp_ref[kb - low] = dp
                dv_ref[kb] += dot(do, p.astype(BF), 0, 0)
                return inner + jnp.sum(p * dp, axis=1, keepdims=True)

            inner = lax.fori_loop(low, query_block + 1, first, jnp.zeros((rows, 1), F32))

            def second(kb, dq):
                ds = (prob_ref[kb - low] * (dp_ref[kb - low] - inner)).astype(BF)
                dk_ref[kb] += dot(query, ds, 1, 0)
                return dq + dot(part(arr_ref, kb, 1), ds, 1, 1)

            dq = lax.fori_loop(low, query_block + 1, second, jnp.zeros((hd, rows), F32))
            res_ref[query_block, :, 0:hw, :] = (dq * scale).astype(BF).reshape(quarters, hw, rows)

        @pl.when(step == pl.num_programs(0) - 1)
        def _():
            for b in range(blocks):
                res_ref[b, :, hw : 2 * hw, :] = (dk_ref[b] * scale).astype(BF).reshape(quarters, hw, rows)
                res_ref[b, :, 2 * hw : 3 * hw, :] = dv_ref[b].astype(BF).reshape(quarters, hw, rows)

    grid_spec = pltpu.PrefetchScalarGridSpec(
        num_scalar_prefetch=1,
        grid=(most,),
        in_specs=[
            whole(arrived.shape),
            whole(seg_col.shape),
            whole(seg_row.shape),
            whole(lse.shape),
            whole(grad_out.shape),
        ],
        out_specs=whole(arrived.shape),
        scratch_shapes=[
            pltpu.VMEM((REACH + 1, rows, rows), F32),
            pltpu.VMEM((REACH + 1, rows, rows), F32),
            pltpu.VMEM((blocks, hd, rows), F32),
            pltpu.VMEM((blocks, hd, rows), F32),
        ],
    )
    return pl.pallas_call(
        body,
        grid_spec=grid_spec,
        out_shape=jax.ShapeDtypeStruct(arrived.shape, BF),
        compiler_params=pltpu.CompilerParams(vmem_limit_bytes=VMEM_LIMIT),
        name="attend_back",
    )(bounds, arrived, seg_col, seg_row, lse, grad_out)


def weight_specs(parts, hidden, width, mats):
    return [pl.BlockSpec((1, hidden, width), lambda s, *_: (s, 0, 0))] * (parts * mats)


def down_products(grads_in, downs):
    count, width = grads_in.shape
    parts = len(downs)
    slots, hidden, _ = downs[0].shape

    def body(dy_ref, *refs):
        for k in range(parts):
            refs[parts][0, k] = dot(dy_ref[...], refs[k][0], 1, 1)

    return pl.pallas_call(
        body,
        grid=(slots,),
        in_specs=[whole(grads_in.shape)] + weight_specs(parts, hidden, width, 1),
        out_specs=pl.BlockSpec((1, parts, count, hidden), lambda s: (s, 0, 0, 0)),
        out_shape=jax.ShapeDtypeStruct((slots, parts, count, hidden), F32),
        compiler_params=pltpu.CompilerParams(vmem_limit_bytes=VMEM_LIMIT),
        name="down_products",
    )(grads_in, *downs)


def swish_parts(g, u, da):
    sig = jax.nn.sigmoid(g)
    swish = g * sig
    return swish * u, da * u * (sig * (1.0 + g * (1.0 - sig))), da * swish


def experts_first(rows_in, down_prod, gates, gate_ws, up_ws):
    count, width = rows_in.shape
    parts = len(gate_ws)
    slots, hidden, _ = gate_ws[0].shape

    def body(x_ref, da_ref, gate_ref, *refs):
        gate_w, up_w = refs[:parts], refs[parts : 2 * parts]
        act_ref, dg_ref, du_ref, gg_ref, dx_ref, acc_ref = refs[2 * parts :]
        s = pl.program_id(0)
        x = x_ref[...]
        lane = lax.broadcasted_iota(jnp.int32, (count, 128), 1)
        gate = jnp.sum(jnp.where(lane == s, gate_ref[...], 0.0), axis=1, keepdims=True)
        total = jnp.zeros((count, 1), F32)

        @pl.when(s == 0)
        def _():
            acc_ref[...] = jnp.zeros(acc_ref.shape, F32)
            gg_ref[...] = jnp.zeros(gg_ref.shape, F32)

        for k in range(parts):
            g = dot(x, gate_w[k][0], 1, 1)
            u = dot(x, up_w[k][0], 1, 1)
            da = da_ref[0, k]
            act, dg, du = swish_parts(g, u, da * gate)
            total = total + jnp.sum(act * da, axis=1, keepdims=True)
            act_ref[0, k] = (act * gate).astype(BF)
            dg_ref[0, k] = dg.astype(BF)
            du_ref[0, k] = du.astype(BF)
            acc_ref[...] += dot(dg_ref[0, k], gate_w[k][0], 1, 0) + dot(du_ref[0, k], up_w[k][0], 1, 0)

        gg_ref[...] += jnp.where(lane == s, total, 0.0)

        @pl.when(s == slots - 1)
        def _():
            dx_ref[...] = acc_ref[...].astype(BF)

    hid = jax.ShapeDtypeStruct((slots, parts, count, hidden), BF)
    hid_spec = pl.BlockSpec((1, parts, count, hidden), lambda s: (s, 0, 0, 0))
    return pl.pallas_call(
        body,
        grid=(slots,),
        in_specs=[whole(rows_in.shape), hid_spec, whole(gates.shape)]
        + weight_specs(parts, hidden, width, 2),
        out_specs=[hid_spec, hid_spec, hid_spec, whole((count, 128)), whole((count, width))],
        out_shape=(
            hid,
            hid,
            hid,
            jax.ShapeDtypeStruct((count, 128), F32),
            jax.ShapeDtypeStruct((count, width), BF),
        ),
        scratch_shapes=[pltpu.VMEM((count, width), F32)],
        compiler_params=pltpu.CompilerParams(vmem_limit_bytes=VMEM_LIMIT),
        name="experts_first",
    )(rows_in, down_prod, gates, *gate_ws, *up_ws)


def experts_second(rows_in, grads_in, act, dgate, dup, downs):
    count, width = rows_in.shape
    parts = len(downs)
    slots, hidden, _ = downs[0].shape

    def body(x_ref, dy_ref, act_ref, dg_ref, du_ref, *refs):
        down_w = refs[:parts]
        out_ref = refs[parts]
        grads = refs[parts + 1 : 4 * parts + 1]
        acc_ref = refs[4 * parts + 1]
        s = pl.program_id(0)

        @pl.when(s == 0)
        def _():
            acc_ref[...] = jnp.zeros(acc_ref.shape, F32)

        for k in range(parts):
            acc_ref[...] += dot(act_ref[0, k], down_w[k][0], 1, 0)
            grads[3 * k][0] = dot(dg_ref[0, k], x_ref[...], 0, 0).astype(BF)
            grads[3 * k + 1][0] = dot(du_ref[0, k], x_ref[...], 0, 0).astype(BF)
            grads[3 * k + 2][0] = dot(act_ref[0, k], dy_ref[...], 0, 0).astype(BF)

        @pl.when(s == slots - 1)
        def _():
            out_ref[...] = acc_ref[...].astype(BF)

    hid_spec = pl.BlockSpec((1, parts, count, hidden), lambda s: (s, 0, 0, 0))
    grad_spec = pl.BlockSpec((1, hidden, width), lambda s: (s, 0, 0))
    grad_shape = jax.ShapeDtypeStruct((slots, hidden, width), BF)
    return pl.pallas_call(
        body,
        grid=(slots,),
        in_specs=[whole(rows_in.shape), whole(grads_in.shape), hid_spec, hid_spec, hid_spec]
        + weight_specs(parts, hidden, width, 1),
        out_specs=[whole((count, width))] + [grad_spec] * (3 * parts),
        out_shape=(jax.ShapeDtypeStruct((count, width), BF),) + (grad_shape,) * (3 * parts),
        scratch_shapes=[pltpu.VMEM((count, width), F32)],
        compiler_params=pltpu.CompilerParams(vmem_limit_bytes=VMEM_LIMIT),
        name="experts_second",
    )(rows_in, grads_in, act, dgate, dup, *downs)


def shared_own(rows, grads, gate_ws, up_ws, down_ws):
    parts = len(gate_ws)

    def body(x_ref, dy_ref, *refs):
        out_ref, dx_ref = refs[3 * parts :]
        for k in range(parts):
            gw, uw, dw = refs[k], refs[parts + k], refs[2 * parts + k]
            act, dg, du = swish_parts(
                dot(x_ref[...], gw[...], 1, 1),
                dot(x_ref[...], uw[...], 1, 1),
                dot(dy_ref[...], dw[...], 1, 1),
            )
            out = dot(act.astype(BF), dw[...], 1, 0)
            dx = dot(dg.astype(BF), gw[...], 1, 0) + dot(du.astype(BF), uw[...], 1, 0)
            if k == 0:
                out_ref[...] = out
                dx_ref[...] = dx
            else:
                out_ref[...] += out
                dx_ref[...] += dx

    shape = jax.ShapeDtypeStruct(rows.shape, F32)
    return pl.pallas_call(
        body,
        out_shape=(shape, shape),
        compiler_params=pltpu.CompilerParams(vmem_limit_bytes=VMEM_LIMIT),
        name="shared_own",
    )(rows, grads, *gate_ws, *up_ws, *down_ws)


def shared_grads(rows_in, grads_in, rows_cut, grads_cut, gate_ws, up_ws, down_ws):
    parts = len(gate_ws)
    hidden = gate_ws[0].shape[0]
    cut = rows_cut.shape[1]

    def body(x_ref, dy_ref, xc_ref, dyc_ref, *refs):
        out_ref = refs[3 * parts]
        for k in range(parts):
            act, dg, du = swish_parts(
                dot(x_ref[...], refs[k][...], 1, 1),
                dot(x_ref[...], refs[parts + k][...], 1, 1),
                dot(dy_ref[...], refs[2 * parts + k][...], 1, 1),
            )
            out_ref[k, 0] = dot(dg.astype(BF), xc_ref[...], 0, 0).astype(BF)
            out_ref[k, 1] = dot(du.astype(BF), xc_ref[...], 0, 0).astype(BF)
            out_ref[k, 2] = dot(act.astype(BF), dyc_ref[...], 0, 0).astype(BF)

    return pl.pallas_call(
        body,
        out_shape=jax.ShapeDtypeStruct((parts, 3, hidden, cut), BF),
        compiler_params=pltpu.CompilerParams(vmem_limit_bytes=VMEM_LIMIT),
        name="shared_grads",
    )(rows_in, grads_in, rows_cut, grads_cut, *gate_ws, *up_ws, *down_ws)


def project_back(back, cosine, sine, normed, wq, wk, wv, groups):
    heads = wq.shape[0]
    pw = wq.shape[2]
    hw = 2 * pw
    rows, width = normed.shape
    span = heads * hw

    def body(back_ref, cos_ref, sin_ref, norm_ref, q_ref, k_ref, v_ref, wt_ref, dx_ref, grad_ref):
        cos = cos_ref[...]
        sin = sin_ref[...]
        for h in range(heads):
            total = back_ref[h].astype(F32)
            for r in range(1, groups):
                total = total + back_ref[r * heads + h].astype(F32)
            for part in range(3):
                a = total[part * hw : part * hw + pw]
                b = total[part * hw + pw : (part + 1) * hw]
                if part < 2:
                    a, b = a * cos + b * sin, b * cos - a * sin
                at = part * span + h * hw
                grad_ref[at : at + hw] = jnp.concatenate([a, b], axis=0).astype(BF)
        wt_ref[...] = dot(norm_ref[...], grad_ref[...], 0, 1).astype(BF)
        dx = dot(grad_ref[0:span], q_ref[...], 0, 0)
        dx = dx + dot(grad_ref[span : 2 * span], k_ref[...], 0, 0)
        dx_ref[...] = (dx + dot(grad_ref[2 * span :], v_ref[...], 0, 0)).astype(BF)

    flat = (span, width)
    return pl.pallas_call(
        body,
        out_shape=(
            jax.ShapeDtypeStruct((width, 3 * span), BF),
            jax.ShapeDtypeStruct((rows, width), BF),
        ),
        scratch_shapes=[pltpu.VMEM((3 * span, rows), BF)],
        compiler_params=pltpu.CompilerParams(vmem_limit_bytes=VMEM_LIMIT),
        name="project_back",
    )(back, cosine, sine, normed, wq.reshape(flat), wk.reshape(flat), wv.reshape(flat))


def after(x, *others):
    return lax.optimization_barrier((x,) + others)[0]


def added(parts):
    total = parts[0].astype(F32)
    for p in parts[1:]:
        total = total + p.astype(F32)
    return total


def swapped(x, by, size):
    return lax.ppermute(x, "tensor", [(i, i ^ by) for i in range(size)])


def exchange(x, axis):
    return lax.all_to_all(x, axis, 0, 0, tiled=True)


def spread(x, axis):
    size = lax.axis_size(axis)
    return lax.all_to_all(
        jnp.broadcast_to(x[None], (size,) + x.shape), axis, 0, 0, tiled=True
    )


def on_device(
    tokens,
    segment_ids,
    expert_ids,
    gate_values,
    expert_slot,
    first_gain,
    second_gain,
    query_weight,
    key_weight,
    value_weight,
    output_weight,
    shared_gate,
    shared_up,
    shared_down,
    routed_gate,
    routed_up,
    routed_down,
    cotangent,
):
    rows, width = tokens.shape
    top = expert_ids.shape[1]
    experts_total = expert_slot.shape[0]
    slots_local = routed_gate.shape[0]
    blocks = lax.axis_size("expert")
    quarters = lax.axis_size("tensor")
    rank = lax.axis_index("expert")
    quarter = lax.axis_index("tensor")
    heads = query_weight.shape[0]
    pair_width = query_weight.shape[2]
    hw = 2 * pair_width
    hd = quarters * hw
    units = blocks * quarters
    groups = units // heads
    own = rows // quarters
    cut = width // blocks
    starts = query_groups(blocks, groups)
    most = max(starts[i + 1] - starts[i] for i in range(groups))
    unit_group = [min(j // heads, groups) for j in range(units)]
    unit = rank * quarters + quarter
    low_table = jnp.array([starts[g] for g in unit_group], jnp.int32)
    high_table = jnp.array([starts[g + 1] if g < groups else starts[g] for g in unit_group], jnp.int32)
    bounds = jnp.stack([low_table[unit], high_table[unit]])
    block_group = jnp.array(
        [max(g for g in range(groups) if starts[g] <= b) for b in range(blocks)], jnp.int32
    )[rank]

    seg_mine = lax.dynamic_slice_in_dim(segment_ids, rank * rows, rows)
    doc_start = jnp.sum((segment_ids[:, None] < seg_mine[None, :]).astype(jnp.int32), axis=0)
    positions = rank * rows + jnp.arange(rows, dtype=jnp.int32) - doc_start
    freq_index = quarter * pair_width + jnp.arange(pair_width, dtype=jnp.int32)
    inverse_freq = 10000.0 ** (-2.0 * freq_index.astype(F32) / HD)
    angles = inverse_freq[:, None] * positions.astype(F32)[None, :]
    cosine = jnp.cos(angles)
    sine = jnp.sin(angles)
    seg_row = segment_ids.reshape(blocks, 1, rows)
    seg_col = jnp.broadcast_to(segment_ids.reshape(blocks, rows, 1), (blocks, rows, 128))

    normed_one, send = project(
        tokens, first_gain, query_weight, key_weight, value_weight, cosine, sine, units, groups
    )
    arrived = exchange(send, BOTH).reshape(blocks, quarters, 3 * hw, rows)

    def across(x):
        return swapped(x, 2, quarters)

    def beside(x):
        return swapped(x, 1, quarters)

    out_mine = output_weight.reshape(heads, hw, width)
    out_far = across(after(out_mine, normed_one))
    gate_far = across(after(routed_gate, normed_one))
    up_far = across(after(routed_up, normed_one))
    down_far = across(after(routed_down, out_far, arrived))
    out_ws = (out_mine, beside(after(out_mine, normed_one)), out_far, beside(out_far))
    gate_ws = (routed_gate, beside(after(routed_gate, normed_one)), gate_far, beside(gate_far))
    up_ws = (routed_up, beside(after(routed_up, normed_one)), up_far, beside(up_far))
    down_ws = (routed_down, beside(after(routed_down, arrived)), down_far, beside(down_far))
    out_full = jnp.zeros((heads, quarters, hw, width), BF)
    for k in range(quarters):
        out_full = lax.dynamic_update_slice(out_full, out_ws[k][:, None], (0, quarter ^ k, 0, 0))
    out_full = out_full.reshape(heads * hd, width)

    own_tokens = lax.dynamic_slice_in_dim(tokens, quarter * own, own).astype(F32)
    own_grads = lax.dynamic_slice_in_dim(cotangent, quarter * own, own)
    own_ids = lax.dynamic_slice_in_dim(expert_ids, quarter * own, own)
    own_gates = lax.dynamic_slice_in_dim(gate_values, quarter * own, own)
    onehot = own_ids[:, :, None] == jnp.arange(experts_total, dtype=jnp.int32)
    own_slots = jnp.sum(jnp.where(onehot, expert_slot[None, None, :], 0), axis=2)
    slot_hot = own_slots[:, :, None] == jnp.arange(experts_total, dtype=jnp.int32)
    dense_gates = jnp.sum(jnp.where(slot_hot, own_gates[:, :, None], 0.0), axis=1)
    gate_send = after(dense_gates, normed_one).T.reshape(blocks, slots_local, own)
    gates_in = exchange(gate_send, "expert").transpose(0, 2, 1).reshape(blocks * own, slots_local)
    gates_in = jnp.concatenate(
        [gates_in, jnp.zeros((blocks * own, 128 - slots_local), F32)], axis=1
    )
    grads_in = spread(after(own_grads, arrived), "expert").reshape(blocks * own, width)

    attended_units, lse = attend(bounds, arrived, seg_col, seg_row, most)
    back = exchange(attended_units.reshape(units, own, hd), BOTH)
    attended_heads = lax.dynamic_slice_in_dim(back, block_group * heads, heads)
    attended = attended_heads.transpose(1, 0, 2).reshape(own, heads * hd)
    hidden_state = own_tokens + jnp.dot(attended, out_full, preferred_element_type=F32)
    second_scale = rms_scale(hidden_state)
    normed_two = (hidden_state * second_scale * second_gain).astype(BF)

    rows_in = spread(normed_two, "expert").reshape(blocks * own, width)
    shared_mine = [after(w, rows_in, down_far) for w in (shared_gate, shared_up, shared_down)]
    shared_ws = []
    for w in shared_mine:
        far = across(w)
        shared_ws.append((w, beside(w), far, beside(far)))

    total_rows = blocks * own
    step = min(total_rows, 512)
    spans = [slice(c, c + step) for c in range(0, total_rows, step)]
    firsts = []
    for c in spans:
        prod = down_products(grads_in[c], down_ws)
        firsts.append(experts_first(rows_in[c], prod, gates_in[c], gate_ws, up_ws))
    grad_rows = jnp.concatenate([f[4] for f in firsts], axis=0)
    gate_sums = jnp.concatenate([f[3] for f in firsts], axis=0)
    grad_home = exchange(grad_rows.reshape(blocks, own, width), "expert")

    rows_cut = lax.dynamic_slice_in_dim(rows_in, rank * cut, cut, axis=1)
    grads_cut = lax.dynamic_slice_in_dim(grads_in, rank * cut, cut, axis=1)
    seconds = [
        experts_second(rows_in[c], grads_in[c], f[0], f[1], f[2], down_ws)
        for c, f in zip(spans, firsts)
    ]
    out_part = jnp.concatenate([s[0] for s in seconds], axis=0)
    if len(seconds) == 1:
        parts = seconds[0][1:]
    else:
        parts = [added([s[1 + i] for s in seconds]).astype(BF) for i in range(3 * quarters)]
    grad_parts = [[parts[3 * k + m] for k in range(quarters)] for m in range(3)]
    shared_out, shared_dx = shared_own(normed_two, own_grads, *shared_ws)
    shared_parts = [
        shared_grads(rows_in[c], grads_in[c], rows_cut[c], grads_cut[c], *shared_ws) for c in spans
    ]
    shared_parts = shared_parts[0] if len(spans) == 1 else added(shared_parts).astype(BF)

    grad_home = after(grad_home, out_part, shared_dx, shared_parts)
    grad_norm_two = jnp.sum(grad_home.astype(F32), axis=0) + shared_dx
    grad_full = own_grads.astype(F32)
    grad_second, second_gain_local = norm_backward(
        grad_norm_two, hidden_state, second_scale, second_gain
    )
    grad_hidden = grad_full + grad_second
    grad_attn = grad_hidden.astype(BF)
    grad_attended = jnp.einsum(
        "td,hcd->htc", grad_attn, out_full.reshape(heads, hd, width), preferred_element_type=F32
    ).astype(BF)
    do_send = jnp.concatenate([grad_attended] * groups + [grad_attended[: units - groups * heads]], axis=0)
    do_units = exchange(do_send, BOTH).reshape(blocks, rows, hd)
    out_home = exchange(after(out_part, grad_home).reshape(blocks, own, width), "expert")

    routed = []
    for m in range(3):
        g = grad_parts[m]
        to_far = (g[2].astype(F32) + beside(g[3]).astype(F32)).astype(BF)
        routed.append(added([g[0], beside(g[1]), across(to_far)]))
    shared = added([shared_parts[0]] + [swapped(shared_parts[k], k, quarters) for k in range(1, quarters)])

    grad_units = attend_back(bounds, arrived, seg_col, seg_row, lse, do_units, most)
    back_grads = exchange(grad_units.reshape(units, 3 * hw, rows), BOTH)

    att_t = after(attended, do_units).T.reshape(heads, quarters, hw, own).transpose(1, 0, 2, 3)
    att_t = exchange(att_t, "tensor")
    attn_all = spread(after(grad_attn, do_units), "tensor").reshape(quarters, own, width)
    attn_all, att_t = lax.optimization_barrier((attn_all, att_t, grad_units))[:2]
    out_grad_t = jnp.einsum(
        "qtd,qhct->dhc", attn_all, att_t.reshape(quarters, heads, hw, own), preferred_element_type=F32
    ).astype(BF)
    out_grad = exchange(out_grad_t.reshape(blocks, cut, heads * hw), "expert")

    qkv_grad_t, grad_one_part = project_back(
        back_grads, cosine, sine, normed_one, query_weight, key_weight, value_weight, groups
    )
    grad_one = jnp.sum(
        exchange(grad_one_part.reshape(quarters, own, width), "tensor").astype(F32), axis=0
    )
    qkv_grad = exchange(qkv_grad_t.reshape(blocks, cut, 3 * heads * hw), "expert")
    first_scale = rms_scale(own_tokens)
    grad_first, first_gain_local = norm_backward(grad_one, own_tokens, first_scale, first_gain)
    input_grad = spread((grad_hidden + grad_first).astype(BF), "tensor").reshape(rows, width)

    out_home = jnp.sum(after(out_home, qkv_grad_t).astype(F32), axis=0) + shared_out
    output = spread((hidden_state + out_home).astype(BF), "tensor").reshape(rows, width)
    gate_back = exchange(
        after(gate_sums, do_units)[:, :slots_local].reshape(blocks, own, slots_local).transpose(0, 2, 1),
        "expert",
    ).reshape(experts_total, own)
    gate_grad = jnp.sum(jnp.where(slot_hot, after(gate_back, grad_units).T[:, None, :], 0.0), axis=2)
    gate_grad = spread(gate_grad, "tensor").reshape(rows, top)

    gains = jnp.stack([first_gain_local, second_gain_local]).reshape(2, blocks, cut).transpose(1, 0, 2)
    gains = jnp.broadcast_to(gains[:, None], (blocks, quarters, 2, cut)).reshape(units, 2, cut)
    gains = jnp.sum(exchange(gains, BOTH), axis=0)

    out_grad = jnp.sum(out_grad.astype(F32), axis=0)
    qkv_grad = jnp.sum(qkv_grad.astype(F32), axis=0)
    weight_shape = (heads, 2, pair_width, cut)
    qkv_rows = qkv_grad.T.reshape(3, *weight_shape)
    return (
        output,
        input_grad,
        gate_grad,
        gains[0],
        gains[1],
        qkv_rows[0],
        qkv_rows[1],
        qkv_rows[2],
        out_grad.T.reshape(weight_shape),
        shared[0],
        shared[1],
        shared[2],
        routed[0],
        routed[1],
        routed[2],
    )


def solution(mesh):
    placed = (
        P("expert", None),
        P(),
        P("expert", None),
        P("expert", None),
        P(),
        P(),
        P(),
        P(None, None, "tensor", None),
        P(None, None, "tensor", None),
        P(None, None, "tensor", None),
        P(None, None, "tensor", None),
        P("tensor", None),
        P("tensor", None),
        P("tensor", None),
        P("expert", "tensor", None),
        P("expert", "tensor", None),
        P("expert", "tensor", None),
        P("expert", None),
    )
    return jax.shard_map(
        on_device,
        mesh=mesh,
        in_specs=placed,
        out_specs=(
            P("expert", None),
            P("expert", None),
            P("expert", None),
            P("expert"),
            P("expert"),
            P(None, None, "tensor", "expert"),
            P(None, None, "tensor", "expert"),
            P(None, None, "tensor", "expert"),
            P(None, None, "tensor", "expert"),
            P("tensor", "expert"),
            P("tensor", "expert"),
            P("tensor", "expert"),
            P("expert", "tensor", None),
            P("expert", "tensor", None),
            P("expert", "tensor", None),
        ),
        check_vma=False,
    )
```

```python
import jax
import jax.numpy as jnp
from jax import lax
from jax.experimental import pallas as pl
from jax.experimental.pallas import tpu as pltpu
from jax.sharding import PartitionSpec as P

HD = 128
REACH = 4
EPSILON = 1e-06
MASKED = -1e30
BF = jnp.bfloat16
F32 = jnp.float32
BOTH = ("expert", "tensor")
VMEM_LIMIT = 60 * 1024 * 1024


def dot(a, b, ca, cb):
    return lax.dot_general(a, b, (((ca,), (cb,)), ((), ())), preferred_element_type=F32)


def whole(shape):
    zeros = (0,) * len(shape)
    return pl.BlockSpec(shape, lambda *_: zeros)


def query_groups(blocks, groups):
    cost = [min(b, REACH) + 1 for b in range(blocks)]
    most = max(cost)
    while True:
        starts, load = [0], 0
        for b in range(blocks):
            if load + cost[b] > most:
                starts.append(b)
                load = 0
            load += cost[b]
        if len(starts) <= groups:
            break
        most += 1
    return starts + [blocks] * (groups + 2 - len(starts))


def rms_scale(values):
    return lax.rsqrt(jnp.mean(values * values, axis=-1, keepdims=True) + EPSILON)


def norm_backward(grad_out, values, inverse_rms, gain_vector):
    weighted = grad_out * gain_vector
    normal = values * inverse_rms
    gain_grad = jnp.sum(grad_out * normal, axis=0)
    grad_in = inverse_rms * (
        weighted - normal * jnp.mean(normal * weighted, axis=-1, keepdims=True)
    )
    return grad_in, gain_grad


def project(tokens, gain, wq, wk, wv, cosine, sine, units, groups):
    rows, width = tokens.shape
    heads = wq.shape[0]
    hw = wq.shape[1] * wq.shape[2]
    pw = wq.shape[2]

    def body(tok, gain_ref, q_ref, k_ref, v_ref, cos_ref, sin_ref, norm_ref, send_ref):
        x = tok[...].astype(F32)
        normed = (x * rms_scale(x) * gain_ref[...]).astype(BF)
        norm_ref[...] = normed
        cos = cos_ref[...]
        sin = sin_ref[...]
        for part, w_ref in enumerate((q_ref, k_ref, v_ref)):
            pre = dot(w_ref[...], normed, 1, 1)
            for h in range(heads):
                a = pre[h * hw : h * hw + pw]
                b = pre[h * hw + pw : (h + 1) * hw]
                if part < 2:
                    a, b = a * cos - b * sin, b * cos + a * sin
                chunk = jnp.concatenate([a, b], axis=0).astype(BF)
                for unit in range(h, units, heads):
                    send_ref[unit, part * hw : (part + 1) * hw] = chunk

    flat = (heads * hw, width)
    return pl.pallas_call(
        body,
        out_shape=(
            jax.ShapeDtypeStruct((rows, width), BF),
            jax.ShapeDtypeStruct((units, 3 * hw, rows), BF),
        ),
        compiler_params=pltpu.CompilerParams(vmem_limit_bytes=VMEM_LIMIT),
        name="project",
    )(tokens, gain[None], wq.reshape(flat), wk.reshape(flat), wv.reshape(flat), cosine, sine)


def allowed_pairs(seg_col, seg_row, query_block, key_block, rows):
    wide = jnp.concatenate([seg_col] * (rows // seg_col.shape[1]), axis=1)
    same = wide == seg_row
    ahead = lax.broadcasted_iota(jnp.int32, (rows, rows), 0) - lax.broadcasted_iota(
        jnp.int32, (rows, rows), 1
    )
    return same & (ahead + (query_block - key_block) * rows >= 0)


def attend(bounds, arrived, seg_col, seg_row, most):
    blocks, quarters, chunk, rows = arrived.shape
    hw = chunk // 3
    hd = quarters * hw
    scale = HD ** (-0.5)

    def part(ref, block, which):
        return ref[block, :, which * hw : (which + 1) * hw, :].reshape(hd, rows)

    def body(bounds_ref, arr_ref, col_ref, row_ref, out_ref, lse_ref, score_ref):
        query_block = bounds_ref[0] + pl.program_id(0)

        @pl.when(query_block < bounds_ref[1])
        def _():
            query = part(arr_ref, query_block, 0)
            col = col_ref[query_block]
            low = jnp.maximum(query_block - REACH, 0)

            def first(kb, best):
                s = dot(query, part(arr_ref, kb, 1), 0, 0) * scale
                s = jnp.where(allowed_pairs(col, row_ref[kb], query_block, kb, rows), s, MASKED)
                score_ref[kb - low] = s
                return jnp.maximum(best, jnp.max(s, axis=1, keepdims=True))

            best = lax.fori_loop(low, query_block + 1, first, jnp.full((rows, 1), MASKED, F32))

            def second(kb, carry):
                total, out = carry
                p = jnp.exp(score_ref[kb - low] - best)
                total = total + jnp.sum(p, axis=1, keepdims=True)
                return total, out + dot(p.astype(BF), part(arr_ref, kb, 2), 1, 1)

            total, out = lax.fori_loop(
                low, query_block + 1, second, (jnp.zeros((rows, 1), F32), jnp.zeros((rows, hd), F32))
            )
            out_ref[query_block] = (out / total).astype(BF)
            lse_ref[query_block] = jnp.broadcast_to(best + jnp.log(total), (rows, 128))

    grid_spec = pltpu.PrefetchScalarGridSpec(
        num_scalar_prefetch=1,
        grid=(most,),
        in_specs=[whole(arrived.shape), whole(seg_col.shape), whole(seg_row.shape)],
        out_specs=[whole((blocks, rows, hd)), whole((blocks, rows, 128))],
        scratch_shapes=[pltpu.VMEM((REACH + 1, rows, rows), F32)],
    )
    return pl.pallas_call(
        body,
        grid_spec=grid_spec,
        out_shape=(
            jax.ShapeDtypeStruct((blocks, rows, hd), BF),
            jax.ShapeDtypeStruct((blocks, rows, 128), F32),
        ),
        compiler_params=pltpu.CompilerParams(vmem_limit_bytes=VMEM_LIMIT),
        name="attend",
    )(bounds, arrived, seg_col, seg_row)


def attend_back(bounds, arrived, seg_col, seg_row, lse, grad_out, most):
    blocks, quarters, chunk, rows = arrived.shape
    hw = chunk // 3
    hd = quarters * hw
    scale = HD ** (-0.5)

    def part(ref, block, which):
        return ref[block, :, which * hw : (which + 1) * hw, :].reshape(hd, rows)

    def body(bounds_ref, arr_ref, col_ref, row_ref, lse_ref, do_ref, res_ref, prob_ref, dp_ref, dk_ref, dv_ref):
        step = pl.program_id(0)
        query_block = bounds_ref[0] + step

        @pl.when(step == 0)
        def _():
            res_ref[...] = jnp.zeros(res_ref.shape, BF)
            dk_ref[...] = jnp.zeros(dk_ref.shape, F32)
            dv_ref[...] = jnp.zeros(dv_ref.shape, F32)

        @pl.when(query_block < bounds_ref[1])
        def _():
            query = part(arr_ref, query_block, 0)
            col = col_ref[query_block]
            lse_now = jnp.concatenate([lse_ref[query_block]] * (rows // 128), axis=1)
            do = do_ref[query_block]
            low = jnp.maximum(query_block - REACH, 0)

            def first(kb, inner):
                s = dot(query, part(arr_ref, kb, 1), 0, 0) * scale
                ok = allowed_pairs(col, row_ref[kb], query_block, kb, rows)
                p = jnp.where(ok, jnp.exp(jnp.where(ok, s - lse_now, 0.0)), 0.0)
                dp = dot(do, part(arr_ref, kb, 2), 1, 0)
                prob_ref[kb - low] = p
                dp_ref[kb - low] = dp
                dv_ref[kb] += dot(do, p.astype(BF), 0, 0)
                return inner + jnp.sum(p * dp, axis=1, keepdims=True)

            inner = lax.fori_loop(low, query_block + 1, first, jnp.zeros((rows, 1), F32))

            def second(kb, dq):
                ds = (prob_ref[kb - low] * (dp_ref[kb - low] - inner)).astype(BF)
                dk_ref[kb] += dot(query, ds, 1, 0)
                return dq + dot(part(arr_ref, kb, 1), ds, 1, 1)

            dq = lax.fori_loop(low, query_block + 1, second, jnp.zeros((hd, rows), F32))
            res_ref[query_block, :, 0:hw, :] = (dq * scale).astype(BF).reshape(quarters, hw, rows)

        @pl.when(step == pl.num_programs(0) - 1)
        def _():
            for b in range(blocks):
                res_ref[b, :, hw : 2 * hw, :] = (dk_ref[b] * scale).astype(BF).reshape(quarters, hw, rows)
                res_ref[b, :, 2 * hw : 3 * hw, :] = dv_ref[b].astype(BF).reshape(quarters, hw, rows)

    grid_spec = pltpu.PrefetchScalarGridSpec(
        num_scalar_prefetch=1,
        grid=(most,),
        in_specs=[
            whole(arrived.shape),
            whole(seg_col.shape),
            whole(seg_row.shape),
            whole(lse.shape),
            whole(grad_out.shape),
        ],
        out_specs=whole(arrived.shape),
        scratch_shapes=[
            pltpu.VMEM((REACH + 1, rows, rows), F32),
            pltpu.VMEM((REACH + 1, rows, rows), F32),
            pltpu.VMEM((blocks, hd, rows), F32),
            pltpu.VMEM((blocks, hd, rows), F32),
        ],
    )
    return pl.pallas_call(
        body,
        grid_spec=grid_spec,
        out_shape=jax.ShapeDtypeStruct(arrived.shape, BF),
        compiler_params=pltpu.CompilerParams(vmem_limit_bytes=VMEM_LIMIT),
        name="attend_back",
    )(bounds, arrived, seg_col, seg_row, lse, grad_out)


def weight_specs(parts, hidden, width, mats):
    return [pl.BlockSpec((1, hidden, width), lambda s, *_: (s, 0, 0))] * (parts * mats)


def down_products(grads_in, downs):
    count, width = grads_in.shape
    parts = len(downs)
    slots, hidden, _ = downs[0].shape

    def body(dy_ref, *refs):
        for k in range(parts):
            refs[parts][0, k] = dot(dy_ref[...], refs[k][0], 1, 1)

    return pl.pallas_call(
        body,
        grid=(slots,),
        in_specs=[whole(grads_in.shape)] + weight_specs(parts, hidden, width, 1),
        out_specs=pl.BlockSpec((1, parts, count, hidden), lambda s: (s, 0, 0, 0)),
        out_shape=jax.ShapeDtypeStruct((slots, parts, count, hidden), F32),
        compiler_params=pltpu.CompilerParams(vmem_limit_bytes=VMEM_LIMIT),
        name="down_products",
    )(grads_in, *downs)


def swish_parts(g, u, da):
    sig = jax.nn.sigmoid(g)
    swish = g * sig
    return swish * u, da * u * (sig * (1.0 + g * (1.0 - sig))), da * swish


def experts_first(rows_in, down_prod, gates, gate_ws, up_ws, own):
    count, width = rows_in.shape
    parts = len(gate_ws)
    slots, hidden, _ = gate_ws[0].shape

    def body(x_ref, da_ref, gate_ref, *refs):
        gate_w, up_w = refs[:parts], refs[parts : 2 * parts]
        act_ref, dg_ref, du_ref, gg_ref = refs[2 * parts : 2 * parts + 4]
        dx_refs, acc_ref = refs[2 * parts + 4 : -1], refs[-1]
        s = pl.program_id(0)
        x = x_ref[...]
        lane = lax.broadcasted_iota(jnp.int32, (count, 128), 1)
        gate = jnp.sum(jnp.where(lane == s, gate_ref[...], 0.0), axis=1, keepdims=True)
        total = jnp.zeros((count, 1), F32)

        @pl.when(s == 0)
        def _():
            acc_ref[...] = jnp.zeros(acc_ref.shape, F32)
            gg_ref[...] = jnp.zeros(gg_ref.shape, F32)

        for k in range(parts):
            g = dot(x, gate_w[k][0], 1, 1)
            u = dot(x, up_w[k][0], 1, 1)
            da = da_ref[0, k]
            act, dg, du = swish_parts(g, u, da * gate)
            total = total + jnp.sum(act * da, axis=1, keepdims=True)
            act_ref[0, k] = (act * gate).astype(BF)
            dg_ref[0, k] = dg.astype(BF)
            du_ref[0, k] = du.astype(BF)
            acc_ref[...] += dot(dg_ref[0, k], gate_w[k][0], 1, 0) + dot(du_ref[0, k], up_w[k][0], 1, 0)

        gg_ref[...] += jnp.where(lane == s, total, 0.0)

        @pl.when(s == slots - 1)
        def _():
            for b, dx_ref in enumerate(dx_refs):
                dx_ref[...] = acc_ref[b * own : (b + 1) * own].astype(BF)

    hid = jax.ShapeDtypeStruct((slots, parts, count, hidden), BF)
    hid_spec = pl.BlockSpec((1, parts, count, hidden), lambda s: (s, 0, 0, 0))
    return pl.pallas_call(
        body,
        grid=(slots,),
        in_specs=[whole(rows_in.shape), hid_spec, whole(gates.shape)]
        + weight_specs(parts, hidden, width, 2),
        out_specs=[hid_spec, hid_spec, hid_spec, whole((count, 128))]
        + [whole((own, width))] * (count // own),
        out_shape=(
            hid,
            hid,
            hid,
            jax.ShapeDtypeStruct((count, 128), F32),
        )
        + (jax.ShapeDtypeStruct((own, width), BF),) * (count // own),
        scratch_shapes=[pltpu.VMEM((count, width), F32)],
        compiler_params=pltpu.CompilerParams(vmem_limit_bytes=VMEM_LIMIT),
        name="experts_first",
    )(rows_in, down_prod, gates, *gate_ws, *up_ws)


def experts_second(rows_in, grads_in, act, dgate, dup, downs, own):
    count, width = rows_in.shape
    parts = len(downs)
    slots, hidden, _ = downs[0].shape
    outs = count // own

    def body(x_ref, dy_ref, act_ref, dg_ref, du_ref, *refs):
        down_w = refs[:parts]
        out_refs = refs[parts : parts + outs]
        grads = refs[parts + outs : -1]
        acc_ref = refs[-1]
        s = pl.program_id(0)

        @pl.when(s == 0)
        def _():
            acc_ref[...] = jnp.zeros(acc_ref.shape, F32)

        for k in range(parts):
            acc_ref[...] += dot(act_ref[0, k], down_w[k][0], 1, 0)
            grads[3 * k][0] = dot(dg_ref[0, k], x_ref[...], 0, 0).astype(BF)
            grads[3 * k + 1][0] = dot(du_ref[0, k], x_ref[...], 0, 0).astype(BF)
            grads[3 * k + 2][0] = dot(act_ref[0, k], dy_ref[...], 0, 0).astype(BF)

        @pl.when(s == slots - 1)
        def _():
            for b, out_ref in enumerate(out_refs):
                out_ref[...] = acc_ref[b * own : (b + 1) * own].astype(BF)

    hid_spec = pl.BlockSpec((1, parts, count, hidden), lambda s: (s, 0, 0, 0))
    grad_spec = pl.BlockSpec((1, hidden, width), lambda s: (s, 0, 0))
    grad_shape = jax.ShapeDtypeStruct((slots, hidden, width), BF)
    return pl.pallas_call(
        body,
        grid=(slots,),
        in_specs=[whole(rows_in.shape), whole(grads_in.shape), hid_spec, hid_spec, hid_spec]
        + weight_specs(parts, hidden, width, 1),
        out_specs=[whole((own, width))] * outs + [grad_spec] * (3 * parts),
        out_shape=(jax.ShapeDtypeStruct((own, width), BF),) * outs + (grad_shape,) * (3 * parts),
        scratch_shapes=[pltpu.VMEM((count, width), F32)],
        compiler_params=pltpu.CompilerParams(vmem_limit_bytes=VMEM_LIMIT),
        name="experts_second",
    )(rows_in, grads_in, act, dgate, dup, *downs)


def shared_own(rows, grads, gate_ws, up_ws, down_ws):
    parts = len(gate_ws)

    def body(x_ref, dy_ref, *refs):
        out_ref, dx_ref = refs[3 * parts :]
        for k in range(parts):
            gw, uw, dw = refs[k], refs[parts + k], refs[2 * parts + k]
            act, dg, du = swish_parts(
                dot(x_ref[...], gw[...], 1, 1),
                dot(x_ref[...], uw[...], 1, 1),
                dot(dy_ref[...], dw[...], 1, 1),
            )
            out = dot(act.astype(BF), dw[...], 1, 0)
            dx = dot(dg.astype(BF), gw[...], 1, 0) + dot(du.astype(BF), uw[...], 1, 0)
            if k == 0:
                out_ref[...] = out
                dx_ref[...] = dx
            else:
                out_ref[...] += out
                dx_ref[...] += dx

    shape = jax.ShapeDtypeStruct(rows.shape, F32)
    return pl.pallas_call(
        body,
        out_shape=(shape, shape),
        compiler_params=pltpu.CompilerParams(vmem_limit_bytes=VMEM_LIMIT),
        name="shared_own",
    )(rows, grads, *gate_ws, *up_ws, *down_ws)


def shared_grads(rows_in, grads_in, rows_cut, grads_cut, gate_ws, up_ws, down_ws):
    parts = len(gate_ws)
    hidden = gate_ws[0].shape[0]
    cut = rows_cut.shape[1]

    def body(x_ref, dy_ref, xc_ref, dyc_ref, *refs):
        out_ref = refs[3 * parts]
        for k in range(parts):
            act, dg, du = swish_parts(
                dot(x_ref[...], refs[k][...], 1, 1),
                dot(x_ref[...], refs[parts + k][...], 1, 1),
                dot(dy_ref[...], refs[2 * parts + k][...], 1, 1),
            )
            out_ref[k, 0] = dot(dg.astype(BF), xc_ref[...], 0, 0).astype(BF)
            out_ref[k, 1] = dot(du.astype(BF), xc_ref[...], 0, 0).astype(BF)
            out_ref[k, 2] = dot(act.astype(BF), dyc_ref[...], 0, 0).astype(BF)

    return pl.pallas_call(
        body,
        out_shape=jax.ShapeDtypeStruct((parts, 3, hidden, cut), BF),
        compiler_params=pltpu.CompilerParams(vmem_limit_bytes=VMEM_LIMIT),
        name="shared_grads",
    )(rows_in, grads_in, rows_cut, grads_cut, *gate_ws, *up_ws, *down_ws)


def store_chunks(place_ref, value, low_ref, high_ref):
    half, cut, _ = low_ref.shape
    for c in range(half):
        first = value[2 * c * cut : (2 * c + 1) * cut]
        second = value[(2 * c + 1) * cut : (2 * c + 2) * cut]
        at = place_ref[0] ^ c
        even = place_ref[1] == 0
        low_ref[at] = jnp.where(even, first, second).astype(BF)
        high_ref[at] = jnp.where(even, second, first).astype(BF)


def output_grads(place, attn_parts, att_parts, heads, hw, blocks):
    parts = len(attn_parts)
    own, width = attn_parts[0].shape
    span = heads * hw
    full = att_parts[0].shape[1]
    hd = full // heads

    def body(place_ref, *refs):
        low_ref, high_ref = refs[2 * parts :]
        attn = jnp.concatenate([r[...] for r in refs[:parts]], axis=0)
        att = jnp.concatenate([r[...] for r in refs[parts : 2 * parts]], axis=0)
        row = lax.broadcasted_iota(jnp.int32, (full, span), 0)
        col = lax.broadcasted_iota(jnp.int32, (full, span), 1)
        source = (col // hw) * hd + place_ref[2] * hw + col % hw
        pick = jnp.where(row == source, 1.0, 0.0).astype(BF)
        mine = dot(att, pick, 1, 0).astype(BF)
        store_chunks(place_ref, dot(attn, mine, 0, 0), low_ref, high_ref)

    shape = (blocks // 2, width // blocks, span)
    return pl.pallas_call(
        body,
        grid_spec=pltpu.PrefetchScalarGridSpec(
            num_scalar_prefetch=1,
            grid=(1,),
            in_specs=[whole((own, width))] * parts + [whole((own, full))] * parts,
            out_specs=[whole(shape)] * 2,
        ),
        out_shape=(jax.ShapeDtypeStruct(shape, BF),) * 2,
        compiler_params=pltpu.CompilerParams(vmem_limit_bytes=VMEM_LIMIT),
        name="output_grads",
    )(place, *attn_parts, *att_parts)


def project_back(place, back, cosine, sine, normed, wq, wk, wv, groups, blocks, quarters):
    heads = wq.shape[0]
    pw = wq.shape[2]
    hw = 2 * pw
    rows, width = normed.shape
    own = rows // quarters
    span = heads * hw

    def body(place_ref, back_ref, cos_ref, sin_ref, norm_ref, q_ref, k_ref, v_ref, *refs):
        dx_ref = refs[0]
        chunk_refs = refs[1:-1]
        grad_ref = refs[-1]
        cos = cos_ref[...]
        sin = sin_ref[...]
        for h in range(heads):
            total = back_ref[h].astype(F32)
            for r in range(1, groups):
                total = total + back_ref[r * heads + h].astype(F32)
            for part in range(3):
                a = total[part * hw : part * hw + pw]
                b = total[part * hw + pw : (part + 1) * hw]
                if part < 2:
                    a, b = a * cos + b * sin, b * cos - a * sin
                at = part * span + h * hw
                grad_ref[at : at + hw] = jnp.concatenate([a, b], axis=0).astype(BF)
        for part in range(3):
            value = dot(norm_ref[...], grad_ref[part * span : (part + 1) * span], 0, 1)
            store_chunks(place_ref, value, chunk_refs[2 * part], chunk_refs[2 * part + 1])
        dx = dot(grad_ref[0:span], q_ref[...], 0, 0)
        dx = dx + dot(grad_ref[span : 2 * span], k_ref[...], 0, 0)
        dx = dx + dot(grad_ref[2 * span :], v_ref[...], 0, 0)
        for j in range(quarters):
            dx_ref[place_ref[2] ^ j] = dx[j * own : (j + 1) * own].astype(BF)

    flat = (span, width)
    chunk = (blocks // 2, width // blocks, span)
    return pl.pallas_call(
        body,
        grid_spec=pltpu.PrefetchScalarGridSpec(
            num_scalar_prefetch=1,
            grid=(1,),
            in_specs=[
                whole(back.shape),
                whole(cosine.shape),
                whole(sine.shape),
                whole(normed.shape),
                whole(flat),
                whole(flat),
                whole(flat),
            ],
            out_specs=[whole((quarters, own, width))] + [whole(chunk)] * 6,
            scratch_shapes=[pltpu.VMEM((3 * span, rows), BF)],
        ),
        out_shape=(jax.ShapeDtypeStruct((quarters, own, width), BF),)
        + (jax.ShapeDtypeStruct(chunk, BF),) * 6,
        compiler_params=pltpu.CompilerParams(vmem_limit_bytes=VMEM_LIMIT),
        name="project_back",
    )(place, back, cosine, sine, normed, wq.reshape(flat), wk.reshape(flat), wv.reshape(flat))


def after(x, *others):
    return lax.optimization_barrier((x,) + others)[0]


def added(parts):
    total = parts[0].astype(F32)
    for p in parts[1:]:
        total = total + p.astype(F32)
    return total


def flip(x, by, axis):
    size = lax.axis_size(axis)
    return lax.ppermute(x, axis, [(i, i ^ by) for i in range(size)])


def exchange(x, axis):
    return lax.all_to_all(x, axis, 0, 0, tiled=True)


def even_blocks(x):
    size = lax.axis_size("expert")
    return [x] + [flip(x, m, "expert") for m in range(2, size, 2)]


def odd_blocks(evens):
    return [flip(x, 1, "expert") for x in evens]


def paired(evens, odds):
    return [
        (a.astype(F32) + flip(b, 1, "expert").astype(F32)).astype(BF) for a, b in zip(evens, odds)
    ]


def collected(sums):
    return added([sums[0]] + [flip(sums[j], 2 * j, "expert") for j in range(1, len(sums))])


def of_quarters(x):
    quarters = lax.axis_size("tensor")
    return [x] + [flip(x, k, "tensor") for k in range(1, quarters)]


def in_order(parts, quarter):
    out = jnp.zeros((len(parts),) + parts[0].shape, parts[0].dtype)
    for k, p in enumerate(parts):
        out = lax.dynamic_update_slice(out, p[None], (quarter ^ k,) + (0,) * p.ndim)
    return out.reshape((-1,) + parts[0].shape[1:])


def on_device(
    tokens,
    segment_ids,
    expert_ids,
    gate_values,
    expert_slot,
    first_gain,
    second_gain,
    query_weight,
    key_weight,
    value_weight,
    output_weight,
    shared_gate,
    shared_up,
    shared_down,
    routed_gate,
    routed_up,
    routed_down,
    cotangent,
):
    rows, width = tokens.shape
    top = expert_ids.shape[1]
    experts_total = expert_slot.shape[0]
    slots_local = routed_gate.shape[0]
    blocks = lax.axis_size("expert")
    quarters = lax.axis_size("tensor")
    rank = lax.axis_index("expert")
    quarter = lax.axis_index("tensor")
    heads = query_weight.shape[0]
    pair_width = query_weight.shape[2]
    hw = 2 * pair_width
    hd = quarters * hw
    units = blocks * quarters
    groups = units // heads
    own = rows // quarters
    cut = width // blocks
    starts = query_groups(blocks, groups)
    most = max(starts[i + 1] - starts[i] for i in range(groups))
    unit_group = [min(j // heads, groups) for j in range(units)]
    unit = rank * quarters + quarter
    low_table = jnp.array([starts[g] for g in unit_group], jnp.int32)
    high_table = jnp.array([starts[g + 1] if g < groups else starts[g] for g in unit_group], jnp.int32)
    bounds = jnp.stack([low_table[unit], high_table[unit]])
    block_group = jnp.array(
        [max(g for g in range(groups) if starts[g] <= b) for b in range(blocks)], jnp.int32
    )[rank]

    seg_mine = lax.dynamic_slice_in_dim(segment_ids, rank * rows, rows)
    doc_start = jnp.sum((segment_ids[:, None] < seg_mine[None, :]).astype(jnp.int32), axis=0)
    positions = rank * rows + jnp.arange(rows, dtype=jnp.int32) - doc_start
    freq_index = quarter * pair_width + jnp.arange(pair_width, dtype=jnp.int32)
    inverse_freq = 10000.0 ** (-2.0 * freq_index.astype(F32) / HD)
    angles = inverse_freq[:, None] * positions.astype(F32)[None, :]
    cosine = jnp.cos(angles)
    sine = jnp.sin(angles)
    seg_row = segment_ids.reshape(blocks, 1, rows)
    seg_col = jnp.broadcast_to(segment_ids.reshape(blocks, rows, 1), (blocks, rows, 128))

    normed_one, send = project(
        tokens, first_gain, query_weight, key_weight, value_weight, cosine, sine, units, groups
    )
    arrived = exchange(send, BOTH).reshape(blocks, quarters, 3 * hw, rows)

    def across(x):
        return flip(x, 2, "tensor")

    def beside(x):
        return flip(x, 1, "tensor")

    def all_quarters(x, far):
        return (x, beside(x), far, beside(far))

    out_mine = after(output_weight.reshape(heads, hw, width), normed_one)
    out_far = across(out_mine)
    gate_mine = after(routed_gate, out_far)
    gate_far = across(gate_mine)
    arrived = after(arrived, out_far)
    up_mine = after(routed_up, arrived)
    up_far = across(up_mine)
    out_ws = all_quarters(out_mine, out_far)
    out_full = jnp.zeros((heads, quarters, hw, width), BF)
    for k in range(quarters):
        out_full = lax.dynamic_update_slice(out_full, out_ws[k][:, None], (0, quarter ^ k, 0, 0))
    out_full = out_full.reshape(heads * hd, width)

    own_tokens = lax.dynamic_slice_in_dim(tokens, quarter * own, own).astype(F32)
    own_grads = lax.dynamic_slice_in_dim(cotangent, quarter * own, own)
    own_ids = lax.dynamic_slice_in_dim(expert_ids, quarter * own, own)
    own_gates = lax.dynamic_slice_in_dim(gate_values, quarter * own, own)
    onehot = own_ids[:, :, None] == jnp.arange(experts_total, dtype=jnp.int32)
    own_slots = jnp.sum(jnp.where(onehot, expert_slot[None, None, :], 0), axis=2)
    slot_hot = own_slots[:, :, None] == jnp.arange(experts_total, dtype=jnp.int32)
    dense_gates = jnp.sum(jnp.where(slot_hot, own_gates[:, :, None], 0.0), axis=1)
    own_grads, dense_gates = lax.optimization_barrier((own_grads, dense_gates, arrived))[:2]
    index = jnp.arange(blocks, dtype=jnp.int32)
    half = blocks // 2
    distance = jnp.where(index < half, 2 * index, 2 * (index - half) + 1)
    gates_in = exchange(dense_gates.T.reshape(blocks, slots_local, own), "expert")
    gates_in = gates_in[rank ^ distance].transpose(0, 2, 1).reshape(blocks * own, slots_local)
    gates_in = jnp.concatenate(
        [gates_in, jnp.zeros((blocks * own, 128 - slots_local), F32)], axis=1
    )
    grads_even = even_blocks(own_grads)

    attended_units, lse = attend(bounds, arrived, seg_col, seg_row, most)
    down_mine = after(routed_down, attended_units)
    down_far = across(down_mine)
    gate_ws = all_quarters(gate_mine, gate_far)
    up_ws = all_quarters(up_mine, up_far)
    down_ws = all_quarters(down_mine, down_far)
    back = exchange(attended_units.reshape(units, own, hd), BOTH)
    back = after(back, out_full, gate_far, *grads_even)
    grads_in = jnp.concatenate(grads_even + odd_blocks(grads_even), axis=0)
    attended_heads = lax.dynamic_slice_in_dim(back, block_group * heads, heads)
    attended = attended_heads.transpose(1, 0, 2).reshape(own, heads * hd)
    hidden_state = own_tokens + jnp.dot(attended, out_full, preferred_element_type=F32)
    second_scale = rms_scale(hidden_state)
    normed_two = (hidden_state * second_scale * second_gain).astype(BF)

    rows_even = even_blocks(normed_two)
    rows_in = jnp.concatenate(rows_even + odd_blocks(rows_even), axis=0)
    shared_mine = [after(w, rows_in) for w in (shared_gate, shared_up, shared_down)]
    shared_far = [across(w) for w in shared_mine]
    shared_ws = [all_quarters(w, far) for w, far in zip(shared_mine, shared_far)]

    total_rows = blocks * own
    step = min(total_rows, 512)
    spans = [slice(c, c + step) for c in range(0, total_rows, step)]
    firsts = []
    for c in spans:
        prod = down_products(grads_in[c], down_ws)
        firsts.append(experts_first(rows_in[c], prod, gates_in[c], gate_ws, up_ws, own))
    grad_rows = [x for f in firsts for x in f[4:]]
    gate_sums = jnp.concatenate([f[3] for f in firsts], axis=0)
    grad_home = [grad_rows[0]]
    for p in range(1, blocks):
        m = 2 * p if p < half else 2 * (p - half) + 1
        grad_home.append(flip(grad_rows[p], m, "expert"))

    rows_cut = lax.dynamic_slice_in_dim(rows_in, rank * cut, cut, axis=1)
    grads_cut = lax.dynamic_slice_in_dim(grads_in, rank * cut, cut, axis=1)
    seconds = []
    for c, f in zip(spans, firsts):
        act = after(f[0], shared_far[0])
        seconds.append(experts_second(rows_in[c], grads_in[c], act, f[1], f[2], down_ws, own))
    outs = step // own
    out_parts = [x for s in seconds for x in s[:outs]]
    if len(seconds) == 1:
        parts = seconds[0][outs:]
    else:
        parts = [added([s[outs + i] for s in seconds]).astype(BF) for i in range(3 * quarters)]
    to_far = [
        (parts[6 + m].astype(F32) + beside(parts[9 + m]).astype(F32)).astype(BF) for m in range(3)
    ]
    near = [(parts[m], beside(parts[3 + m])) for m in range(3)]
    shared_out, shared_dx = shared_own(
        after(normed_two, out_parts[0]), own_grads, *shared_ws
    )

    grad_home = lax.optimization_barrier((tuple(grad_home), shared_dx, to_far[0], to_far[1]))[0]
    grad_norm_two = added(grad_home) + shared_dx
    grad_full = own_grads.astype(F32)
    grad_second, second_gain_local = norm_backward(
        grad_norm_two, hidden_state, second_scale, second_gain
    )
    grad_hidden = grad_full + grad_second
    grad_attn = grad_hidden.astype(BF)
    grad_attended = jnp.einsum(
        "td,hcd->htc", grad_attn, out_full.reshape(heads, hd, width), preferred_element_type=F32
    ).astype(BF)
    do_send = jnp.concatenate([grad_attended] * groups + [grad_attended[: units - groups * heads]], axis=0)
    do_units = exchange(do_send, BOTH).reshape(blocks, rows, hd)

    out_pairs = paired(out_parts[:half], out_parts[half:])
    place = jnp.stack([rank // 2, rank % 2, quarter])
    out_low, out_high = output_grads(
        place, of_quarters(grad_attn), of_quarters(attended), heads, hw, blocks
    )
    do_units = lax.optimization_barrier((do_units, to_far[2], tuple(out_pairs), out_low))[0]

    grad_units = attend_back(bounds, arrived, seg_col, seg_row, lse, do_units, most)
    routed_far = [across(g) for g in to_far]
    out_home = collected(out_pairs)
    out_grad_pairs = paired([out_low], [out_high])[0]
    gate_send = gate_sums[:, :slots_local].reshape(blocks, own, slots_local).transpose(0, 2, 1)
    away = rank ^ index
    gate_send = after(gate_send, do_units)[away // 2 + (away % 2) * half]
    gate_back = exchange(gate_send, "expert").reshape(experts_total, own)
    grad_units = lax.optimization_barrier(
        (grad_units, out_home, out_grad_pairs, routed_far[0], gate_back)
    )[0]
    back_grads = exchange(grad_units.reshape(units, 3 * hw, rows), BOTH)

    shared_parts = [
        shared_grads(
            after(rows_in, grad_units)[c], grads_in[c], rows_cut[c], grads_cut[c], *shared_ws
        )
        for c in spans
    ]
    shared_parts = shared_parts[0] if len(spans) == 1 else added(shared_parts).astype(BF)
    out_grad = collected([out_grad_pairs[j] for j in range(half)])
    output = in_order(of_quarters((hidden_state + out_home + shared_out).astype(BF)), quarter)
    gate_grad = jnp.sum(jnp.where(slot_hot, after(gate_back, grad_units).T[:, None, :], 0.0), axis=2)
    gate_grad = in_order(of_quarters(gate_grad), quarter)
    routed = [added([a, b, c]) for (a, b), c in zip(near, routed_far)]
    back_grads = lax.optimization_barrier(
        (back_grads, shared_parts, out_grad, routed_far[1], routed[0])
    )[0]

    back_out = project_back(
        place,
        back_grads,
        cosine,
        sine,
        normed_one,
        query_weight,
        key_weight,
        value_weight,
        groups,
        blocks,
        quarters,
    )
    grad_one = added([back_out[0][0]] + [flip(back_out[0][k], k, "tensor") for k in range(1, quarters)])
    qkv_grads = []
    for m in range(3):
        sums = paired([back_out[1 + 2 * m]], [back_out[2 + 2 * m]])[0]
        qkv_grads.append(collected([sums[j] for j in range(half)]))
    first_scale = rms_scale(own_tokens)
    grad_first, first_gain_local = norm_backward(grad_one, own_tokens, first_scale, first_gain)
    input_grad = in_order(of_quarters((grad_hidden + grad_first).astype(BF)), quarter)
    shared = added([shared_parts[0]] + [flip(shared_parts[k], k, "tensor") for k in range(1, quarters)])

    gains = jnp.stack([first_gain_local, second_gain_local]).reshape(2, blocks, cut).transpose(1, 0, 2)
    gains = jnp.broadcast_to(gains[:, None], (blocks, quarters, 2, cut)).reshape(units, 2, cut)
    gains = jnp.sum(exchange(gains, BOTH), axis=0)

    weight_shape = (heads, 2, pair_width, cut)
    return (
        output,
        input_grad,
        gate_grad,
        gains[0],
        gains[1],
        qkv_grads[0].T.reshape(weight_shape),
        qkv_grads[1].T.reshape(weight_shape),
        qkv_grads[2].T.reshape(weight_shape),
        out_grad.T.reshape(weight_shape),
        shared[0],
        shared[1],
        shared[2],
        routed[0],
        routed[1],
        routed[2],
    )


def solution(mesh):
    placed = (
        P("expert", None),
        P(),
        P("expert", None),
        P("expert", None),
        P(),
        P(),
        P(),
        P(None, None, "tensor", None),
        P(None, None, "tensor", None),
        P(None, None, "tensor", None),
        P(None, None, "tensor", None),
        P("tensor", None),
        P("tensor", None),
        P("tensor", None),
        P("expert", "tensor", None),
        P("expert", "tensor", None),
        P("expert", "tensor", None),
        P("expert", None),
    )
    return jax.shard_map(
        on_device,
        mesh=mesh,
        in_specs=placed,
        out_specs=(
            P("expert", None),
            P("expert", None),
            P("expert", None),
            P("expert"),
            P("expert"),
            P(None, None, "tensor", "expert"),
            P(None, None, "tensor", "expert"),
            P(None, None, "tensor", "expert"),
            P(None, None, "tensor", "expert"),
            P("tensor", "expert"),
            P("tensor", "expert"),
            P("tensor", "expert"),
            P("expert", "tensor", None),
            P("expert", "tensor", None),
            P("expert", "tensor", None),
        ),
        check_vma=False,
    )
```

```python
import jax
import jax.numpy as jnp
from jax import lax
from jax.experimental import pallas as pl
from jax.experimental.pallas import tpu as pltpu
from jax.sharding import PartitionSpec as P

HD = 128
REACH = 4
EPSILON = 1e-06
MASKED = -1e30
BF = jnp.bfloat16
F32 = jnp.float32
BOTH = ("expert", "tensor")
VMEM_LIMIT = 60 * 1024 * 1024


def dot(a, b, ca, cb):
    return lax.dot_general(a, b, (((ca,), (cb,)), ((), ())), preferred_element_type=F32)


def whole(shape):
    zeros = (0,) * len(shape)
    return pl.BlockSpec(shape, lambda *_: zeros)


def query_groups(blocks, groups):
    cost = [min(b, REACH) + 1 for b in range(blocks)]
    most = max(cost)
    while True:
        starts, load = [0], 0
        for b in range(blocks):
            if load + cost[b] > most:
                starts.append(b)
                load = 0
            load += cost[b]
        if len(starts) <= groups:
            break
        most += 1
    return starts + [blocks] * (groups + 2 - len(starts))


def rms_scale(values):
    return lax.rsqrt(jnp.mean(values * values, axis=-1, keepdims=True) + EPSILON)


def norm_backward(grad_out, values, inverse_rms, gain_vector):
    weighted = grad_out * gain_vector
    normal = values * inverse_rms
    gain_grad = jnp.sum(grad_out * normal, axis=0)
    grad_in = inverse_rms * (
        weighted - normal * jnp.mean(normal * weighted, axis=-1, keepdims=True)
    )
    return grad_in, gain_grad


def project(tokens, gain, wq, wk, wv, cosine, sine, units, groups):
    rows, width = tokens.shape
    heads = wq.shape[0]
    hw = wq.shape[1] * wq.shape[2]
    pw = wq.shape[2]

    def body(tok, gain_ref, q_ref, k_ref, v_ref, cos_ref, sin_ref, norm_ref, send_ref):
        x = tok[...].astype(F32)
        normed = (x * rms_scale(x) * gain_ref[...]).astype(BF)
        norm_ref[...] = normed
        cos = cos_ref[...]
        sin = sin_ref[...]
        for part, w_ref in enumerate((q_ref, k_ref, v_ref)):
            pre = dot(w_ref[...], normed, 1, 1)
            for h in range(heads):
                a = pre[h * hw : h * hw + pw]
                b = pre[h * hw + pw : (h + 1) * hw]
                if part < 2:
                    a, b = a * cos - b * sin, b * cos + a * sin
                chunk = jnp.concatenate([a, b], axis=0).astype(BF)
                for unit in range(h, units, heads):
                    send_ref[unit, part * hw : (part + 1) * hw] = chunk

    flat = (heads * hw, width)
    return pl.pallas_call(
        body,
        out_shape=(
            jax.ShapeDtypeStruct((rows, width), BF),
            jax.ShapeDtypeStruct((units, 3 * hw, rows), BF),
        ),
        compiler_params=pltpu.CompilerParams(vmem_limit_bytes=VMEM_LIMIT),
        name="project",
    )(tokens, gain[None], wq.reshape(flat), wk.reshape(flat), wv.reshape(flat), cosine, sine)


def allowed_pairs(seg_col, seg_row, query_block, key_block, rows):
    wide = jnp.concatenate([seg_col] * (rows // seg_col.shape[1]), axis=1)
    same = wide == seg_row
    ahead = lax.broadcasted_iota(jnp.int32, (rows, rows), 0) - lax.broadcasted_iota(
        jnp.int32, (rows, rows), 1
    )
    return same & (ahead + (query_block - key_block) * rows >= 0)


def attend(bounds, arrived, seg_col, seg_row, most):
    blocks, quarters, chunk, rows = arrived.shape
    hw = chunk // 3
    hd = quarters * hw
    scale = HD ** (-0.5)

    def part(ref, block, which):
        return ref[block, :, which * hw : (which + 1) * hw, :].reshape(hd, rows)

    def body(bounds_ref, arr_ref, col_ref, row_ref, out_ref, lse_ref, score_ref):
        query_block = bounds_ref[0] + pl.program_id(0)

        @pl.when(query_block < bounds_ref[1])
        def _():
            query = part(arr_ref, query_block, 0)
            col = col_ref[query_block]
            low = jnp.maximum(query_block - REACH, 0)

            def first(kb, best):
                s = dot(query, part(arr_ref, kb, 1), 0, 0) * scale
                s = jnp.where(allowed_pairs(col, row_ref[kb], query_block, kb, rows), s, MASKED)
                score_ref[kb - low] = s
                return jnp.maximum(best, jnp.max(s, axis=1, keepdims=True))

            best = lax.fori_loop(low, query_block + 1, first, jnp.full((rows, 1), MASKED, F32))

            def second(kb, carry):
                total, out = carry
                p = jnp.exp(score_ref[kb - low] - best)
                total = total + jnp.sum(p, axis=1, keepdims=True)
                return total, out + dot(p.astype(BF), part(arr_ref, kb, 2), 1, 1)

            total, out = lax.fori_loop(
                low, query_block + 1, second, (jnp.zeros((rows, 1), F32), jnp.zeros((rows, hd), F32))
            )
            out_ref[query_block] = (out / total).astype(BF)
            lse_ref[query_block] = jnp.broadcast_to(best + jnp.log(total), (rows, 128))

    grid_spec = pltpu.PrefetchScalarGridSpec(
        num_scalar_prefetch=1,
        grid=(most,),
        in_specs=[whole(arrived.shape), whole(seg_col.shape), whole(seg_row.shape)],
        out_specs=[whole((blocks, rows, hd)), whole((blocks, rows, 128))],
        scratch_shapes=[pltpu.VMEM((REACH + 1, rows, rows), F32)],
    )
    return pl.pallas_call(
        body,
        grid_spec=grid_spec,
        out_shape=(
            jax.ShapeDtypeStruct((blocks, rows, hd), BF),
            jax.ShapeDtypeStruct((blocks, rows, 128), F32),
        ),
        compiler_params=pltpu.CompilerParams(vmem_limit_bytes=VMEM_LIMIT),
        name="attend",
    )(bounds, arrived, seg_col, seg_row)


def attend_back(bounds, arrived, seg_col, seg_row, lse, grad_out, most):
    blocks, quarters, chunk, rows = arrived.shape
    hw = chunk // 3
    hd = quarters * hw
    scale = HD ** (-0.5)

    def part(ref, block, which):
        return ref[block, :, which * hw : (which + 1) * hw, :].reshape(hd, rows)

    def body(bounds_ref, arr_ref, col_ref, row_ref, lse_ref, do_ref, res_ref, prob_ref, dp_ref, dk_ref, dv_ref):
        step = pl.program_id(0)
        query_block = bounds_ref[0] + step

        @pl.when(step == 0)
        def _():
            res_ref[...] = jnp.zeros(res_ref.shape, BF)
            dk_ref[...] = jnp.zeros(dk_ref.shape, F32)
            dv_ref[...] = jnp.zeros(dv_ref.shape, F32)

        @pl.when(query_block < bounds_ref[1])
        def _():
            query = part(arr_ref, query_block, 0)
            col = col_ref[query_block]
            lse_now = jnp.concatenate([lse_ref[query_block]] * (rows // 128), axis=1)
            do = do_ref[query_block]
            low = jnp.maximum(query_block - REACH, 0)

            def first(kb, inner):
                s = dot(query, part(arr_ref, kb, 1), 0, 0) * scale
                ok = allowed_pairs(col, row_ref[kb], query_block, kb, rows)
                p = jnp.where(ok, jnp.exp(jnp.where(ok, s - lse_now, 0.0)), 0.0)
                dp = dot(do, part(arr_ref, kb, 2), 1, 0)
                prob_ref[kb - low] = p
                dp_ref[kb - low] = dp
                dv_ref[kb] += dot(do, p.astype(BF), 0, 0)
                return inner + jnp.sum(p * dp, axis=1, keepdims=True)

            inner = lax.fori_loop(low, query_block + 1, first, jnp.zeros((rows, 1), F32))

            def second(kb, dq):
                ds = (prob_ref[kb - low] * (dp_ref[kb - low] - inner)).astype(BF)
                dk_ref[kb] += dot(query, ds, 1, 0)
                return dq + dot(part(arr_ref, kb, 1), ds, 1, 1)

            dq = lax.fori_loop(low, query_block + 1, second, jnp.zeros((hd, rows), F32))
            res_ref[query_block, :, 0:hw, :] = (dq * scale).astype(BF).reshape(quarters, hw, rows)

        @pl.when(step == pl.num_programs(0) - 1)
        def _():
            for b in range(blocks):
                res_ref[b, :, hw : 2 * hw, :] = (dk_ref[b] * scale).astype(BF).reshape(quarters, hw, rows)
                res_ref[b, :, 2 * hw : 3 * hw, :] = dv_ref[b].astype(BF).reshape(quarters, hw, rows)

    grid_spec = pltpu.PrefetchScalarGridSpec(
        num_scalar_prefetch=1,
        grid=(most,),
        in_specs=[
            whole(arrived.shape),
            whole(seg_col.shape),
            whole(seg_row.shape),
            whole(lse.shape),
            whole(grad_out.shape),
        ],
        out_specs=whole(arrived.shape),
        scratch_shapes=[
            pltpu.VMEM((REACH + 1, rows, rows), F32),
            pltpu.VMEM((REACH + 1, rows, rows), F32),
            pltpu.VMEM((blocks, hd, rows), F32),
            pltpu.VMEM((blocks, hd, rows), F32),
        ],
    )
    return pl.pallas_call(
        body,
        grid_spec=grid_spec,
        out_shape=jax.ShapeDtypeStruct(arrived.shape, BF),
        compiler_params=pltpu.CompilerParams(vmem_limit_bytes=VMEM_LIMIT),
        name="attend_back",
    )(bounds, arrived, seg_col, seg_row, lse, grad_out)


def weight_specs(parts, hidden, width, mats):
    return [pl.BlockSpec((1, hidden, width), lambda s, *_: (s, 0, 0))] * (parts * mats)


def down_products(place, even, odd, first, count, width, downs):
    half, own, wide = even.shape
    parts = len(downs)
    slots, hidden, _ = downs[0].shape
    lanes = wide - width

    def body(place_ref, even_ref, odd_ref, *refs):
        da_ref, dy_ref, gate_ref = refs[parts:]

        @pl.when(pl.program_id(0) == 0)
        def _():
            for c in range(count // own // 2):
                at = place_ref[0] ^ (first + c)
                for parity in range(2):

                    @pl.when(place_ref[1] == parity)
                    def _():
                        for b, ref in ((2 * c + parity, even_ref), (2 * c + 1 - parity, odd_ref)):
                            dy_ref[b * own : (b + 1) * own] = ref[at, :, 0:width]
                            gate_ref[b * own : (b + 1) * own] = ref[at, :, width:wide]

        for k in range(parts):
            da_ref[0, k] = dot(dy_ref[...], refs[k][0], 1, 1)

    return pl.pallas_call(
        body,
        grid_spec=pltpu.PrefetchScalarGridSpec(
            num_scalar_prefetch=1,
            grid=(slots,),
            in_specs=[whole(even.shape), whole(odd.shape)] + weight_specs(parts, hidden, width, 1),
            out_specs=[
                pl.BlockSpec((1, parts, count, hidden), lambda s, *_: (s, 0, 0, 0)),
                whole((count, width)),
                whole((count, lanes)),
            ],
        ),
        out_shape=(
            jax.ShapeDtypeStruct((slots, parts, count, hidden), F32),
            jax.ShapeDtypeStruct((count, width), BF),
            jax.ShapeDtypeStruct((count, lanes), BF),
        ),
        compiler_params=pltpu.CompilerParams(vmem_limit_bytes=VMEM_LIMIT),
        name="down_products",
    )(place, even, odd, *downs)


def pieces(x):
    high = lax.reduce_precision(x, 8, 7)
    middle = lax.reduce_precision(x - high, 8, 7)
    return [high, middle, x - high - middle]


def swish_parts(g, u, da):
    sig = jax.nn.sigmoid(g)
    swish = g * sig
    return swish * u, da * u * (sig * (1.0 + g * (1.0 - sig))), da * swish


def experts_first(place, rows_in, down_prod, gates, gate_ws, up_ws, experts):
    count, width = rows_in.shape
    parts = len(gate_ws)
    slots, hidden, _ = gate_ws[0].shape
    lanes = gates.shape[1]

    def body(place_ref, x_ref, da_ref, gate_ref, *refs):
        gate_w, up_w = refs[:parts], refs[parts : 2 * parts]
        act_ref, dg_ref, du_ref, gg_ref, dx_ref, acc_ref, sum_ref = refs[2 * parts :]
        s = pl.program_id(0)
        x = x_ref[...]
        lane = lax.broadcasted_iota(jnp.int32, (count, lanes), 1)
        slot = place_ref[3] * slots + s
        mine = lane % experts == slot
        gate = jnp.sum(jnp.where(mine, gate_ref[...].astype(F32), 0.0), axis=1, keepdims=True)
        total = jnp.zeros((count, 1), F32)

        @pl.when(s == 0)
        def _():
            acc_ref[...] = jnp.zeros(acc_ref.shape, F32)
            sum_ref[...] = jnp.zeros(sum_ref.shape, F32)

        for k in range(parts):
            g = dot(x, gate_w[k][0], 1, 1)
            u = dot(x, up_w[k][0], 1, 1)
            da = da_ref[0, k]
            act, dg, du = swish_parts(g, u, da * gate)
            total = total + jnp.sum(act * da, axis=1, keepdims=True)
            act_ref[0, k] = (act * gate).astype(BF)
            dg_ref[0, k] = dg.astype(BF)
            du_ref[0, k] = du.astype(BF)
            acc_ref[...] += dot(dg_ref[0, k], gate_w[k][0], 1, 0) + dot(du_ref[0, k], up_w[k][0], 1, 0)

        high = total.astype(BF).astype(F32)
        middle = (total - high).astype(BF).astype(F32)
        for n, piece in enumerate((high, middle, total - high - middle)):
            sum_ref[...] += jnp.where(lane == n * experts + slot, piece, 0.0)

        @pl.when(s == slots - 1)
        def _():
            dx_ref[...] = acc_ref[...].astype(BF)
            gg_ref[...] = sum_ref[...].astype(BF)

    hid = jax.ShapeDtypeStruct((slots, parts, count, hidden), BF)
    hid_spec = pl.BlockSpec((1, parts, count, hidden), lambda s, *_: (s, 0, 0, 0))
    return pl.pallas_call(
        body,
        grid_spec=pltpu.PrefetchScalarGridSpec(
            num_scalar_prefetch=1,
            grid=(slots,),
            in_specs=[whole(rows_in.shape), hid_spec, whole(gates.shape)]
            + weight_specs(parts, hidden, width, 2),
            out_specs=[hid_spec, hid_spec, hid_spec, whole((count, lanes)), whole((count, width))],
            scratch_shapes=[pltpu.VMEM((count, width), F32), pltpu.VMEM((count, lanes), F32)],
        ),
        out_shape=(
            hid,
            hid,
            hid,
            jax.ShapeDtypeStruct((count, lanes), BF),
            jax.ShapeDtypeStruct((count, width), BF),
        ),
        compiler_params=pltpu.CompilerParams(vmem_limit_bytes=VMEM_LIMIT),
        name="experts_first",
    )(place, rows_in, down_prod, gates, *gate_ws, *up_ws)


def experts_second(place, rows_in, grads_in, sums, act, dgate, dup, downs, own):
    count, width = rows_in.shape
    parts = len(downs)
    slots, hidden, _ = downs[0].shape
    wide = width + sums.shape[1]
    half = count // own // 2

    def body(place_ref, x_ref, dy_ref, sum_ref, act_ref, dg_ref, du_ref, *refs):
        down_w = refs[:parts]
        low_ref, high_ref = refs[parts : parts + 2]
        grads = refs[parts + 2 : -1]
        acc_ref = refs[-1]
        s = pl.program_id(0)

        @pl.when(s == 0)
        def _():
            acc_ref[...] = jnp.zeros(acc_ref.shape, F32)

        for k in range(parts):
            acc_ref[...] += dot(act_ref[0, k], down_w[k][0], 1, 0)
            grads[k][0, 0] = dot(dg_ref[0, k], x_ref[...], 0, 0).astype(BF)
            grads[k][1, 0] = dot(du_ref[0, k], x_ref[...], 0, 0).astype(BF)
            grads[k][2, 0] = dot(act_ref[0, k], dy_ref[...], 0, 0).astype(BF)

        @pl.when(s == slots - 1)
        def _():
            for c in range(half):
                at = (place_ref[0] % half) ^ c
                for parity in range(2):

                    @pl.when(place_ref[1] == parity)
                    def _():
                        for b, ref in ((2 * c + parity, low_ref), (2 * c + 1 - parity, high_ref)):
                            ref[at, :, 0:width] = acc_ref[b * own : (b + 1) * own].astype(BF)
                            ref[at, :, width:wide] = sum_ref[b * own : (b + 1) * own]

    hid_spec = pl.BlockSpec((1, parts, count, hidden), lambda s, *_: (s, 0, 0, 0))
    out_shape = (half, own, wide)
    return pl.pallas_call(
        body,
        grid_spec=pltpu.PrefetchScalarGridSpec(
            num_scalar_prefetch=1,
            grid=(slots,),
            in_specs=[whole(rows_in.shape), whole(grads_in.shape), whole(sums.shape)]
            + [hid_spec] * 3
            + weight_specs(parts, hidden, width, 1),
            out_specs=[whole(out_shape)] * 2
            + [pl.BlockSpec((3, 1, hidden, width), lambda s, *_: (0, s, 0, 0))] * parts,
            scratch_shapes=[pltpu.VMEM((count, width), F32)],
        ),
        out_shape=(jax.ShapeDtypeStruct(out_shape, BF),) * 2
        + (jax.ShapeDtypeStruct((3, slots, hidden, width), BF),) * parts,
        compiler_params=pltpu.CompilerParams(vmem_limit_bytes=VMEM_LIMIT),
        name="experts_second",
    )(place, rows_in, grads_in, sums, act, dgate, dup, *downs)


def shared_own(rows, grads, weights):
    parts = len(weights)

    def body(x_ref, dy_ref, *refs):
        out_ref, dx_ref = refs[parts:]
        for k in range(parts):
            gw, uw, dw = refs[k][0], refs[k][1], refs[k][2]
            act, dg, du = swish_parts(
                dot(x_ref[...], gw, 1, 1),
                dot(x_ref[...], uw, 1, 1),
                dot(dy_ref[...], dw, 1, 1),
            )
            out = dot(act.astype(BF), dw, 1, 0)
            dx = dot(dg.astype(BF), gw, 1, 0) + dot(du.astype(BF), uw, 1, 0)
            if k == 0:
                out_ref[...] = out
                dx_ref[...] = dx
            else:
                out_ref[...] += out
                dx_ref[...] += dx

    shape = jax.ShapeDtypeStruct(rows.shape, F32)
    return pl.pallas_call(
        body,
        out_shape=(shape, shape),
        compiler_params=pltpu.CompilerParams(vmem_limit_bytes=VMEM_LIMIT),
        name="shared_own",
    )(rows, grads, *weights)


def shared_grads(rows_in, grads_in, rows_cut, grads_cut, weights):
    parts = len(weights)
    hidden = weights[0].shape[1]
    cut = rows_cut.shape[1]

    def body(x_ref, dy_ref, xc_ref, dyc_ref, *refs):
        out_ref = refs[parts]
        for k in range(parts):
            act, dg, du = swish_parts(
                dot(x_ref[...], refs[k][0], 1, 1),
                dot(x_ref[...], refs[k][1], 1, 1),
                dot(dy_ref[...], refs[k][2], 1, 1),
            )
            out_ref[k, 0] = dot(dg.astype(BF), xc_ref[...], 0, 0).astype(BF)
            out_ref[k, 1] = dot(du.astype(BF), xc_ref[...], 0, 0).astype(BF)
            out_ref[k, 2] = dot(act.astype(BF), dyc_ref[...], 0, 0).astype(BF)

    return pl.pallas_call(
        body,
        out_shape=jax.ShapeDtypeStruct((parts, 3, hidden, cut), BF),
        compiler_params=pltpu.CompilerParams(vmem_limit_bytes=VMEM_LIMIT),
        name="shared_grads",
    )(rows_in, grads_in, rows_cut, grads_cut, *weights)


def store_chunks(place_ref, value, low_ref, high_ref):
    half, cut, _ = low_ref.shape
    for c in range(half):
        first = value[2 * c * cut : (2 * c + 1) * cut]
        second = value[(2 * c + 1) * cut : (2 * c + 2) * cut]
        at = place_ref[0] ^ c
        even = place_ref[1] == 0
        low_ref[at] = jnp.where(even, first, second).astype(BF)
        high_ref[at] = jnp.where(even, second, first).astype(BF)


def output_grads(place, attn_parts, att_parts, heads, hw, blocks):
    parts = len(attn_parts)
    own, width = attn_parts[0].shape
    span = heads * hw
    full = att_parts[0].shape[1]
    hd = full // heads

    def body(place_ref, *refs):
        low_ref, high_ref = refs[2 * parts :]
        attn = jnp.concatenate([r[...] for r in refs[:parts]], axis=0)
        att = jnp.concatenate([r[...] for r in refs[parts : 2 * parts]], axis=0)
        row = lax.broadcasted_iota(jnp.int32, (full, span), 0)
        col = lax.broadcasted_iota(jnp.int32, (full, span), 1)
        source = (col // hw) * hd + place_ref[2] * hw + col % hw
        pick = jnp.where(row == source, 1.0, 0.0).astype(BF)
        mine = dot(att, pick, 1, 0).astype(BF)
        store_chunks(place_ref, dot(attn, mine, 0, 0), low_ref, high_ref)

    shape = (blocks // 2, width // blocks, span)
    return pl.pallas_call(
        body,
        grid_spec=pltpu.PrefetchScalarGridSpec(
            num_scalar_prefetch=1,
            grid=(1,),
            in_specs=[whole((own, width))] * parts + [whole((own, full))] * parts,
            out_specs=[whole(shape)] * 2,
        ),
        out_shape=(jax.ShapeDtypeStruct(shape, BF),) * 2,
        compiler_params=pltpu.CompilerParams(vmem_limit_bytes=VMEM_LIMIT),
        name="output_grads",
    )(place, *attn_parts, *att_parts)


def project_back(place, back, cosine, sine, tokens, normed, wq, wk, wv, groups, blocks, quarters):
    heads = wq.shape[0]
    pw = wq.shape[2]
    hw = 2 * pw
    rows, width = normed.shape
    own = rows // quarters
    span = heads * hw

    def body(place_ref, back_ref, cos_ref, sin_ref, tok_ref, norm_ref, q_ref, k_ref, v_ref, *refs):
        dx_ref, gain_ref = refs[:2]
        chunk_refs = refs[2:-1]
        grad_ref = refs[-1]
        cos = cos_ref[...]
        sin = sin_ref[...]
        for h in range(heads):
            total = back_ref[h].astype(F32)
            for r in range(1, groups):
                total = total + back_ref[r * heads + h].astype(F32)
            for part in range(3):
                a = total[part * hw : part * hw + pw]
                b = total[part * hw + pw : (part + 1) * hw]
                if part < 2:
                    a, b = a * cos + b * sin, b * cos - a * sin
                at = part * span + h * hw
                grad_ref[at : at + hw] = jnp.concatenate([a, b], axis=0).astype(BF)
        for part in range(3):
            value = dot(norm_ref[...], grad_ref[part * span : (part + 1) * span], 0, 1)
            store_chunks(place_ref, value, chunk_refs[2 * part], chunk_refs[2 * part + 1])
        dx = dot(grad_ref[0:span], q_ref[...], 0, 0)
        dx = dx + dot(grad_ref[span : 2 * span], k_ref[...], 0, 0)
        dx = dx + dot(grad_ref[2 * span :], v_ref[...], 0, 0)
        for j in range(quarters):
            dx_ref[place_ref[2] ^ j] = dx[j * own : (j + 1) * own].astype(BF)
        x = tok_ref[...].astype(F32)
        gain_ref[...] = jnp.sum(dx * (x * rms_scale(x)), axis=0, keepdims=True)

    flat = (span, width)
    chunk = (blocks // 2, width // blocks, span)
    return pl.pallas_call(
        body,
        grid_spec=pltpu.PrefetchScalarGridSpec(
            num_scalar_prefetch=1,
            grid=(1,),
            in_specs=[
                whole(back.shape),
                whole(cosine.shape),
                whole(sine.shape),
                whole(tokens.shape),
                whole(normed.shape),
                whole(flat),
                whole(flat),
                whole(flat),
            ],
            out_specs=[whole((quarters, own, width)), whole((1, width))] + [whole(chunk)] * 6,
            scratch_shapes=[pltpu.VMEM((3 * span, rows), BF)],
        ),
        out_shape=(
            jax.ShapeDtypeStruct((quarters, own, width), BF),
            jax.ShapeDtypeStruct((1, width), F32),
        )
        + (jax.ShapeDtypeStruct(chunk, BF),) * 6,
        compiler_params=pltpu.CompilerParams(vmem_limit_bytes=VMEM_LIMIT),
        name="project_back",
    )(place, back, cosine, sine, tokens, normed, wq.reshape(flat), wk.reshape(flat), wv.reshape(flat))


def after(x, *others):
    return lax.optimization_barrier((x,) + others)[0]


def added(parts):
    total = parts[0].astype(F32)
    for p in parts[1:]:
        total = total + p.astype(F32)
    return total


def flip(x, by, axis):
    size = lax.axis_size(axis)
    return lax.ppermute(x, axis, [(i, i ^ by) for i in range(size)])


def exchange(x, axis):
    return lax.all_to_all(x, axis, 0, 0, tiled=True)


def spread(x, axis):
    size = lax.axis_size(axis)
    return exchange(jnp.broadcast_to(x[None], (size,) + x.shape), axis)


def even_blocks(x):
    size = lax.axis_size("expert")
    return jnp.stack([x] + [flip(x, m, "expert") for m in range(2, size, 2)])


def odd_blocks(evens):
    return flip(evens, 1, "expert")


def paired(evens, odds):
    return (evens.astype(F32) + flip(odds, 1, "expert").astype(F32)).astype(BF)


def collected(sums):
    return added([sums[0]] + [flip(sums[j], 2 * j, "expert") for j in range(1, sums.shape[0])])


def of_quarters(x):
    quarters = lax.axis_size("tensor")
    return [x] + [flip(x, k, "tensor") for k in range(1, quarters)]


def in_order(parts, quarter):
    out = jnp.zeros((len(parts),) + parts[0].shape, parts[0].dtype)
    for k, p in enumerate(parts):
        out = lax.dynamic_update_slice(out, p[None], (quarter ^ k,) + (0,) * p.ndim)
    return out.reshape((-1,) + parts[0].shape[1:])


def on_device(
    tokens,
    segment_ids,
    expert_ids,
    gate_values,
    expert_slot,
    first_gain,
    second_gain,
    query_weight,
    key_weight,
    value_weight,
    output_weight,
    shared_gate,
    shared_up,
    shared_down,
    routed_gate,
    routed_up,
    routed_down,
    cotangent,
):
    rows, width = tokens.shape
    top = expert_ids.shape[1]
    experts_total = expert_slot.shape[0]
    slots_local = routed_gate.shape[0]
    blocks = lax.axis_size("expert")
    quarters = lax.axis_size("tensor")
    rank = lax.axis_index("expert")
    quarter = lax.axis_index("tensor")
    heads = query_weight.shape[0]
    pair_width = query_weight.shape[2]
    hw = 2 * pair_width
    hd = quarters * hw
    units = blocks * quarters
    groups = units // heads
    own = rows // quarters
    cut = width // blocks
    starts = query_groups(blocks, groups)
    most = max(starts[i + 1] - starts[i] for i in range(groups))
    unit_group = [min(j // heads, groups) for j in range(units)]
    unit = rank * quarters + quarter
    low_table = jnp.array([starts[g] for g in unit_group], jnp.int32)
    high_table = jnp.array([starts[g + 1] if g < groups else starts[g] for g in unit_group], jnp.int32)
    bounds = jnp.stack([low_table[unit], high_table[unit]])
    block_group = jnp.array(
        [max(g for g in range(groups) if starts[g] <= b) for b in range(blocks)], jnp.int32
    )[rank]

    seg_mine = lax.dynamic_slice_in_dim(segment_ids, rank * rows, rows)
    doc_start = jnp.sum((segment_ids[:, None] < seg_mine[None, :]).astype(jnp.int32), axis=0)
    positions = rank * rows + jnp.arange(rows, dtype=jnp.int32) - doc_start
    freq_index = quarter * pair_width + jnp.arange(pair_width, dtype=jnp.int32)
    inverse_freq = 10000.0 ** (-2.0 * freq_index.astype(F32) / HD)
    angles = inverse_freq[:, None] * positions.astype(F32)[None, :]
    cosine = jnp.cos(angles)
    sine = jnp.sin(angles)
    seg_row = segment_ids.reshape(blocks, 1, rows)
    seg_col = jnp.broadcast_to(segment_ids.reshape(blocks, rows, 1), (blocks, rows, 128))

    normed_one, send = project(
        tokens, first_gain, query_weight, key_weight, value_weight, cosine, sine, units, groups
    )
    arrived = exchange(send, BOTH).reshape(blocks, quarters, 3 * hw, rows)

    def across(x):
        return flip(x, 2, "tensor")

    def beside(x):
        return flip(x, 1, "tensor")

    def all_quarters(x, far):
        return (x, beside(x), far, beside(far))

    out_mine = after(output_weight.reshape(heads, hw, width), normed_one)
    out_far = across(out_mine)
    gate_mine = after(routed_gate, out_far)
    gate_far = across(gate_mine)
    arrived = after(arrived, out_far)
    up_mine = after(routed_up, arrived)
    up_far = across(up_mine)
    out_ws = all_quarters(out_mine, out_far)
    out_full = jnp.zeros((heads, quarters, hw, width), BF)
    for k in range(quarters):
        out_full = lax.dynamic_update_slice(out_full, out_ws[k][:, None], (0, quarter ^ k, 0, 0))
    out_full = out_full.reshape(heads * hd, width)

    half = blocks // 2
    place = jnp.stack([rank // 2, rank % 2, quarter, rank])
    own_tokens = lax.dynamic_slice_in_dim(tokens, quarter * own, own).astype(F32)
    own_grads = lax.dynamic_slice_in_dim(cotangent, quarter * own, own)
    own_ids = lax.dynamic_slice_in_dim(expert_ids, quarter * own, own)
    own_gates = lax.dynamic_slice_in_dim(gate_values, quarter * own, own)
    onehot = own_ids[:, :, None] == jnp.arange(experts_total, dtype=jnp.int32)
    own_slots = jnp.sum(jnp.where(onehot, expert_slot[None, None, :], 0), axis=2)
    slot_hot = own_slots[:, :, None] == jnp.arange(experts_total, dtype=jnp.int32)
    dense_gates = jnp.sum(jnp.where(slot_hot, own_gates[:, :, None], 0.0), axis=1)
    lanes = -(-3 * experts_total // 128) * 128
    spare = jnp.zeros((own, lanes - 3 * experts_total), BF)
    own_wide = jnp.concatenate(
        [own_grads] + [p.astype(BF) for p in pieces(dense_gates)] + [spare], axis=1
    )
    grads_even = even_blocks(after(own_wide, arrived))
    grads_odd = odd_blocks(grads_even)

    attended_units, lse = attend(bounds, arrived, seg_col, seg_row, most)
    down_mine = after(routed_down, attended_units)
    down_far = across(down_mine)
    gate_ws = all_quarters(gate_mine, gate_far)
    up_ws = all_quarters(up_mine, up_far)
    down_ws = all_quarters(down_mine, down_far)
    back = exchange(attended_units.reshape(units, own, hd), BOTH)
    back = after(back, out_full, gate_far, grads_even)
    attended_heads = lax.dynamic_slice_in_dim(back, block_group * heads, heads)
    attended = attended_heads.transpose(1, 0, 2).reshape(own, heads * hd)
    hidden_state = own_tokens + jnp.dot(attended, out_full, preferred_element_type=F32)
    second_scale = rms_scale(hidden_state)
    normed_two = (hidden_state * second_scale * second_gain).astype(BF)

    rows_in = spread(normed_two, "expert").reshape(blocks * own, width)
    shared_mine = after(jnp.stack([shared_gate, shared_up, shared_down]), normed_two)
    shared_far = across(shared_mine)
    shared_near = beside(shared_mine)
    shared_ws = (shared_mine, shared_near, shared_far, beside(shared_far))

    total_rows = blocks * own
    step = min(total_rows, 512)
    spans = [slice(c, c + step) for c in range(0, total_rows, step)]
    prods = [
        down_products(place, grads_even, grads_odd, c.start // own // 2, step, width, down_ws)
        for c in spans
    ]
    firsts = [
        experts_first(place, rows_in[c], p[0], p[2], gate_ws, up_ws, experts_total)
        for c, p in zip(spans, prods)
    ]
    grads_in = jnp.concatenate([p[1] for p in prods], axis=0)
    grad_rows = jnp.concatenate([f[4] for f in firsts], axis=0)
    grad_home = exchange(grad_rows.reshape(blocks, own, width), "expert")

    rows_cut = lax.dynamic_slice_in_dim(rows_in, rank * cut, cut, axis=1)
    grads_cut = lax.dynamic_slice_in_dim(grads_in, rank * cut, cut, axis=1)
    seconds = []
    for c, f in zip(spans, firsts):
        act = lax.optimization_barrier((f[0], shared_far, shared_near))[0]
        seconds.append(
            experts_second(place, rows_in[c], grads_in[c], f[3], act, f[1], f[2], down_ws, own)
        )
    if len(seconds) == 1:
        out_low, out_high = seconds[0][:2]
        parts = seconds[0][2:]
    else:
        order = (rank // (step // own)) ^ jnp.arange(len(seconds), dtype=jnp.int32)
        out_low, out_high = (
            jnp.stack([s[i] for s in seconds])[order].reshape(half, own, width + lanes)
            for i in range(2)
        )
        parts = [added([s[2 + k] for s in seconds]).astype(BF) for k in range(quarters)]
    shared_out, shared_dx = shared_own(after(normed_two, out_low), own_grads, shared_ws)
    att_parts = of_quarters(after(attended, shared_far))

    out_pairs = paired(out_low, out_high)
    grad_home, out_pairs = lax.optimization_barrier(
        (grad_home, out_pairs, shared_dx, tuple(att_parts))
    )[:2]
    grad_norm_two = jnp.sum(grad_home.astype(F32), axis=0) + shared_dx
    grad_full = own_grads.astype(F32)
    grad_second, second_gain_local = norm_backward(
        grad_norm_two, hidden_state, second_scale, second_gain
    )
    grad_hidden = grad_full + grad_second
    grad_attn = grad_hidden.astype(BF)
    grad_attended = jnp.einsum(
        "td,hcd->htc", grad_attn, out_full.reshape(heads, hd, width), preferred_element_type=F32
    ).astype(BF)
    do_send = jnp.concatenate([grad_attended] * groups + [grad_attended[: units - groups * heads]], axis=0)
    do_units = exchange(do_send, BOTH).reshape(blocks, rows, hd)

    from_far = beside(after(parts[3], grad_home))
    to_far = [(parts[2][m].astype(F32) + from_far[m].astype(F32)).astype(BF) for m in range(3)]
    near = beside(after(parts[1], from_far))
    routed_far = [across(to_far[0]), across(to_far[1])]
    proj_low, proj_high = output_grads(
        place, of_quarters(grad_attn), att_parts, heads, hw, blocks
    )
    do_units, to_far_last = lax.optimization_barrier(
        (do_units, to_far[2], proj_low)
    )[:2]

    grad_units = attend_back(bounds, arrived, seg_col, seg_row, lse, do_units, most)
    routed_far.append(across(to_far_last))
    out_home = collected(out_pairs)
    proj_pairs = paired(proj_low, proj_high)
    grad_units = lax.optimization_barrier((grad_units, out_home, proj_pairs, routed_far[0]))[0]
    back_grads = exchange(grad_units.reshape(units, 3 * hw, rows), BOTH)

    rows_late = after(rows_in, grad_units)
    shared_parts = [
        shared_grads(rows_late[c], grads_in[c], rows_cut[c], grads_cut[c], shared_ws) for c in spans
    ]
    shared_parts = shared_parts[0] if len(spans) == 1 else added(shared_parts).astype(BF)
    out_grad = collected(proj_pairs)
    moe_out = out_home[:, :width] + shared_out
    output = in_order(of_quarters((hidden_state + moe_out).astype(BF)), quarter)
    slot_sums = out_home[:, width : width + 3 * experts_total].reshape(own, 3, experts_total)
    slot_sums = jnp.sum(slot_sums, axis=1)
    gate_grad = jnp.sum(jnp.where(slot_hot, slot_sums[:, None, :], 0.0), axis=2)
    gate_grad = in_order(of_quarters(gate_grad), quarter)
    routed = [added([parts[0][m], near[m], routed_far[m]]) for m in range(2)]
    back_grads = lax.optimization_barrier(
        (back_grads, shared_parts, out_grad, output, routed[0], routed_far[1])
    )[0]

    back_out = project_back(
        place,
        back_grads,
        cosine,
        sine,
        tokens,
        normed_one,
        query_weight,
        key_weight,
        value_weight,
        groups,
        blocks,
        quarters,
    )
    gains = jnp.stack([back_out[1][0], second_gain_local]).reshape(2, blocks, cut).transpose(1, 0, 2)
    gains = jnp.broadcast_to(gains[:, None], (blocks, quarters, 2, cut)).reshape(units, 2, cut)
    gains = exchange(gains, BOTH)
    dx_parts = [back_out[0][0]] + [flip(back_out[0][k], k, "tensor") for k in range(1, quarters)]
    pair_q = paired(back_out[2], back_out[3])
    pair_k = paired(back_out[4], after(back_out[5], pair_q))
    dx_parts, pair_q = lax.optimization_barrier((tuple(dx_parts), pair_q))
    grad_one = added(dx_parts)
    pair_v = paired(back_out[6], after(back_out[7], pair_k))
    qkv_grads = [collected(p) for p in (pair_q, pair_k, pair_v)]
    first_scale = rms_scale(own_tokens)
    grad_first, _ = norm_backward(grad_one, own_tokens, first_scale, first_gain)
    input_mine = after((grad_hidden + grad_first).astype(BF), pair_k)
    input_grad = in_order(of_quarters(input_mine), quarter)
    shared = added([shared_parts[0]] + [flip(shared_parts[k], k, "tensor") for k in range(1, quarters)])
    gains = jnp.sum(after(gains, pair_v), axis=0)
    routed.append(added([parts[0][2], near[2], after(routed_far[2], pair_q)]))

    weight_shape = (heads, 2, pair_width, cut)
    return (
        output,
        input_grad,
        gate_grad,
        gains[0],
        gains[1],
        qkv_grads[0].T.reshape(weight_shape),
        qkv_grads[1].T.reshape(weight_shape),
        qkv_grads[2].T.reshape(weight_shape),
        out_grad.T.reshape(weight_shape),
        shared[0],
        shared[1],
        shared[2],
        routed[0],
        routed[1],
        routed[2],
    )


def solution(mesh):
    placed = (
        P("expert", None),
        P(),
        P("expert", None),
        P("expert", None),
        P(),
        P(),
        P(),
        P(None, None, "tensor", None),
        P(None, None, "tensor", None),
        P(None, None, "tensor", None),
        P(None, None, "tensor", None),
        P("tensor", None),
        P("tensor", None),
        P("tensor", None),
        P("expert", "tensor", None),
        P("expert", "tensor", None),
        P("expert", "tensor", None),
        P("expert", None),
    )
    return jax.shard_map(
        on_device,
        mesh=mesh,
        in_specs=placed,
        out_specs=(
            P("expert", None),
            P("expert", None),
            P("expert", None),
            P("expert"),
            P("expert"),
            P(None, None, "tensor", "expert"),
            P(None, None, "tensor", "expert"),
            P(None, None, "tensor", "expert"),
            P(None, None, "tensor", "expert"),
            P("tensor", "expert"),
            P("tensor", "expert"),
            P("tensor", "expert"),
            P("expert", "tensor", None),
            P("expert", "tensor", None),
            P("expert", "tensor", None),
        ),
        check_vma=False,
    )
```

```python
import jax
import jax.numpy as jnp
from jax import lax
from jax.experimental import pallas as pl
from jax.experimental.pallas import tpu as pltpu
from jax.sharding import PartitionSpec as P

HD = 128
REACH = 4
EPSILON = 1e-06
MASKED = -1e30
BF = jnp.bfloat16
F32 = jnp.float32
BOTH = ("expert", "tensor")
VMEM_LIMIT = 60 * 1024 * 1024


def dot(a, b, ca, cb):
    return lax.dot_general(a, b, (((ca,), (cb,)), ((), ())), preferred_element_type=F32)


def whole(shape):
    zeros = (0,) * len(shape)
    return pl.BlockSpec(shape, lambda *_: zeros)


def query_groups(blocks, groups):
    cost = [min(b, REACH) + 1 for b in range(blocks)]
    most = max(cost)
    while True:
        starts, load = [0], 0
        for b in range(blocks):
            if load + cost[b] > most:
                starts.append(b)
                load = 0
            load += cost[b]
        if len(starts) <= groups:
            break
        most += 1
    return starts + [blocks] * (groups + 2 - len(starts))


def rms_scale(values):
    return lax.rsqrt(jnp.mean(values * values, axis=-1, keepdims=True) + EPSILON)


def norm_backward(grad_out, values, inverse_rms, gain_vector):
    weighted = grad_out * gain_vector
    normal = values * inverse_rms
    gain_grad = jnp.sum(grad_out * normal, axis=0)
    grad_in = inverse_rms * (
        weighted - normal * jnp.mean(normal * weighted, axis=-1, keepdims=True)
    )
    return grad_in, gain_grad


def project(tokens, gain, wq, wk, wv, cosine, sine, units, groups):
    rows, width = tokens.shape
    heads = wq.shape[0]
    hw = wq.shape[1] * wq.shape[2]
    pw = wq.shape[2]

    def body(tok, gain_ref, q_ref, k_ref, v_ref, cos_ref, sin_ref, norm_ref, send_ref):
        x = tok[...].astype(F32)
        normed = (x * rms_scale(x) * gain_ref[...]).astype(BF)
        norm_ref[...] = normed
        cos = cos_ref[...]
        sin = sin_ref[...]
        for part, w_ref in enumerate((q_ref, k_ref, v_ref)):
            pre = dot(w_ref[...], normed, 1, 1)
            for h in range(heads):
                a = pre[h * hw : h * hw + pw]
                b = pre[h * hw + pw : (h + 1) * hw]
                if part < 2:
                    a, b = a * cos - b * sin, b * cos + a * sin
                chunk = jnp.concatenate([a, b], axis=0).astype(BF)
                for unit in range(h, units, heads):
                    send_ref[unit, part * hw : (part + 1) * hw] = chunk

    flat = (heads * hw, width)
    return pl.pallas_call(
        body,
        out_shape=(
            jax.ShapeDtypeStruct((rows, width), BF),
            jax.ShapeDtypeStruct((units, 3 * hw, rows), BF),
        ),
        compiler_params=pltpu.CompilerParams(vmem_limit_bytes=VMEM_LIMIT),
        name="project",
    )(tokens, gain[None], wq.reshape(flat), wk.reshape(flat), wv.reshape(flat), cosine, sine)


def allowed_pairs(seg_col, seg_row, query_block, key_block, rows):
    wide = jnp.concatenate([seg_col] * (rows // seg_col.shape[1]), axis=1)
    same = wide == seg_row
    ahead = lax.broadcasted_iota(jnp.int32, (rows, rows), 0) - lax.broadcasted_iota(
        jnp.int32, (rows, rows), 1
    )
    return same & (ahead + (query_block - key_block) * rows >= 0)


def attend(bounds, arrived, seg_col, seg_row, most):
    blocks, quarters, chunk, rows = arrived.shape
    hw = chunk // 3
    hd = quarters * hw
    scale = HD ** (-0.5)

    def part(ref, block, which):
        return ref[block, :, which * hw : (which + 1) * hw, :].reshape(hd, rows)

    def body(bounds_ref, arr_ref, col_ref, row_ref, out_ref, lse_ref, score_ref):
        query_block = bounds_ref[0] + pl.program_id(0)

        @pl.when(query_block < bounds_ref[1])
        def _():
            query = part(arr_ref, query_block, 0)
            col = col_ref[query_block]
            low = jnp.maximum(query_block - REACH, 0)

            def first(kb, best):
                s = dot(query, part(arr_ref, kb, 1), 0, 0) * scale
                s = jnp.where(allowed_pairs(col, row_ref[kb], query_block, kb, rows), s, MASKED)
                score_ref[kb - low] = s
                return jnp.maximum(best, jnp.max(s, axis=1, keepdims=True))

            best = lax.fori_loop(low, query_block + 1, first, jnp.full((rows, 1), MASKED, F32))

            def second(kb, carry):
                total, out = carry
                p = jnp.exp(score_ref[kb - low] - best)
                total = total + jnp.sum(p, axis=1, keepdims=True)
                return total, out + dot(p.astype(BF), part(arr_ref, kb, 2), 1, 1)

            total, out = lax.fori_loop(
                low, query_block + 1, second, (jnp.zeros((rows, 1), F32), jnp.zeros((rows, hd), F32))
            )
            out_ref[query_block] = (out / total).astype(BF)
            lse_ref[query_block] = jnp.broadcast_to(best + jnp.log(total), (rows, 128))

    grid_spec = pltpu.PrefetchScalarGridSpec(
        num_scalar_prefetch=1,
        grid=(most,),
        in_specs=[whole(arrived.shape), whole(seg_col.shape), whole(seg_row.shape)],
        out_specs=[whole((blocks, rows, hd)), whole((blocks, rows, 128))],
        scratch_shapes=[pltpu.VMEM((REACH + 1, rows, rows), F32)],
    )
    return pl.pallas_call(
        body,
        grid_spec=grid_spec,
        out_shape=(
            jax.ShapeDtypeStruct((blocks, rows, hd), BF),
            jax.ShapeDtypeStruct((blocks, rows, 128), F32),
        ),
        compiler_params=pltpu.CompilerParams(vmem_limit_bytes=VMEM_LIMIT),
        name="attend",
    )(bounds, arrived, seg_col, seg_row)


def attend_back(bounds, arrived, seg_col, seg_row, lse, grad_out, most):
    blocks, quarters, chunk, rows = arrived.shape
    hw = chunk // 3
    hd = quarters * hw
    scale = HD ** (-0.5)

    def part(ref, block, which):
        return ref[block, :, which * hw : (which + 1) * hw, :].reshape(hd, rows)

    def body(bounds_ref, arr_ref, col_ref, row_ref, lse_ref, do_ref, res_ref, prob_ref, dp_ref, dk_ref, dv_ref):
        step = pl.program_id(0)
        query_block = bounds_ref[0] + step

        @pl.when(step == 0)
        def _():
            res_ref[...] = jnp.zeros(res_ref.shape, BF)
            dk_ref[...] = jnp.zeros(dk_ref.shape, F32)
            dv_ref[...] = jnp.zeros(dv_ref.shape, F32)

        @pl.when(query_block < bounds_ref[1])
        def _():
            query = part(arr_ref, query_block, 0)
            col = col_ref[query_block]
            lse_now = jnp.concatenate([lse_ref[query_block]] * (rows // 128), axis=1)
            do = do_ref[query_block]
            low = jnp.maximum(query_block - REACH, 0)

            def first(kb, inner):
                s = dot(query, part(arr_ref, kb, 1), 0, 0) * scale
                ok = allowed_pairs(col, row_ref[kb], query_block, kb, rows)
                p = jnp.where(ok, jnp.exp(jnp.where(ok, s - lse_now, 0.0)), 0.0)
                dp = dot(do, part(arr_ref, kb, 2), 1, 0)
                prob_ref[kb - low] = p
                dp_ref[kb - low] = dp
                dv_ref[kb] += dot(do, p.astype(BF), 0, 0)
                return inner + jnp.sum(p * dp, axis=1, keepdims=True)

            inner = lax.fori_loop(low, query_block + 1, first, jnp.zeros((rows, 1), F32))

            def second(kb, dq):
                ds = (prob_ref[kb - low] * (dp_ref[kb - low] - inner)).astype(BF)
                dk_ref[kb] += dot(query, ds, 1, 0)
                return dq + dot(part(arr_ref, kb, 1), ds, 1, 1)

            dq = lax.fori_loop(low, query_block + 1, second, jnp.zeros((hd, rows), F32))
            res_ref[query_block, :, 0:hw, :] = (dq * scale).astype(BF).reshape(quarters, hw, rows)

        @pl.when(step == pl.num_programs(0) - 1)
        def _():
            for b in range(blocks):
                res_ref[b, :, hw : 2 * hw, :] = (dk_ref[b] * scale).astype(BF).reshape(quarters, hw, rows)
                res_ref[b, :, 2 * hw : 3 * hw, :] = dv_ref[b].astype(BF).reshape(quarters, hw, rows)

    grid_spec = pltpu.PrefetchScalarGridSpec(
        num_scalar_prefetch=1,
        grid=(most,),
        in_specs=[
            whole(arrived.shape),
            whole(seg_col.shape),
            whole(seg_row.shape),
            whole(lse.shape),
            whole(grad_out.shape),
        ],
        out_specs=whole(arrived.shape),
        scratch_shapes=[
            pltpu.VMEM((REACH + 1, rows, rows), F32),
            pltpu.VMEM((REACH + 1, rows, rows), F32),
            pltpu.VMEM((blocks, hd, rows), F32),
            pltpu.VMEM((blocks, hd, rows), F32),
        ],
    )
    return pl.pallas_call(
        body,
        grid_spec=grid_spec,
        out_shape=jax.ShapeDtypeStruct(arrived.shape, BF),
        compiler_params=pltpu.CompilerParams(vmem_limit_bytes=VMEM_LIMIT),
        name="attend_back",
    )(bounds, arrived, seg_col, seg_row, lse, grad_out)


def weight_specs(parts, hidden, width, mats):
    return [pl.BlockSpec((1, hidden, width), lambda s, *_: (s, 0, 0))] * (parts * mats)


def down_products(place, even, odd, first, count, width, downs):
    half, own, wide = even.shape
    parts = len(downs)
    slots, hidden, _ = downs[0].shape
    lanes = wide - width

    def body(place_ref, even_ref, odd_ref, *refs):
        da_ref, dy_ref, gate_ref = refs[parts:]

        @pl.when(pl.program_id(0) == 0)
        def _():
            for c in range(count // own // 2):
                at = place_ref[0] ^ (first + c)
                for parity in range(2):

                    @pl.when(place_ref[1] == parity)
                    def _():
                        for b, ref in ((2 * c + parity, even_ref), (2 * c + 1 - parity, odd_ref)):
                            dy_ref[b * own : (b + 1) * own] = ref[at, :, 0:width]
                            gate_ref[b * own : (b + 1) * own] = ref[at, :, width:wide]

        for k in range(parts):
            da_ref[0, k] = dot(dy_ref[...], refs[k][0], 1, 1)

    return pl.pallas_call(
        body,
        grid_spec=pltpu.PrefetchScalarGridSpec(
            num_scalar_prefetch=1,
            grid=(slots,),
            in_specs=[whole(even.shape), whole(odd.shape)] + weight_specs(parts, hidden, width, 1),
            out_specs=[
                pl.BlockSpec((1, parts, count, hidden), lambda s, *_: (s, 0, 0, 0)),
                whole((count, width)),
                whole((count, lanes)),
            ],
        ),
        out_shape=(
            jax.ShapeDtypeStruct((slots, parts, count, hidden), F32),
            jax.ShapeDtypeStruct((count, width), BF),
            jax.ShapeDtypeStruct((count, lanes), BF),
        ),
        compiler_params=pltpu.CompilerParams(vmem_limit_bytes=VMEM_LIMIT),
        name="down_products",
    )(place, even, odd, *downs)


def pieces(x):
    high = lax.reduce_precision(x, 8, 7)
    middle = lax.reduce_precision(x - high, 8, 7)
    return [high, middle, x - high - middle]


def swish_parts(g, u, da):
    sig = jax.nn.sigmoid(g)
    swish = g * sig
    return swish * u, da * u * (sig * (1.0 + g * (1.0 - sig))), da * swish


def experts_first(place, rows_in, down_prod, gates, gate_ws, up_ws, experts):
    count, width = rows_in.shape
    parts = len(gate_ws)
    slots, hidden, _ = gate_ws[0].shape
    lanes = gates.shape[1]

    def body(place_ref, x_ref, da_ref, gate_ref, *refs):
        gate_w, up_w = refs[:parts], refs[parts : 2 * parts]
        act_ref, dg_ref, du_ref, gg_ref, dx_ref, acc_ref, sum_ref = refs[2 * parts :]
        s = pl.program_id(0)
        x = x_ref[...]
        lane = lax.broadcasted_iota(jnp.int32, (count, lanes), 1)
        slot = place_ref[3] * slots + s
        mine = lane % experts == slot
        gate = jnp.sum(jnp.where(mine, gate_ref[...].astype(F32), 0.0), axis=1, keepdims=True)
        total = jnp.zeros((count, 1), F32)

        @pl.when(s == 0)
        def _():
            acc_ref[...] = jnp.zeros(acc_ref.shape, F32)
            sum_ref[...] = jnp.zeros(sum_ref.shape, F32)

        for k in range(parts):
            g = dot(x, gate_w[k][0], 1, 1)
            u = dot(x, up_w[k][0], 1, 1)
            da = da_ref[0, k]
            act, dg, du = swish_parts(g, u, da * gate)
            total = total + jnp.sum(act * da, axis=1, keepdims=True)
            act_ref[0, k] = (act * gate).astype(BF)
            dg_ref[0, k] = dg.astype(BF)
            du_ref[0, k] = du.astype(BF)
            acc_ref[...] += dot(dg_ref[0, k], gate_w[k][0], 1, 0) + dot(du_ref[0, k], up_w[k][0], 1, 0)

        high = total.astype(BF).astype(F32)
        middle = (total - high).astype(BF).astype(F32)
        for n, piece in enumerate((high, middle, total - high - middle)):
            sum_ref[...] += jnp.where(lane == n * experts + slot, piece, 0.0)

        @pl.when(s == slots - 1)
        def _():
            dx_ref[...] = acc_ref[...].astype(BF)
            gg_ref[...] = sum_ref[...].astype(BF)

    hid = jax.ShapeDtypeStruct((slots, parts, count, hidden), BF)
    hid_spec = pl.BlockSpec((1, parts, count, hidden), lambda s, *_: (s, 0, 0, 0))
    return pl.pallas_call(
        body,
        grid_spec=pltpu.PrefetchScalarGridSpec(
            num_scalar_prefetch=1,
            grid=(slots,),
            in_specs=[whole(rows_in.shape), hid_spec, whole(gates.shape)]
            + weight_specs(parts, hidden, width, 2),
            out_specs=[hid_spec, hid_spec, hid_spec, whole((count, lanes)), whole((count, width))],
            scratch_shapes=[pltpu.VMEM((count, width), F32), pltpu.VMEM((count, lanes), F32)],
        ),
        out_shape=(
            hid,
            hid,
            hid,
            jax.ShapeDtypeStruct((count, lanes), BF),
            jax.ShapeDtypeStruct((count, width), BF),
        ),
        compiler_params=pltpu.CompilerParams(vmem_limit_bytes=VMEM_LIMIT),
        name="experts_first",
    )(place, rows_in, down_prod, gates, *gate_ws, *up_ws)


def experts_second(place, rows_in, grads_in, sums, act, dgate, dup, downs, own):
    count, width = rows_in.shape
    parts = len(downs)
    slots, hidden, _ = downs[0].shape
    wide = width + sums.shape[1]
    half = count // own // 2

    def body(place_ref, x_ref, dy_ref, sum_ref, act_ref, dg_ref, du_ref, *refs):
        down_w = refs[:parts]
        low_ref, high_ref = refs[parts : parts + 2]
        grads = refs[parts + 2 : -1]
        acc_ref = refs[-1]
        s = pl.program_id(0)

        @pl.when(s == 0)
        def _():
            acc_ref[...] = jnp.zeros(acc_ref.shape, F32)

        for k in range(parts):
            acc_ref[...] += dot(act_ref[0, k], down_w[k][0], 1, 0)
            grads[k][0, 0] = dot(dg_ref[0, k], x_ref[...], 0, 0).astype(BF)
            grads[k][1, 0] = dot(du_ref[0, k], x_ref[...], 0, 0).astype(BF)
            grads[k][2, 0] = dot(act_ref[0, k], dy_ref[...], 0, 0).astype(BF)

        @pl.when(s == slots - 1)
        def _():
            for c in range(half):
                at = (place_ref[0] % half) ^ c
                for parity in range(2):

                    @pl.when(place_ref[1] == parity)
                    def _():
                        for b, ref in ((2 * c + parity, low_ref), (2 * c + 1 - parity, high_ref)):
                            ref[at, :, 0:width] = acc_ref[b * own : (b + 1) * own].astype(BF)
                            ref[at, :, width:wide] = sum_ref[b * own : (b + 1) * own]

    hid_spec = pl.BlockSpec((1, parts, count, hidden), lambda s, *_: (s, 0, 0, 0))
    out_shape = (half, own, wide)
    return pl.pallas_call(
        body,
        grid_spec=pltpu.PrefetchScalarGridSpec(
            num_scalar_prefetch=1,
            grid=(slots,),
            in_specs=[whole(rows_in.shape), whole(grads_in.shape), whole(sums.shape)]
            + [hid_spec] * 3
            + weight_specs(parts, hidden, width, 1),
            out_specs=[whole(out_shape)] * 2
            + [pl.BlockSpec((3, 1, hidden, width), lambda s, *_: (0, s, 0, 0))] * parts,
            scratch_shapes=[pltpu.VMEM((count, width), F32)],
        ),
        out_shape=(jax.ShapeDtypeStruct(out_shape, BF),) * 2
        + (jax.ShapeDtypeStruct((3, slots, hidden, width), BF),) * parts,
        compiler_params=pltpu.CompilerParams(vmem_limit_bytes=VMEM_LIMIT),
        name="experts_second",
    )(place, rows_in, grads_in, sums, act, dgate, dup, *downs)


def shared_own(rows, grads, weights):
    parts = len(weights)

    def body(x_ref, dy_ref, *refs):
        out_ref, dx_ref = refs[parts:]
        for k in range(parts):
            gw, uw, dw = refs[k][0], refs[k][1], refs[k][2]
            act, dg, du = swish_parts(
                dot(x_ref[...], gw, 1, 1),
                dot(x_ref[...], uw, 1, 1),
                dot(dy_ref[...], dw, 1, 1),
            )
            out = dot(act.astype(BF), dw, 1, 0)
            dx = dot(dg.astype(BF), gw, 1, 0) + dot(du.astype(BF), uw, 1, 0)
            if k == 0:
                out_ref[...] = out
                dx_ref[...] = dx
            else:
                out_ref[...] += out
                dx_ref[...] += dx

    shape = jax.ShapeDtypeStruct(rows.shape, F32)
    return pl.pallas_call(
        body,
        out_shape=(shape, shape),
        compiler_params=pltpu.CompilerParams(vmem_limit_bytes=VMEM_LIMIT),
        name="shared_own",
    )(rows, grads, *weights)


def shared_grads(rows_in, grads_in, rows_cut, grads_cut, weights):
    parts = len(weights)
    hidden = weights[0].shape[1]
    cut = rows_cut.shape[1]

    def body(x_ref, dy_ref, xc_ref, dyc_ref, *refs):
        out_ref = refs[parts]
        for k in range(parts):
            act, dg, du = swish_parts(
                dot(x_ref[...], refs[k][0], 1, 1),
                dot(x_ref[...], refs[k][1], 1, 1),
                dot(dy_ref[...], refs[k][2], 1, 1),
            )
            out_ref[k, 0] = dot(dg.astype(BF), xc_ref[...], 0, 0).astype(BF)
            out_ref[k, 1] = dot(du.astype(BF), xc_ref[...], 0, 0).astype(BF)
            out_ref[k, 2] = dot(act.astype(BF), dyc_ref[...], 0, 0).astype(BF)

    return pl.pallas_call(
        body,
        out_shape=jax.ShapeDtypeStruct((parts, 3, hidden, cut), BF),
        compiler_params=pltpu.CompilerParams(vmem_limit_bytes=VMEM_LIMIT),
        name="shared_grads",
    )(rows_in, grads_in, rows_cut, grads_cut, *weights)


def store_chunks(place_ref, value, low_ref, high_ref):
    half, cut, _ = low_ref.shape
    for c in range(half):
        first = value[2 * c * cut : (2 * c + 1) * cut]
        second = value[(2 * c + 1) * cut : (2 * c + 2) * cut]
        at = place_ref[0] ^ c
        even = place_ref[1] == 0
        low_ref[at] = jnp.where(even, first, second).astype(BF)
        high_ref[at] = jnp.where(even, second, first).astype(BF)


def output_grads(place, attn_parts, att_parts, heads, hw, blocks):
    parts = len(attn_parts)
    own, width = attn_parts[0].shape
    span = heads * hw
    full = att_parts[0].shape[1]
    hd = full // heads

    def body(place_ref, *refs):
        low_ref, high_ref = refs[2 * parts :]
        attn = jnp.concatenate([r[...] for r in refs[:parts]], axis=0)
        att = jnp.concatenate([r[...] for r in refs[parts : 2 * parts]], axis=0)
        row = lax.broadcasted_iota(jnp.int32, (full, span), 0)
        col = lax.broadcasted_iota(jnp.int32, (full, span), 1)
        source = (col // hw) * hd + place_ref[2] * hw + col % hw
        pick = jnp.where(row == source, 1.0, 0.0).astype(BF)
        mine = dot(att, pick, 1, 0).astype(BF)
        store_chunks(place_ref, dot(attn, mine, 0, 0), low_ref, high_ref)

    shape = (blocks // 2, width // blocks, span)
    return pl.pallas_call(
        body,
        grid_spec=pltpu.PrefetchScalarGridSpec(
            num_scalar_prefetch=1,
            grid=(1,),
            in_specs=[whole((own, width))] * parts + [whole((own, full))] * parts,
            out_specs=[whole(shape)] * 2,
        ),
        out_shape=(jax.ShapeDtypeStruct(shape, BF),) * 2,
        compiler_params=pltpu.CompilerParams(vmem_limit_bytes=VMEM_LIMIT),
        name="output_grads",
    )(place, *attn_parts, *att_parts)


def project_back(place, back, cosine, sine, tokens, normed, wq, wk, wv, groups, blocks, quarters):
    heads = wq.shape[0]
    pw = wq.shape[2]
    hw = 2 * pw
    rows, width = normed.shape
    own = rows // quarters
    span = heads * hw

    def body(place_ref, back_ref, cos_ref, sin_ref, tok_ref, norm_ref, q_ref, k_ref, v_ref, *refs):
        dx_ref, gain_ref = refs[:2]
        chunk_refs = refs[2:-1]
        grad_ref = refs[-1]
        cos = cos_ref[...]
        sin = sin_ref[...]
        for h in range(heads):
            total = back_ref[h].astype(F32)
            for r in range(1, groups):
                total = total + back_ref[r * heads + h].astype(F32)
            for part in range(3):
                a = total[part * hw : part * hw + pw]
                b = total[part * hw + pw : (part + 1) * hw]
                if part < 2:
                    a, b = a * cos + b * sin, b * cos - a * sin
                at = part * span + h * hw
                grad_ref[at : at + hw] = jnp.concatenate([a, b], axis=0).astype(BF)
        for part in range(3):
            value = dot(norm_ref[...], grad_ref[part * span : (part + 1) * span], 0, 1)
            store_chunks(place_ref, value, chunk_refs[2 * part], chunk_refs[2 * part + 1])
        dx = dot(grad_ref[0:span], q_ref[...], 0, 0)
        dx = dx + dot(grad_ref[span : 2 * span], k_ref[...], 0, 0)
        dx = dx + dot(grad_ref[2 * span :], v_ref[...], 0, 0)
        for j in range(quarters):
            dx_ref[place_ref[2] ^ j] = dx[j * own : (j + 1) * own].astype(BF)
        x = tok_ref[...].astype(F32)
        gain_ref[...] = jnp.sum(dx * (x * rms_scale(x)), axis=0, keepdims=True)

    flat = (span, width)
    chunk = (blocks // 2, width // blocks, span)
    return pl.pallas_call(
        body,
        grid_spec=pltpu.PrefetchScalarGridSpec(
            num_scalar_prefetch=1,
            grid=(1,),
            in_specs=[
                whole(back.shape),
                whole(cosine.shape),
                whole(sine.shape),
                whole(tokens.shape),
                whole(normed.shape),
                whole(flat),
                whole(flat),
                whole(flat),
            ],
            out_specs=[whole((quarters, own, width)), whole((1, width))] + [whole(chunk)] * 6,
            scratch_shapes=[pltpu.VMEM((3 * span, rows), BF)],
        ),
        out_shape=(
            jax.ShapeDtypeStruct((quarters, own, width), BF),
            jax.ShapeDtypeStruct((1, width), F32),
        )
        + (jax.ShapeDtypeStruct(chunk, BF),) * 6,
        compiler_params=pltpu.CompilerParams(vmem_limit_bytes=VMEM_LIMIT),
        name="project_back",
    )(place, back, cosine, sine, tokens, normed, wq.reshape(flat), wk.reshape(flat), wv.reshape(flat))


def after(x, *others):
    return lax.optimization_barrier((x,) + others)[0]


def added(parts):
    total = parts[0].astype(F32)
    for p in parts[1:]:
        total = total + p.astype(F32)
    return total


def flip(x, by, axis):
    size = lax.axis_size(axis)
    return lax.ppermute(x, axis, [(i, i ^ by) for i in range(size)])


def exchange(x, axis):
    return lax.all_to_all(x, axis, 0, 0, tiled=True)


def spread(x, axis):
    size = lax.axis_size(axis)
    return exchange(jnp.broadcast_to(x[None], (size,) + x.shape), axis)


def even_blocks(x):
    size = lax.axis_size("expert")
    return jnp.stack([x] + [flip(x, m, "expert") for m in range(2, size, 2)])


def odd_blocks(evens):
    return flip(evens, 1, "expert")


def paired(evens, odds, *others):
    got = after(flip(odds, 1, "expert"), *others) if others else flip(odds, 1, "expert")
    return (evens.astype(F32) + got.astype(F32)).astype(BF)


def collected(sums):
    return added([sums[0]] + [flip(sums[j], 2 * j, "expert") for j in range(1, sums.shape[0])])


def of_quarters(x):
    quarters = lax.axis_size("tensor")
    return [x] + [flip(x, k, "tensor") for k in range(1, quarters)]


def in_order(parts, quarter):
    out = jnp.zeros((len(parts),) + parts[0].shape, parts[0].dtype)
    for k, p in enumerate(parts):
        out = lax.dynamic_update_slice(out, p[None], (quarter ^ k,) + (0,) * p.ndim)
    return out.reshape((-1,) + parts[0].shape[1:])


def on_device(
    tokens,
    segment_ids,
    expert_ids,
    gate_values,
    expert_slot,
    first_gain,
    second_gain,
    query_weight,
    key_weight,
    value_weight,
    output_weight,
    shared_gate,
    shared_up,
    shared_down,
    routed_gate,
    routed_up,
    routed_down,
    cotangent,
):
    rows, width = tokens.shape
    top = expert_ids.shape[1]
    experts_total = expert_slot.shape[0]
    slots_local = routed_gate.shape[0]
    blocks = lax.axis_size("expert")
    quarters = lax.axis_size("tensor")
    rank = lax.axis_index("expert")
    quarter = lax.axis_index("tensor")
    heads = query_weight.shape[0]
    pair_width = query_weight.shape[2]
    hw = 2 * pair_width
    hd = quarters * hw
    units = blocks * quarters
    groups = units // heads
    own = rows // quarters
    cut = width // blocks
    starts = query_groups(blocks, groups)
    most = max(starts[i + 1] - starts[i] for i in range(groups))
    unit_group = [min(j // heads, groups) for j in range(units)]
    unit = rank * quarters + quarter
    low_table = jnp.array([starts[g] for g in unit_group], jnp.int32)
    high_table = jnp.array([starts[g + 1] if g < groups else starts[g] for g in unit_group], jnp.int32)
    bounds = jnp.stack([low_table[unit], high_table[unit]])
    block_group = jnp.array(
        [max(g for g in range(groups) if starts[g] <= b) for b in range(blocks)], jnp.int32
    )[rank]

    seg_mine = lax.dynamic_slice_in_dim(segment_ids, rank * rows, rows)
    doc_start = jnp.sum((segment_ids[:, None] < seg_mine[None, :]).astype(jnp.int32), axis=0)
    positions = rank * rows + jnp.arange(rows, dtype=jnp.int32) - doc_start
    freq_index = quarter * pair_width + jnp.arange(pair_width, dtype=jnp.int32)
    inverse_freq = 10000.0 ** (-2.0 * freq_index.astype(F32) / HD)
    angles = inverse_freq[:, None] * positions.astype(F32)[None, :]
    cosine = jnp.cos(angles)
    sine = jnp.sin(angles)
    seg_row = segment_ids.reshape(blocks, 1, rows)
    seg_col = jnp.broadcast_to(segment_ids.reshape(blocks, rows, 1), (blocks, rows, 128))

    normed_one, send = project(
        tokens, first_gain, query_weight, key_weight, value_weight, cosine, sine, units, groups
    )
    arrived = exchange(send, BOTH).reshape(blocks, quarters, 3 * hw, rows)

    def across(x):
        return flip(x, 2, "tensor")

    def beside(x):
        return flip(x, 1, "tensor")

    def all_quarters(x, far):
        return (x, beside(x), far, beside(far))

    out_mine = after(output_weight.reshape(heads, hw, width), normed_one)
    out_far = across(out_mine)
    gate_mine = after(routed_gate, out_far)
    gate_far = across(gate_mine)
    arrived = after(arrived, out_far)
    up_mine = after(routed_up, arrived)
    up_far = across(up_mine)
    out_ws = all_quarters(out_mine, out_far)
    out_full = jnp.zeros((heads, quarters, hw, width), BF)
    for k in range(quarters):
        out_full = lax.dynamic_update_slice(out_full, out_ws[k][:, None], (0, quarter ^ k, 0, 0))
    out_full = out_full.reshape(heads * hd, width)

    half = blocks // 2
    place = jnp.stack([rank // 2, rank % 2, quarter, rank])
    own_tokens = lax.dynamic_slice_in_dim(tokens, quarter * own, own).astype(F32)
    own_grads = lax.dynamic_slice_in_dim(cotangent, quarter * own, own)
    own_ids = lax.dynamic_slice_in_dim(expert_ids, quarter * own, own)
    own_gates = lax.dynamic_slice_in_dim(gate_values, quarter * own, own)
    onehot = own_ids[:, :, None] == jnp.arange(experts_total, dtype=jnp.int32)
    own_slots = jnp.sum(jnp.where(onehot, expert_slot[None, None, :], 0), axis=2)
    slot_hot = own_slots[:, :, None] == jnp.arange(experts_total, dtype=jnp.int32)
    dense_gates = jnp.sum(jnp.where(slot_hot, own_gates[:, :, None], 0.0), axis=1)
    lanes = -(-3 * experts_total // 128) * 128
    spare = jnp.zeros((own, lanes - 3 * experts_total), BF)
    own_wide = jnp.concatenate(
        [own_grads] + [p.astype(BF) for p in pieces(dense_gates)] + [spare], axis=1
    )
    grads_even = even_blocks(after(own_wide, arrived))
    grads_odd = odd_blocks(grads_even)

    attended_units, lse = attend(bounds, arrived, seg_col, seg_row, most)
    down_mine = after(routed_down, attended_units)
    down_far = across(down_mine)
    gate_ws = all_quarters(gate_mine, gate_far)
    up_ws = all_quarters(up_mine, up_far)
    down_ws = all_quarters(down_mine, down_far)
    back = exchange(attended_units.reshape(units, own, hd), BOTH)
    back = after(back, out_full, gate_far, grads_even)
    attended_heads = lax.dynamic_slice_in_dim(back, block_group * heads, heads)
    attended = attended_heads.transpose(1, 0, 2).reshape(own, heads * hd)
    hidden_state = own_tokens + jnp.dot(attended, out_full, preferred_element_type=F32)
    second_scale = rms_scale(hidden_state)
    normed_two = (hidden_state * second_scale * second_gain).astype(BF)

    rows_in = spread(normed_two, "expert").reshape(blocks * own, width)
    shared_mine = after(jnp.stack([shared_gate, shared_up, shared_down]), normed_two)
    shared_far = across(shared_mine)
    shared_near = beside(shared_mine)
    shared_ws = (shared_mine, shared_near, shared_far, beside(shared_far))

    total_rows = blocks * own
    step = min(total_rows, 512)
    spans = [slice(c, c + step) for c in range(0, total_rows, step)]
    prods = [
        down_products(place, grads_even, grads_odd, c.start // own // 2, step, width, down_ws)
        for c in spans
    ]
    firsts = [
        experts_first(place, rows_in[c], p[0], p[2], gate_ws, up_ws, experts_total)
        for c, p in zip(spans, prods)
    ]
    grads_in = jnp.concatenate([p[1] for p in prods], axis=0)
    grad_rows = jnp.concatenate([f[4] for f in firsts], axis=0)
    grad_home = exchange(grad_rows.reshape(blocks, own, width), "expert")

    seconds = []
    for c, f in zip(spans, firsts):
        act = lax.optimization_barrier((f[0], shared_far, shared_near))[0]
        seconds.append(
            experts_second(place, rows_in[c], grads_in[c], f[3], act, f[1], f[2], down_ws, own)
        )
    if len(seconds) == 1:
        out_low, out_high = seconds[0][:2]
        parts = seconds[0][2:]
    else:
        order = (rank // (step // own)) ^ jnp.arange(len(seconds), dtype=jnp.int32)
        out_low, out_high = (
            jnp.stack([s[i] for s in seconds])[order].reshape(half, own, width + lanes)
            for i in range(2)
        )
        parts = [added([s[2 + k] for s in seconds]).astype(BF) for k in range(quarters)]
    shared_out, shared_dx = shared_own(after(normed_two, out_low), own_grads, shared_ws)
    att_parts = of_quarters(after(attended, shared_far))

    out_pairs = paired(out_low, out_high, shared_dx)
    grad_home, out_pairs = lax.optimization_barrier(
        (grad_home, out_pairs, shared_dx, tuple(att_parts))
    )[:2]
    grad_norm_two = jnp.sum(grad_home.astype(F32), axis=0) + shared_dx
    grad_full = own_grads.astype(F32)
    grad_second, second_gain_local = norm_backward(
        grad_norm_two, hidden_state, second_scale, second_gain
    )
    grad_hidden = grad_full + grad_second
    grad_attn = grad_hidden.astype(BF)
    grad_attended = jnp.einsum(
        "td,hcd->htc", grad_attn, out_full.reshape(heads, hd, width), preferred_element_type=F32
    ).astype(BF)
    do_send = jnp.concatenate([grad_attended] * groups + [grad_attended[: units - groups * heads]], axis=0)
    do_units = exchange(do_send, BOTH).reshape(blocks, rows, hd)

    grad_attn_sent, out_pairs = lax.optimization_barrier((grad_attn, out_pairs, do_send))[:2]
    from_far = beside(after(parts[3], do_send))
    to_far = [(parts[2][m].astype(F32) + from_far[m].astype(F32)).astype(BF) for m in range(3)]
    near = beside(after(parts[1], from_far))
    routed_far = [across(to_far[0])]
    proj_low, proj_high = output_grads(
        place, of_quarters(grad_attn_sent), att_parts, heads, hw, blocks
    )
    do_units, to_far = lax.optimization_barrier((do_units, to_far, proj_low))[:2]

    grad_units = attend_back(bounds, arrived, seg_col, seg_row, lse, do_units, most)
    out_home = collected(out_pairs)
    proj_pairs = paired(proj_low, proj_high)
    grad_units = lax.optimization_barrier((grad_units, out_home, proj_pairs, routed_far[0]))[0]
    back_grads = exchange(grad_units.reshape(units, 3 * hw, rows), BOTH)

    rows_late, grads_late = lax.optimization_barrier((rows_in, grads_in, grad_units))[:2]
    rows_cut = lax.dynamic_slice_in_dim(rows_late, rank * cut, cut, axis=1)
    grads_cut = lax.dynamic_slice_in_dim(grads_late, rank * cut, cut, axis=1)
    shared_parts = [
        shared_grads(rows_late[c], grads_late[c], rows_cut[c], grads_cut[c], shared_ws) for c in spans
    ]
    shared_parts = shared_parts[0] if len(spans) == 1 else added(shared_parts).astype(BF)
    out_grad = collected(after(proj_pairs, grad_units))
    moe_out = out_home[:, :width] + shared_out
    slot_sums = out_home[:, width : width + 3 * experts_total].reshape(own, 3, experts_total)
    slot_sums = jnp.sum(slot_sums, axis=1)
    gate_grad = jnp.sum(jnp.where(slot_hot, slot_sums[:, None, :], 0.0), axis=2)
    final = [(hidden_state + moe_out).astype(BF)] + [p.astype(BF) for p in pieces(gate_grad)]
    final = jnp.concatenate(final + [jnp.zeros((own, 128 - 3 * top), BF)], axis=1)
    final = in_order(of_quarters(after(final, grad_units)), quarter)
    output = final[:, :width]
    gate_grad = jnp.sum(final[:, width : width + 3 * top].reshape(rows, 3, top).astype(F32), axis=1)
    routed = [added([parts[0][0], near[0], routed_far[0]])]
    back_grads = lax.optimization_barrier((back_grads, shared_parts, out_grad, output, routed[0]))[0]

    back_out = project_back(
        place,
        back_grads,
        cosine,
        sine,
        tokens,
        normed_one,
        query_weight,
        key_weight,
        value_weight,
        groups,
        blocks,
        quarters,
    )
    gains = jnp.stack([back_out[1][0], second_gain_local]).reshape(2, blocks, cut).transpose(1, 0, 2)
    gains = jnp.broadcast_to(gains[:, None], (blocks, quarters, 2, cut)).reshape(units, 2, cut)
    gains = exchange(gains, BOTH)
    dx_parts = [back_out[0][0]] + [flip(back_out[0][k], k, "tensor") for k in range(1, quarters)]
    pair_q = paired(back_out[2], back_out[3])
    pair_k = paired(back_out[4], after(back_out[5], pair_q))
    far_one = across(after(to_far[1], grad_units))
    dx_parts, pair_q, far_one = lax.optimization_barrier((tuple(dx_parts), pair_q, far_one))
    grad_one = added(dx_parts)
    pair_v = paired(back_out[6], after(back_out[7], pair_k))
    far_two = across(after(to_far[2], far_one))
    qkv_grads = [collected(p) for p in (pair_q, pair_k, pair_v)]
    first_scale = rms_scale(own_tokens)
    grad_first, _ = norm_backward(grad_one, own_tokens, first_scale, first_gain)
    input_mine = after((grad_hidden + grad_first).astype(BF), pair_v)
    input_grad = in_order(of_quarters(input_mine), quarter)
    shared = added([shared_parts[0]] + [flip(shared_parts[k], k, "tensor") for k in range(1, quarters)])
    gains = jnp.sum(after(gains, pair_v), axis=0)
    routed.append(added([parts[0][1], near[1], after(far_one, pair_v)]))
    routed.append(added([parts[0][2], near[2], far_two]))

    weight_shape = (heads, 2, pair_width, cut)
    return (
        output,
        input_grad,
        gate_grad,
        gains[0],
        gains[1],
        qkv_grads[0].T.reshape(weight_shape),
        qkv_grads[1].T.reshape(weight_shape),
        qkv_grads[2].T.reshape(weight_shape),
        out_grad.T.reshape(weight_shape),
        shared[0],
        shared[1],
        shared[2],
        routed[0],
        routed[1],
        routed[2],
    )


def solution(mesh):
    placed = (
        P("expert", None),
        P(),
        P("expert", None),
        P("expert", None),
        P(),
        P(),
        P(),
        P(None, None, "tensor", None),
        P(None, None, "tensor", None),
        P(None, None, "tensor", None),
        P(None, None, "tensor", None),
        P("tensor", None),
        P("tensor", None),
        P("tensor", None),
        P("expert", "tensor", None),
        P("expert", "tensor", None),
        P("expert", "tensor", None),
        P("expert", None),
    )
    return jax.shard_map(
        on_device,
        mesh=mesh,
        in_specs=placed,
        out_specs=(
            P("expert", None),
            P("expert", None),
            P("expert", None),
            P("expert"),
            P("expert"),
            P(None, None, "tensor", "expert"),
            P(None, None, "tensor", "expert"),
            P(None, None, "tensor", "expert"),
            P(None, None, "tensor", "expert"),
            P("tensor", "expert"),
            P("tensor", "expert"),
            P("tensor", "expert"),
            P("expert", "tensor", None),
            P("expert", "tensor", None),
            P("expert", "tensor", None),
        ),
        check_vma=False,
    )
```

```python
import jax
import jax.numpy as jnp
from jax import lax
from jax.experimental import pallas as pl
from jax.experimental.pallas import tpu as pltpu
from jax.sharding import PartitionSpec as P

HD = 128
REACH = 4
EPSILON = 1e-06
MASKED = -1e30
BF = jnp.bfloat16
F32 = jnp.float32
BOTH = ("expert", "tensor")
VMEM_LIMIT = 60 * 1024 * 1024


def dot(a, b, ca, cb):
    return lax.dot_general(a, b, (((ca,), (cb,)), ((), ())), preferred_element_type=F32)


def whole(shape):
    zeros = (0,) * len(shape)
    return pl.BlockSpec(shape, lambda *_: zeros)


def query_groups(blocks, groups):
    cost = [min(b, REACH) + 1 for b in range(blocks)]
    most = max(cost)
    while True:
        starts, load = [0], 0
        for b in range(blocks):
            if load + cost[b] > most:
                starts.append(b)
                load = 0
            load += cost[b]
        if len(starts) <= groups:
            break
        most += 1
    return starts + [blocks] * (groups + 2 - len(starts))


def rms_scale(values):
    return lax.rsqrt(jnp.mean(values * values, axis=-1, keepdims=True) + EPSILON)


def norm_backward(grad_out, values, inverse_rms, gain_vector):
    weighted = grad_out * gain_vector
    normal = values * inverse_rms
    gain_grad = jnp.sum(grad_out * normal, axis=0)
    grad_in = inverse_rms * (
        weighted - normal * jnp.mean(normal * weighted, axis=-1, keepdims=True)
    )
    return grad_in, gain_grad


def project(tokens, gain, wq, wk, wv, cosine, sine, units, groups):
    rows, width = tokens.shape
    heads = wq.shape[0]
    hw = wq.shape[1] * wq.shape[2]
    pw = wq.shape[2]

    def body(tok, gain_ref, q_ref, k_ref, v_ref, cos_ref, sin_ref, norm_ref, send_ref):
        x = tok[...].astype(F32)
        normed = (x * rms_scale(x) * gain_ref[...]).astype(BF)
        norm_ref[...] = normed
        cos = cos_ref[...]
        sin = sin_ref[...]
        for part, w_ref in enumerate((q_ref, k_ref, v_ref)):
            pre = dot(w_ref[...], normed, 1, 1)
            for h in range(heads):
                a = pre[h * hw : h * hw + pw]
                b = pre[h * hw + pw : (h + 1) * hw]
                if part < 2:
                    a, b = a * cos - b * sin, b * cos + a * sin
                chunk = jnp.concatenate([a, b], axis=0).astype(BF)
                for unit in range(h, units, heads):
                    send_ref[unit, part * hw : (part + 1) * hw] = chunk

    flat = (heads * hw, width)
    return pl.pallas_call(
        body,
        out_shape=(
            jax.ShapeDtypeStruct((rows, width), BF),
            jax.ShapeDtypeStruct((units, 3 * hw, rows), BF),
        ),
        compiler_params=pltpu.CompilerParams(vmem_limit_bytes=VMEM_LIMIT),
        name="project",
    )(tokens, gain[None], wq.reshape(flat), wk.reshape(flat), wv.reshape(flat), cosine, sine)


def allowed_pairs(seg_col, seg_row, query_block, key_block, rows):
    wide = jnp.concatenate([seg_col] * (rows // seg_col.shape[1]), axis=1)
    same = wide == seg_row
    ahead = lax.broadcasted_iota(jnp.int32, (rows, rows), 0) - lax.broadcasted_iota(
        jnp.int32, (rows, rows), 1
    )
    return same & (ahead + (query_block - key_block) * rows >= 0)


def attend(bounds, arrived, seg_col, seg_row, most):
    blocks, quarters, chunk, rows = arrived.shape
    hw = chunk // 3
    hd = quarters * hw
    scale = HD ** (-0.5)

    def part(ref, block, which):
        return ref[block, :, which * hw : (which + 1) * hw, :].reshape(hd, rows)

    def body(bounds_ref, arr_ref, col_ref, row_ref, out_ref, lse_ref, score_ref):
        query_block = bounds_ref[0] + pl.program_id(0)

        @pl.when(query_block < bounds_ref[1])
        def _():
            query = part(arr_ref, query_block, 0)
            col = col_ref[query_block]
            low = jnp.maximum(query_block - REACH, 0)

            def first(kb, best):
                s = dot(query, part(arr_ref, kb, 1), 0, 0) * scale
                s = jnp.where(allowed_pairs(col, row_ref[kb], query_block, kb, rows), s, MASKED)
                score_ref[kb - low] = s
                return jnp.maximum(best, jnp.max(s, axis=1, keepdims=True))

            best = lax.fori_loop(low, query_block + 1, first, jnp.full((rows, 1), MASKED, F32))

            def second(kb, carry):
                total, out = carry
                p = jnp.exp(score_ref[kb - low] - best)
                total = total + jnp.sum(p, axis=1, keepdims=True)
                return total, out + dot(p.astype(BF), part(arr_ref, kb, 2), 1, 1)

            total, out = lax.fori_loop(
                low, query_block + 1, second, (jnp.zeros((rows, 1), F32), jnp.zeros((rows, hd), F32))
            )
            out_ref[query_block] = (out / total).astype(BF)
            lse_ref[query_block] = jnp.broadcast_to(best + jnp.log(total), (rows, 128))

    grid_spec = pltpu.PrefetchScalarGridSpec(
        num_scalar_prefetch=1,
        grid=(most,),
        in_specs=[whole(arrived.shape), whole(seg_col.shape), whole(seg_row.shape)],
        out_specs=[whole((blocks, rows, hd)), whole((blocks, rows, 128))],
        scratch_shapes=[pltpu.VMEM((REACH + 1, rows, rows), F32)],
    )
    return pl.pallas_call(
        body,
        grid_spec=grid_spec,
        out_shape=(
            jax.ShapeDtypeStruct((blocks, rows, hd), BF),
            jax.ShapeDtypeStruct((blocks, rows, 128), F32),
        ),
        compiler_params=pltpu.CompilerParams(vmem_limit_bytes=VMEM_LIMIT),
        name="attend",
    )(bounds, arrived, seg_col, seg_row)


def attend_back(bounds, arrived, seg_col, seg_row, lse, grad_out, most):
    blocks, quarters, chunk, rows = arrived.shape
    hw = chunk // 3
    hd = quarters * hw
    scale = HD ** (-0.5)

    def part(ref, block, which):
        return ref[block, :, which * hw : (which + 1) * hw, :].reshape(hd, rows)

    def body(bounds_ref, arr_ref, col_ref, row_ref, lse_ref, do_ref, res_ref, prob_ref, dp_ref, dk_ref, dv_ref):
        step = pl.program_id(0)
        query_block = bounds_ref[0] + step

        @pl.when(step == 0)
        def _():
            res_ref[...] = jnp.zeros(res_ref.shape, BF)
            dk_ref[...] = jnp.zeros(dk_ref.shape, F32)
            dv_ref[...] = jnp.zeros(dv_ref.shape, F32)

        @pl.when(query_block < bounds_ref[1])
        def _():
            query = part(arr_ref, query_block, 0)
            col = col_ref[query_block]
            lse_now = jnp.concatenate([lse_ref[query_block]] * (rows // 128), axis=1)
            do = do_ref[query_block]
            low = jnp.maximum(query_block - REACH, 0)

            def first(kb, inner):
                s = dot(query, part(arr_ref, kb, 1), 0, 0) * scale
                ok = allowed_pairs(col, row_ref[kb], query_block, kb, rows)
                p = jnp.where(ok, jnp.exp(jnp.where(ok, s - lse_now, 0.0)), 0.0)
                dp = dot(do, part(arr_ref, kb, 2), 1, 0)
                prob_ref[kb - low] = p
                dp_ref[kb - low] = dp
                dv_ref[kb] += dot(do, p.astype(BF), 0, 0)
                return inner + jnp.sum(p * dp, axis=1, keepdims=True)

            inner = lax.fori_loop(low, query_block + 1, first, jnp.zeros((rows, 1), F32))

            def second(kb, dq):
                ds = (prob_ref[kb - low] * (dp_ref[kb - low] - inner)).astype(BF)
                dk_ref[kb] += dot(query, ds, 1, 0)
                return dq + dot(part(arr_ref, kb, 1), ds, 1, 1)

            dq = lax.fori_loop(low, query_block + 1, second, jnp.zeros((hd, rows), F32))
            res_ref[query_block, :, 0:hw, :] = (dq * scale).astype(BF).reshape(quarters, hw, rows)

        @pl.when(step == pl.num_programs(0) - 1)
        def _():
            for b in range(blocks):
                res_ref[b, :, hw : 2 * hw, :] = (dk_ref[b] * scale).astype(BF).reshape(quarters, hw, rows)
                res_ref[b, :, 2 * hw : 3 * hw, :] = dv_ref[b].astype(BF).reshape(quarters, hw, rows)

    grid_spec = pltpu.PrefetchScalarGridSpec(
        num_scalar_prefetch=1,
        grid=(most,),
        in_specs=[
            whole(arrived.shape),
            whole(seg_col.shape),
            whole(seg_row.shape),
            whole(lse.shape),
            whole(grad_out.shape),
        ],
        out_specs=whole(arrived.shape),
        scratch_shapes=[
            pltpu.VMEM((REACH + 1, rows, rows), F32),
            pltpu.VMEM((REACH + 1, rows, rows), F32),
            pltpu.VMEM((blocks, hd, rows), F32),
            pltpu.VMEM((blocks, hd, rows), F32),
        ],
    )
    return pl.pallas_call(
        body,
        grid_spec=grid_spec,
        out_shape=jax.ShapeDtypeStruct(arrived.shape, BF),
        compiler_params=pltpu.CompilerParams(vmem_limit_bytes=VMEM_LIMIT),
        name="attend_back",
    )(bounds, arrived, seg_col, seg_row, lse, grad_out)


def weight_specs(parts, hidden, width, mats):
    return [pl.BlockSpec((1, hidden, width), lambda s, *_: (s, 0, 0))] * (parts * mats)


def down_products(place, even, odd, first, count, width, downs):
    half, own, wide = even.shape
    parts = len(downs)
    slots, hidden, _ = downs[0].shape
    lanes = wide - width

    def body(place_ref, even_ref, odd_ref, *refs):
        da_ref, dy_ref, gate_ref = refs[parts:]

        @pl.when(pl.program_id(0) == 0)
        def _():
            for c in range(count // own // 2):
                at = place_ref[0] ^ (first + c)
                for parity in range(2):

                    @pl.when(place_ref[1] == parity)
                    def _():
                        for b, ref in ((2 * c + parity, even_ref), (2 * c + 1 - parity, odd_ref)):
                            dy_ref[b * own : (b + 1) * own] = ref[at, :, 0:width]
                            gate_ref[b * own : (b + 1) * own] = ref[at, :, width:wide]

        for k in range(parts):
            da_ref[0, k] = dot(dy_ref[...], refs[k][0], 1, 1)

    return pl.pallas_call(
        body,
        grid_spec=pltpu.PrefetchScalarGridSpec(
            num_scalar_prefetch=1,
            grid=(slots,),
            in_specs=[whole(even.shape), whole(odd.shape)] + weight_specs(parts, hidden, width, 1),
            out_specs=[
                pl.BlockSpec((1, parts, count, hidden), lambda s, *_: (s, 0, 0, 0)),
                whole((count, width)),
                whole((count, lanes)),
            ],
        ),
        out_shape=(
            jax.ShapeDtypeStruct((slots, parts, count, hidden), F32),
            jax.ShapeDtypeStruct((count, width), BF),
            jax.ShapeDtypeStruct((count, lanes), BF),
        ),
        compiler_params=pltpu.CompilerParams(vmem_limit_bytes=VMEM_LIMIT),
        name="down_products",
    )(place, even, odd, *downs)


def pieces(x):
    high = lax.reduce_precision(x, 8, 7)
    middle = lax.reduce_precision(x - high, 8, 7)
    return [high, middle, x - high - middle]


def swish_parts(g, u, da):
    sig = jax.nn.sigmoid(g)
    swish = g * sig
    return swish * u, da * u * (sig * (1.0 + g * (1.0 - sig))), da * swish


def experts_first(place, rows_in, down_prod, gates, gate_ws, up_ws, experts):
    count, width = rows_in.shape
    parts = len(gate_ws)
    slots, hidden, _ = gate_ws[0].shape
    lanes = gates.shape[1]

    def body(place_ref, x_ref, da_ref, gate_ref, *refs):
        gate_w, up_w = refs[:parts], refs[parts : 2 * parts]
        act_ref, dg_ref, du_ref, gg_ref, dx_ref, acc_ref, sum_ref = refs[2 * parts :]
        s = pl.program_id(0)
        x = x_ref[...]
        lane = lax.broadcasted_iota(jnp.int32, (count, lanes), 1)
        slot = place_ref[3] * slots + s
        mine = lane % experts == slot
        gate = jnp.sum(jnp.where(mine, gate_ref[...].astype(F32), 0.0), axis=1, keepdims=True)
        total = jnp.zeros((count, 1), F32)

        @pl.when(s == 0)
        def _():
            acc_ref[...] = jnp.zeros(acc_ref.shape, F32)
            sum_ref[...] = jnp.zeros(sum_ref.shape, F32)

        for k in range(parts):
            g = dot(x, gate_w[k][0], 1, 1)
            u = dot(x, up_w[k][0], 1, 1)
            da = da_ref[0, k]
            act, dg, du = swish_parts(g, u, da * gate)
            total = total + jnp.sum(act * da, axis=1, keepdims=True)
            act_ref[0, k] = (act * gate).astype(BF)
            dg_ref[0, k] = dg.astype(BF)
            du_ref[0, k] = du.astype(BF)
            acc_ref[...] += dot(dg_ref[0, k], gate_w[k][0], 1, 0) + dot(du_ref[0, k], up_w[k][0], 1, 0)

        high = total.astype(BF).astype(F32)
        middle = (total - high).astype(BF).astype(F32)
        for n, piece in enumerate((high, middle, total - high - middle)):
            sum_ref[...] += jnp.where(lane == n * experts + slot, piece, 0.0)

        @pl.when(s == slots - 1)
        def _():
            dx_ref[...] = acc_ref[...].astype(BF)
            gg_ref[...] = sum_ref[...].astype(BF)

    hid = jax.ShapeDtypeStruct((slots, parts, count, hidden), BF)
    hid_spec = pl.BlockSpec((1, parts, count, hidden), lambda s, *_: (s, 0, 0, 0))
    return pl.pallas_call(
        body,
        grid_spec=pltpu.PrefetchScalarGridSpec(
            num_scalar_prefetch=1,
            grid=(slots,),
            in_specs=[whole(rows_in.shape), hid_spec, whole(gates.shape)]
            + weight_specs(parts, hidden, width, 2),
            out_specs=[hid_spec, hid_spec, hid_spec, whole((count, lanes)), whole((count, width))],
            scratch_shapes=[pltpu.VMEM((count, width), F32), pltpu.VMEM((count, lanes), F32)],
        ),
        out_shape=(
            hid,
            hid,
            hid,
            jax.ShapeDtypeStruct((count, lanes), BF),
            jax.ShapeDtypeStruct((count, width), BF),
        ),
        compiler_params=pltpu.CompilerParams(vmem_limit_bytes=VMEM_LIMIT),
        name="experts_first",
    )(place, rows_in, down_prod, gates, *gate_ws, *up_ws)


def experts_second(place, rows_in, grads_in, sums, act, dgate, dup, downs, own):
    count, width = rows_in.shape
    parts = len(downs)
    slots, hidden, _ = downs[0].shape
    wide = width + sums.shape[1]
    half = count // own // 2

    def body(place_ref, x_ref, dy_ref, sum_ref, act_ref, dg_ref, du_ref, *refs):
        down_w = refs[:parts]
        low_ref, high_ref = refs[parts : parts + 2]
        grads = refs[parts + 2 : -1]
        acc_ref = refs[-1]
        s = pl.program_id(0)

        @pl.when(s == 0)
        def _():
            acc_ref[...] = jnp.zeros(acc_ref.shape, F32)

        for k in range(parts):
            acc_ref[...] += dot(act_ref[0, k], down_w[k][0], 1, 0)
            for m, (left, right) in enumerate(((dg_ref, x_ref), (du_ref, x_ref), (act_ref, dy_ref))):
                grad = dot(left[0, k], right[...], 0, 0).astype(BF)
                if k < parts - 1:
                    grads[k][m, 0] = grad
                else:
                    grads[k + m][0] = grad

        @pl.when(s == slots - 1)
        def _():
            for c in range(half):
                at = (place_ref[0] % half) ^ c
                for parity in range(2):

                    @pl.when(place_ref[1] == parity)
                    def _():
                        for b, ref in ((2 * c + parity, low_ref), (2 * c + 1 - parity, high_ref)):
                            ref[at, :, 0:width] = acc_ref[b * own : (b + 1) * own].astype(BF)
                            ref[at, :, width:wide] = sum_ref[b * own : (b + 1) * own]

    hid_spec = pl.BlockSpec((1, parts, count, hidden), lambda s, *_: (s, 0, 0, 0))
    out_shape = (half, own, wide)
    return pl.pallas_call(
        body,
        grid_spec=pltpu.PrefetchScalarGridSpec(
            num_scalar_prefetch=1,
            grid=(slots,),
            in_specs=[whole(rows_in.shape), whole(grads_in.shape), whole(sums.shape)]
            + [hid_spec] * 3
            + weight_specs(parts, hidden, width, 1),
            out_specs=[whole(out_shape)] * 2
            + [pl.BlockSpec((3, 1, hidden, width), lambda s, *_: (0, s, 0, 0))] * (parts - 1)
            + [pl.BlockSpec((1, hidden, width), lambda s, *_: (s, 0, 0))] * 3,
            scratch_shapes=[pltpu.VMEM((count, width), F32)],
        ),
        out_shape=(jax.ShapeDtypeStruct(out_shape, BF),) * 2
        + (jax.ShapeDtypeStruct((3, slots, hidden, width), BF),) * (parts - 1)
        + (jax.ShapeDtypeStruct((slots, hidden, width), BF),) * 3,
        compiler_params=pltpu.CompilerParams(vmem_limit_bytes=VMEM_LIMIT),
        name="experts_second",
    )(place, rows_in, grads_in, sums, act, dgate, dup, *downs)


def shared_own(rows, grads, weights):
    parts = len(weights)

    def body(x_ref, dy_ref, *refs):
        out_ref, dx_ref = refs[parts:]
        for k in range(parts):
            gw, uw, dw = refs[k][0], refs[k][1], refs[k][2]
            act, dg, du = swish_parts(
                dot(x_ref[...], gw, 1, 1),
                dot(x_ref[...], uw, 1, 1),
                dot(dy_ref[...], dw, 1, 1),
            )
            out = dot(act.astype(BF), dw, 1, 0)
            dx = dot(dg.astype(BF), gw, 1, 0) + dot(du.astype(BF), uw, 1, 0)
            if k == 0:
                out_ref[...] = out
                dx_ref[...] = dx
            else:
                out_ref[...] += out
                dx_ref[...] += dx

    shape = jax.ShapeDtypeStruct(rows.shape, F32)
    return pl.pallas_call(
        body,
        out_shape=(shape, shape),
        compiler_params=pltpu.CompilerParams(vmem_limit_bytes=VMEM_LIMIT),
        name="shared_own",
    )(rows, grads, *weights)


def shared_grads(rows_in, grads_in, rows_cut, grads_cut, weights):
    parts = len(weights)
    hidden = weights[0].shape[1]
    cut = rows_cut.shape[1]

    def body(x_ref, dy_ref, xc_ref, dyc_ref, *refs):
        out_ref = refs[parts]
        for k in range(parts):
            act, dg, du = swish_parts(
                dot(x_ref[...], refs[k][0], 1, 1),
                dot(x_ref[...], refs[k][1], 1, 1),
                dot(dy_ref[...], refs[k][2], 1, 1),
            )
            out_ref[k, 0] = dot(dg.astype(BF), xc_ref[...], 0, 0).astype(BF)
            out_ref[k, 1] = dot(du.astype(BF), xc_ref[...], 0, 0).astype(BF)
            out_ref[k, 2] = dot(act.astype(BF), dyc_ref[...], 0, 0).astype(BF)

    return pl.pallas_call(
        body,
        out_shape=jax.ShapeDtypeStruct((parts, 3, hidden, cut), BF),
        compiler_params=pltpu.CompilerParams(vmem_limit_bytes=VMEM_LIMIT),
        name="shared_grads",
    )(rows_in, grads_in, rows_cut, grads_cut, *weights)


def store_chunks(place_ref, value, low_ref, high_ref):
    half, cut, _ = low_ref.shape
    for c in range(half):
        first = value[2 * c * cut : (2 * c + 1) * cut]
        second = value[(2 * c + 1) * cut : (2 * c + 2) * cut]
        at = place_ref[0] ^ c
        even = place_ref[1] == 0
        low_ref[at] = jnp.where(even, first, second).astype(BF)
        high_ref[at] = jnp.where(even, second, first).astype(BF)


def output_grads(place, attn_parts, att_parts, heads, hw, blocks):
    parts = len(attn_parts)
    own, width = attn_parts[0].shape
    span = heads * hw
    full = att_parts[0].shape[1]
    hd = full // heads

    def body(place_ref, *refs):
        low_ref, high_ref = refs[2 * parts :]
        attn = jnp.concatenate([r[...] for r in refs[:parts]], axis=0)
        att = jnp.concatenate([r[...] for r in refs[parts : 2 * parts]], axis=0)
        row = lax.broadcasted_iota(jnp.int32, (full, span), 0)
        col = lax.broadcasted_iota(jnp.int32, (full, span), 1)
        source = (col // hw) * hd + place_ref[2] * hw + col % hw
        pick = jnp.where(row == source, 1.0, 0.0).astype(BF)
        mine = dot(att, pick, 1, 0).astype(BF)
        store_chunks(place_ref, dot(attn, mine, 0, 0), low_ref, high_ref)

    shape = (blocks // 2, width // blocks, span)
    return pl.pallas_call(
        body,
        grid_spec=pltpu.PrefetchScalarGridSpec(
            num_scalar_prefetch=1,
            grid=(1,),
            in_specs=[whole((own, width))] * parts + [whole((own, full))] * parts,
            out_specs=[whole(shape)] * 2,
        ),
        out_shape=(jax.ShapeDtypeStruct(shape, BF),) * 2,
        compiler_params=pltpu.CompilerParams(vmem_limit_bytes=VMEM_LIMIT),
        name="output_grads",
    )(place, *attn_parts, *att_parts)


def project_back(place, back, cosine, sine, tokens, normed, wq, wk, wv, groups, blocks, quarters):
    heads = wq.shape[0]
    pw = wq.shape[2]
    hw = 2 * pw
    rows, width = normed.shape
    own = rows // quarters
    span = heads * hw

    def body(place_ref, back_ref, cos_ref, sin_ref, tok_ref, norm_ref, q_ref, k_ref, v_ref, *refs):
        dx_ref, gain_ref = refs[:2]
        chunk_refs = refs[2:-1]
        grad_ref = refs[-1]
        cos = cos_ref[...]
        sin = sin_ref[...]
        for h in range(heads):
            total = back_ref[h].astype(F32)
            for r in range(1, groups):
                total = total + back_ref[r * heads + h].astype(F32)
            for part in range(3):
                a = total[part * hw : part * hw + pw]
                b = total[part * hw + pw : (part + 1) * hw]
                if part < 2:
                    a, b = a * cos + b * sin, b * cos - a * sin
                at = part * span + h * hw
                grad_ref[at : at + hw] = jnp.concatenate([a, b], axis=0).astype(BF)
        for part in range(3):
            value = dot(norm_ref[...], grad_ref[part * span : (part + 1) * span], 0, 1)
            store_chunks(place_ref, value, chunk_refs[2 * part], chunk_refs[2 * part + 1])
        dx = dot(grad_ref[0:span], q_ref[...], 0, 0)
        dx = dx + dot(grad_ref[span : 2 * span], k_ref[...], 0, 0)
        dx = dx + dot(grad_ref[2 * span :], v_ref[...], 0, 0)
        for j in range(quarters):
            dx_ref[place_ref[2] ^ j] = dx[j * own : (j + 1) * own].astype(BF)
        x = tok_ref[...].astype(F32)
        gain_ref[...] = jnp.sum(dx * (x * rms_scale(x)), axis=0, keepdims=True)

    flat = (span, width)
    chunk = (blocks // 2, width // blocks, span)
    return pl.pallas_call(
        body,
        grid_spec=pltpu.PrefetchScalarGridSpec(
            num_scalar_prefetch=1,
            grid=(1,),
            in_specs=[
                whole(back.shape),
                whole(cosine.shape),
                whole(sine.shape),
                whole(tokens.shape),
                whole(normed.shape),
                whole(flat),
                whole(flat),
                whole(flat),
            ],
            out_specs=[whole((quarters, own, width)), whole((1, width))] + [whole(chunk)] * 6,
            scratch_shapes=[pltpu.VMEM((3 * span, rows), BF)],
        ),
        out_shape=(
            jax.ShapeDtypeStruct((quarters, own, width), BF),
            jax.ShapeDtypeStruct((1, width), F32),
        )
        + (jax.ShapeDtypeStruct(chunk, BF),) * 6,
        compiler_params=pltpu.CompilerParams(vmem_limit_bytes=VMEM_LIMIT),
        name="project_back",
    )(place, back, cosine, sine, tokens, normed, wq.reshape(flat), wk.reshape(flat), wv.reshape(flat))


def after(x, *others):
    return lax.optimization_barrier((x,) + others)[0]


def added(parts):
    total = parts[0].astype(F32)
    for p in parts[1:]:
        total = total + p.astype(F32)
    return total


def flip(x, by, axis):
    size = lax.axis_size(axis)
    return lax.ppermute(x, axis, [(i, i ^ by) for i in range(size)])


def exchange(x, axis):
    return lax.all_to_all(x, axis, 0, 0, tiled=True)


def spread(x, axis):
    size = lax.axis_size(axis)
    return exchange(jnp.broadcast_to(x[None], (size,) + x.shape), axis)


def even_blocks(x):
    size = lax.axis_size("expert")
    return [x] + [flip(x, m, "expert") for m in range(2, size, 2)]


def odd_blocks(evens):
    return flip(evens, 1, "expert")


def paired(evens, odds):
    return added([evens, flip(odds, 1, "expert")]).astype(BF)


def collected(sums):
    return added([sums[0]] + [flip(sums[j], 2 * j, "expert") for j in range(1, sums.shape[0])])


def of_quarters(x):
    quarters = lax.axis_size("tensor")
    return [x] + [flip(x, k, "tensor") for k in range(1, quarters)]


def in_order(parts, quarter):
    out = jnp.zeros((len(parts),) + parts[0].shape, parts[0].dtype)
    for k, p in enumerate(parts):
        out = lax.dynamic_update_slice(out, p[None], (quarter ^ k,) + (0,) * p.ndim)
    return out.reshape((-1,) + parts[0].shape[1:])


def on_device(
    tokens,
    segment_ids,
    expert_ids,
    gate_values,
    expert_slot,
    first_gain,
    second_gain,
    query_weight,
    key_weight,
    value_weight,
    output_weight,
    shared_gate,
    shared_up,
    shared_down,
    routed_gate,
    routed_up,
    routed_down,
    cotangent,
):
    rows, width = tokens.shape
    top = expert_ids.shape[1]
    experts_total = expert_slot.shape[0]
    slots_local = routed_gate.shape[0]
    blocks = lax.axis_size("expert")
    quarters = lax.axis_size("tensor")
    rank = lax.axis_index("expert")
    quarter = lax.axis_index("tensor")
    heads = query_weight.shape[0]
    pair_width = query_weight.shape[2]
    hw = 2 * pair_width
    hd = quarters * hw
    units = blocks * quarters
    groups = units // heads
    own = rows // quarters
    cut = width // blocks
    starts = query_groups(blocks, groups)
    most = max(starts[i + 1] - starts[i] for i in range(groups))
    unit_group = [min(j // heads, groups) for j in range(units)]
    unit = rank * quarters + quarter
    low_table = jnp.array([starts[g] for g in unit_group], jnp.int32)
    high_table = jnp.array([starts[g + 1] if g < groups else starts[g] for g in unit_group], jnp.int32)
    bounds = jnp.stack([low_table[unit], high_table[unit]])
    block_group = jnp.array(
        [max(g for g in range(groups) if starts[g] <= b) for b in range(blocks)], jnp.int32
    )[rank]

    seg_mine = lax.dynamic_slice_in_dim(segment_ids, rank * rows, rows)
    doc_start = jnp.sum((segment_ids[:, None] < seg_mine[None, :]).astype(jnp.int32), axis=0)
    positions = rank * rows + jnp.arange(rows, dtype=jnp.int32) - doc_start
    freq_index = quarter * pair_width + jnp.arange(pair_width, dtype=jnp.int32)
    inverse_freq = 10000.0 ** (-2.0 * freq_index.astype(F32) / HD)
    angles = inverse_freq[:, None] * positions.astype(F32)[None, :]
    cosine = jnp.cos(angles)
    sine = jnp.sin(angles)
    seg_row = segment_ids.reshape(blocks, 1, rows)
    seg_col = jnp.broadcast_to(segment_ids.reshape(blocks, rows, 1), (blocks, rows, 128))

    normed_one, send = project(
        tokens, first_gain, query_weight, key_weight, value_weight, cosine, sine, units, groups
    )
    arrived = exchange(send, BOTH).reshape(blocks, quarters, 3 * hw, rows)

    def across(x):
        return flip(x, 2, "tensor")

    def beside(x):
        return flip(x, 1, "tensor")

    def all_quarters(x, far):
        return (x, beside(x), far, beside(far))

    out_mine = after(output_weight.reshape(heads, hw, width), normed_one)
    out_far = across(out_mine)
    gate_mine = after(routed_gate, out_far)
    gate_far = across(gate_mine)
    arrived = after(arrived, out_far)
    up_mine = after(routed_up, arrived)
    up_far = across(up_mine)
    out_ws = all_quarters(out_mine, out_far)
    out_full = jnp.zeros((heads, quarters, hw, width), BF)
    for k in range(quarters):
        out_full = lax.dynamic_update_slice(out_full, out_ws[k][:, None], (0, quarter ^ k, 0, 0))
    out_full = out_full.reshape(heads * hd, width)

    half = blocks // 2
    place = jnp.stack([rank // 2, rank % 2, quarter, rank])
    own_tokens = lax.dynamic_slice_in_dim(tokens, quarter * own, own).astype(F32)
    own_grads = lax.dynamic_slice_in_dim(cotangent, quarter * own, own)
    own_ids = lax.dynamic_slice_in_dim(expert_ids, quarter * own, own)
    own_gates = lax.dynamic_slice_in_dim(gate_values, quarter * own, own)
    onehot = own_ids[:, :, None] == jnp.arange(experts_total, dtype=jnp.int32)
    own_slots = jnp.sum(jnp.where(onehot, expert_slot[None, None, :], 0), axis=2)
    slot_hot = own_slots[:, :, None] == jnp.arange(experts_total, dtype=jnp.int32)
    dense_gates = jnp.sum(jnp.where(slot_hot, own_gates[:, :, None], 0.0), axis=1)
    lanes = -(-3 * experts_total // 128) * 128
    spare = jnp.zeros((own, lanes - 3 * experts_total), BF)
    own_wide = jnp.concatenate(
        [own_grads] + [p.astype(BF) for p in pieces(dense_gates)] + [spare], axis=1
    )
    grads_even = even_blocks(after(own_wide, arrived))

    attended_units, lse = attend(bounds, arrived, seg_col, seg_row, most)
    attended_units, grads_even = lax.optimization_barrier((attended_units, tuple(grads_even)))
    grads_even = jnp.stack(grads_even)
    grads_odd = odd_blocks(grads_even)
    down_mine = after(routed_down, attended_units)
    down_far = across(down_mine)
    gate_ws = all_quarters(gate_mine, gate_far)
    up_ws = all_quarters(up_mine, up_far)
    down_ws = all_quarters(down_mine, down_far)
    back = exchange(attended_units.reshape(units, own, hd), BOTH)
    back, grads_odd = lax.optimization_barrier((back, grads_odd, out_full, gate_far))[:2]
    attended_heads = lax.dynamic_slice_in_dim(back, block_group * heads, heads)
    attended = attended_heads.transpose(1, 0, 2).reshape(own, heads * hd)
    hidden_state = own_tokens + jnp.dot(attended, out_full, preferred_element_type=F32)
    second_scale = rms_scale(hidden_state)
    normed_two = (hidden_state * second_scale * second_gain).astype(BF)

    rows_in = spread(normed_two, "expert").reshape(blocks * own, width)
    shared_mine = after(jnp.stack([shared_gate, shared_up, shared_down]), normed_two)
    shared_far = across(shared_mine)
    shared_near = beside(shared_mine)
    shared_ws = (shared_mine, shared_near, shared_far, beside(shared_far))

    total_rows = blocks * own
    step = min(total_rows, 512)
    spans = [slice(c, c + step) for c in range(0, total_rows, step)]
    prods = [
        down_products(place, grads_even, grads_odd, c.start // own // 2, step, width, down_ws)
        for c in spans
    ]
    firsts = [
        experts_first(place, rows_in[c], p[0], p[2], gate_ws, up_ws, experts_total)
        for c, p in zip(spans, prods)
    ]
    grads_in = jnp.concatenate([p[1] for p in prods], axis=0)
    grad_rows = jnp.concatenate([f[4] for f in firsts], axis=0)
    grad_home = exchange(grad_rows.reshape(blocks, own, width), "expert")

    seconds = []
    for c, f in zip(spans, firsts):
        act = lax.optimization_barrier((f[0], shared_far, shared_near))[0]
        seconds.append(
            experts_second(place, rows_in[c], grads_in[c], f[3], act, f[1], f[2], down_ws, own)
        )
    if len(seconds) == 1:
        out_low, out_high = seconds[0][:2]
        parts = seconds[0][2:]
    else:
        order = (rank // (step // own)) ^ jnp.arange(len(seconds), dtype=jnp.int32)
        out_low, out_high = (
            jnp.stack([s[i] for s in seconds])[order].reshape(half, own, width + lanes)
            for i in range(2)
        )
        parts = [added([s[2 + k] for s in seconds]).astype(BF) for k in range(quarters + 2)]
    shared_out, shared_dx = shared_own(after(normed_two, out_low), own_grads, shared_ws)
    att_parts = of_quarters(after(attended, shared_far))

    to_far = [added([parts[2][0], beside(parts[3])]).astype(BF)]
    grad_home, to_far[0], att_parts = lax.optimization_barrier(
        (grad_home, to_far[0], tuple(att_parts), shared_dx)
    )[:3]
    grad_norm_two = jnp.sum(grad_home.astype(F32), axis=0) + shared_dx
    grad_full = own_grads.astype(F32)
    grad_second, second_gain_local = norm_backward(
        grad_norm_two, hidden_state, second_scale, second_gain
    )
    grad_hidden = grad_full + grad_second
    grad_attn = grad_hidden.astype(BF)
    grad_attended = jnp.einsum(
        "td,hcd->htc", grad_attn, out_full.reshape(heads, hd, width), preferred_element_type=F32
    ).astype(BF)
    out_got = flip(out_high, 1, "expert")
    grad_attended, out_got = lax.optimization_barrier((grad_attended, out_got))
    do_send = jnp.concatenate([grad_attended] * groups + [grad_attended[: units - groups * heads]], axis=0)
    do_units = exchange(do_send, BOTH).reshape(blocks, rows, hd)

    grad_attn_sent = after(grad_attn, do_send)
    routed_far = [across(to_far[0])]
    from_far = [beside(after(parts[3 + m], do_send)) for m in (1, 2)]
    routed_far[0], att_parts = lax.optimization_barrier((routed_far[0], att_parts))
    proj_low, proj_high = output_grads(
        place, of_quarters(grad_attn_sent), att_parts, heads, hw, blocks
    )
    from_far = lax.optimization_barrier((tuple(from_far), proj_low))[0]
    to_far += [added([parts[2][m], from_far[m - 1]]).astype(BF) for m in (1, 2)]
    near = beside(after(parts[1], from_far[1]))
    out_pairs = added([out_low, after(out_got, proj_low)]).astype(BF)
    do_units, out_pairs = lax.optimization_barrier((do_units, out_pairs, proj_low))[:2]

    grad_units = attend_back(bounds, arrived, seg_col, seg_row, lse, do_units, most)
    out_home = collected(out_pairs)
    proj_pairs = paired(proj_low, proj_high)
    grad_units = lax.optimization_barrier((grad_units, out_home, proj_pairs, routed_far[0]))[0]
    back_grads = exchange(grad_units.reshape(units, 3 * hw, rows), BOTH)

    rows_late, grads_late = lax.optimization_barrier((rows_in, grads_in, grad_units))[:2]
    rows_cut = lax.dynamic_slice_in_dim(rows_late, rank * cut, cut, axis=1)
    grads_cut = lax.dynamic_slice_in_dim(grads_late, rank * cut, cut, axis=1)
    shared_parts = [
        shared_grads(rows_late[c], grads_late[c], rows_cut[c], grads_cut[c], shared_ws) for c in spans
    ]
    shared_parts = shared_parts[0] if len(spans) == 1 else added(shared_parts).astype(BF)
    shared_gots = [flip(shared_parts[k], k, "tensor") for k in range(1, quarters)]
    out_grad = collected(after(proj_pairs, grad_units))
    moe_out = out_home[:, :width] + shared_out
    slot_sums = out_home[:, width : width + 3 * experts_total].reshape(own, 3, experts_total)
    slot_sums = jnp.sum(slot_sums, axis=1)
    gate_grad = jnp.sum(jnp.where(slot_hot, slot_sums[:, None, :], 0.0), axis=2)
    final = [(hidden_state + moe_out).astype(BF)] + [p.astype(BF) for p in pieces(gate_grad)]
    final = jnp.concatenate(final + [jnp.zeros((own, 128 - 3 * top), BF)], axis=1)
    final = in_order(of_quarters(after(final, grad_units)), quarter)
    output = final[:, :width]
    gate_grad = jnp.sum(final[:, width : width + 3 * top].reshape(rows, 3, top).astype(F32), axis=1)
    routed = [added([parts[0][0], near[0], routed_far[0]])]
    back_grads = lax.optimization_barrier((back_grads, shared_parts, out_grad, output, routed[0]))[0]

    back_out = project_back(
        place,
        back_grads,
        cosine,
        sine,
        tokens,
        normed_one,
        query_weight,
        key_weight,
        value_weight,
        groups,
        blocks,
        quarters,
    )
    gains = jnp.stack([back_out[1][0], second_gain_local]).reshape(2, blocks, cut).transpose(1, 0, 2)
    gains = jnp.broadcast_to(gains[:, None], (blocks, quarters, 2, cut)).reshape(units, 2, cut)
    gains = exchange(gains, BOTH)
    dx_parts = [back_out[0][0]] + [flip(back_out[0][k], k, "tensor") for k in range(1, quarters)]
    pair_q = paired(back_out[2], back_out[3])
    pair_k = paired(back_out[4], after(back_out[5], pair_q))
    far_one = across(lax.optimization_barrier((to_far[1], tuple(shared_gots)))[0])
    dx_parts, pair_q, far_one = lax.optimization_barrier((tuple(dx_parts), pair_q, far_one))
    grad_one = added(dx_parts)
    pair_v = paired(back_out[6], after(back_out[7], pair_k))
    far_two = across(after(to_far[2], far_one))
    qkv_grads = [collected(p) for p in (pair_q, pair_k, pair_v)]
    first_scale = rms_scale(own_tokens)
    grad_first, _ = norm_backward(grad_one, own_tokens, first_scale, first_gain)
    input_mine = after((grad_hidden + grad_first).astype(BF), pair_v)
    input_grad = in_order(of_quarters(input_mine), quarter)
    shared = added([shared_parts[0]] + shared_gots)
    gains = jnp.sum(after(gains, pair_v), axis=0)
    routed.append(added([parts[0][1], near[1], after(far_one, pair_v)]))
    routed.append(added([parts[0][2], near[2], far_two]))

    weight_shape = (heads, 2, pair_width, cut)
    return (
        output,
        input_grad,
        gate_grad,
        gains[0],
        gains[1],
        qkv_grads[0].T.reshape(weight_shape),
        qkv_grads[1].T.reshape(weight_shape),
        qkv_grads[2].T.reshape(weight_shape),
        out_grad.T.reshape(weight_shape),
        shared[0],
        shared[1],
        shared[2],
        routed[0],
        routed[1],
        routed[2],
    )


def solution(mesh):
    placed = (
        P("expert", None),
        P(),
        P("expert", None),
        P("expert", None),
        P(),
        P(),
        P(),
        P(None, None, "tensor", None),
        P(None, None, "tensor", None),
        P(None, None, "tensor", None),
        P(None, None, "tensor", None),
        P("tensor", None),
        P("tensor", None),
        P("tensor", None),
        P("expert", "tensor", None),
        P("expert", "tensor", None),
        P("expert", "tensor", None),
        P("expert", None),
    )
    return jax.shard_map(
        on_device,
        mesh=mesh,
        in_specs=placed,
        out_specs=(
            P("expert", None),
            P("expert", None),
            P("expert", None),
            P("expert"),
            P("expert"),
            P(None, None, "tensor", "expert"),
            P(None, None, "tensor", "expert"),
            P(None, None, "tensor", "expert"),
            P(None, None, "tensor", "expert"),
            P("tensor", "expert"),
            P("tensor", "expert"),
            P("tensor", "expert"),
            P("expert", "tensor", None),
            P("expert", "tensor", None),
            P("expert", "tensor", None),
        ),
        check_vma=False,
    )
```

```python
import jax
import jax.numpy as jnp
from jax import lax
from jax.experimental import pallas as pl
from jax.experimental.pallas import tpu as pltpu
from jax.sharding import PartitionSpec as P

HD = 128
REACH = 4
EPSILON = 1e-06
MASKED = -1e30
BF = jnp.bfloat16
F32 = jnp.float32
BOTH = ("expert", "tensor")
VMEM_LIMIT = 60 * 1024 * 1024


def dot(a, b, ca, cb):
    return lax.dot_general(a, b, (((ca,), (cb,)), ((), ())), preferred_element_type=F32)


def whole(shape):
    zeros = (0,) * len(shape)
    return pl.BlockSpec(shape, lambda *_: zeros)


def query_groups(blocks, groups):
    cost = [min(b, REACH) + 1 for b in range(blocks)]
    most = max(cost)
    while True:
        starts, load = [0], 0
        for b in range(blocks):
            if load + cost[b] > most:
                starts.append(b)
                load = 0
            load += cost[b]
        if len(starts) <= groups:
            break
        most += 1
    return starts + [blocks] * (groups + 2 - len(starts))


def rms_scale(values):
    return lax.rsqrt(jnp.mean(values * values, axis=-1, keepdims=True) + EPSILON)


def norm_backward(grad_out, values, inverse_rms, gain_vector):
    weighted = grad_out * gain_vector
    normal = values * inverse_rms
    gain_grad = jnp.sum(grad_out * normal, axis=0)
    grad_in = inverse_rms * (
        weighted - normal * jnp.mean(normal * weighted, axis=-1, keepdims=True)
    )
    return grad_in, gain_grad


def project(tokens, gain, wq, wk, wv, cosine, sine, units, groups):
    rows, width = tokens.shape
    heads = wq.shape[0]
    hw = wq.shape[1] * wq.shape[2]
    pw = wq.shape[2]

    def body(tok, gain_ref, q_ref, k_ref, v_ref, cos_ref, sin_ref, norm_ref, send_ref):
        x = tok[...].astype(F32)
        normed = (x * rms_scale(x) * gain_ref[...]).astype(BF)
        norm_ref[...] = normed
        cos = cos_ref[...]
        sin = sin_ref[...]
        for part, w_ref in enumerate((q_ref, k_ref, v_ref)):
            pre = dot(w_ref[...], normed, 1, 1)
            for h in range(heads):
                a = pre[h * hw : h * hw + pw]
                b = pre[h * hw + pw : (h + 1) * hw]
                if part < 2:
                    a, b = a * cos - b * sin, b * cos + a * sin
                chunk = jnp.concatenate([a, b], axis=0).astype(BF)
                for unit in range(h, units, heads):
                    send_ref[unit, part * hw : (part + 1) * hw] = chunk

    flat = (heads * hw, width)
    return pl.pallas_call(
        body,
        out_shape=(
            jax.ShapeDtypeStruct((rows, width), BF),
            jax.ShapeDtypeStruct((units, 3 * hw, rows), BF),
        ),
        compiler_params=pltpu.CompilerParams(vmem_limit_bytes=VMEM_LIMIT),
        name="project",
    )(tokens, gain[None], wq.reshape(flat), wk.reshape(flat), wv.reshape(flat), cosine, sine)


def allowed_pairs(seg_col, seg_row, query_block, key_block, rows):
    wide = jnp.concatenate([seg_col] * (rows // seg_col.shape[1]), axis=1)
    same = wide == seg_row
    ahead = lax.broadcasted_iota(jnp.int32, (rows, rows), 0) - lax.broadcasted_iota(
        jnp.int32, (rows, rows), 1
    )
    return same & (ahead + (query_block - key_block) * rows >= 0)


def attend(bounds, arrived, seg_col, seg_row, most):
    blocks, quarters, chunk, rows = arrived.shape
    hw = chunk // 3
    hd = quarters * hw
    scale = HD ** (-0.5)

    def part(ref, block, which):
        return ref[block, :, which * hw : (which + 1) * hw, :].reshape(hd, rows)

    def body(bounds_ref, arr_ref, col_ref, row_ref, out_ref, lse_ref, score_ref):
        query_block = bounds_ref[0] + pl.program_id(0)

        @pl.when(query_block < bounds_ref[1])
        def _():
            query = part(arr_ref, query_block, 0)
            col = col_ref[query_block]
            low = jnp.maximum(query_block - REACH, 0)

            def first(kb, best):
                s = dot(query, part(arr_ref, kb, 1), 0, 0) * scale
                s = jnp.where(allowed_pairs(col, row_ref[kb], query_block, kb, rows), s, MASKED)
                score_ref[kb - low] = s
                return jnp.maximum(best, jnp.max(s, axis=1, keepdims=True))

            best = lax.fori_loop(low, query_block + 1, first, jnp.full((rows, 1), MASKED, F32))

            def second(kb, carry):
                total, out = carry
                p = jnp.exp(score_ref[kb - low] - best)
                total = total + jnp.sum(p, axis=1, keepdims=True)
                return total, out + dot(p.astype(BF), part(arr_ref, kb, 2), 1, 1)

            total, out = lax.fori_loop(
                low, query_block + 1, second, (jnp.zeros((rows, 1), F32), jnp.zeros((rows, hd), F32))
            )
            out_ref[query_block] = (out / total).astype(BF)
            lse_ref[query_block] = jnp.broadcast_to(best + jnp.log(total), (rows, 128))

    grid_spec = pltpu.PrefetchScalarGridSpec(
        num_scalar_prefetch=1,
        grid=(most,),
        in_specs=[whole(arrived.shape), whole(seg_col.shape), whole(seg_row.shape)],
        out_specs=[whole((blocks, rows, hd)), whole((blocks, rows, 128))],
        scratch_shapes=[pltpu.VMEM((REACH + 1, rows, rows), F32)],
    )
    return pl.pallas_call(
        body,
        grid_spec=grid_spec,
        out_shape=(
            jax.ShapeDtypeStruct((blocks, rows, hd), BF),
            jax.ShapeDtypeStruct((blocks, rows, 128), F32),
        ),
        compiler_params=pltpu.CompilerParams(vmem_limit_bytes=VMEM_LIMIT),
        name="attend",
    )(bounds, arrived, seg_col, seg_row)


def attend_back(bounds, arrived, seg_col, seg_row, lse, grad_out, most):
    blocks, quarters, chunk, rows = arrived.shape
    hw = chunk // 3
    hd = quarters * hw
    scale = HD ** (-0.5)

    def part(ref, block, which):
        return ref[block, :, which * hw : (which + 1) * hw, :].reshape(hd, rows)

    def body(bounds_ref, arr_ref, col_ref, row_ref, lse_ref, do_ref, res_ref, prob_ref, dp_ref, dk_ref, dv_ref):
        step = pl.program_id(0)
        query_block = bounds_ref[0] + step

        @pl.when(step == 0)
        def _():
            res_ref[...] = jnp.zeros(res_ref.shape, BF)
            dk_ref[...] = jnp.zeros(dk_ref.shape, F32)
            dv_ref[...] = jnp.zeros(dv_ref.shape, F32)

        @pl.when(query_block < bounds_ref[1])
        def _():
            query = part(arr_ref, query_block, 0)
            col = col_ref[query_block]
            lse_now = jnp.concatenate([lse_ref[query_block]] * (rows // 128), axis=1)
            do = do_ref[query_block]
            low = jnp.maximum(query_block - REACH, 0)

            def first(kb, inner):
                s = dot(query, part(arr_ref, kb, 1), 0, 0) * scale
                ok = allowed_pairs(col, row_ref[kb], query_block, kb, rows)
                p = jnp.where(ok, jnp.exp(jnp.where(ok, s - lse_now, 0.0)), 0.0)
                dp = dot(do, part(arr_ref, kb, 2), 1, 0)
                prob_ref[kb - low] = p
                dp_ref[kb - low] = dp
                dv_ref[kb] += dot(do, p.astype(BF), 0, 0)
                return inner + jnp.sum(p * dp, axis=1, keepdims=True)

            inner = lax.fori_loop(low, query_block + 1, first, jnp.zeros((rows, 1), F32))

            def second(kb, dq):
                ds = (prob_ref[kb - low] * (dp_ref[kb - low] - inner)).astype(BF)
                dk_ref[kb] += dot(query, ds, 1, 0)
                return dq + dot(part(arr_ref, kb, 1), ds, 1, 1)

            dq = lax.fori_loop(low, query_block + 1, second, jnp.zeros((hd, rows), F32))
            res_ref[query_block, :, 0:hw, :] = (dq * scale).astype(BF).reshape(quarters, hw, rows)

        @pl.when(step == pl.num_programs(0) - 1)
        def _():
            for b in range(blocks):
                res_ref[b, :, hw : 2 * hw, :] = (dk_ref[b] * scale).astype(BF).reshape(quarters, hw, rows)
                res_ref[b, :, 2 * hw : 3 * hw, :] = dv_ref[b].astype(BF).reshape(quarters, hw, rows)

    grid_spec = pltpu.PrefetchScalarGridSpec(
        num_scalar_prefetch=1,
        grid=(most,),
        in_specs=[
            whole(arrived.shape),
            whole(seg_col.shape),
            whole(seg_row.shape),
            whole(lse.shape),
            whole(grad_out.shape),
        ],
        out_specs=whole(arrived.shape),
        scratch_shapes=[
            pltpu.VMEM((REACH + 1, rows, rows), F32),
            pltpu.VMEM((REACH + 1, rows, rows), F32),
            pltpu.VMEM((blocks, hd, rows), F32),
            pltpu.VMEM((blocks, hd, rows), F32),
        ],
    )
    return pl.pallas_call(
        body,
        grid_spec=grid_spec,
        out_shape=jax.ShapeDtypeStruct(arrived.shape, BF),
        compiler_params=pltpu.CompilerParams(vmem_limit_bytes=VMEM_LIMIT),
        name="attend_back",
    )(bounds, arrived, seg_col, seg_row, lse, grad_out)


def weight_specs(parts, hidden, width, mats):
    return [pl.BlockSpec((1, hidden, width), lambda s, *_: (s, 0, 0))] * (parts * mats)


def down_products(place, even, odd, first, count, width, downs):
    half, own, wide = even.shape
    parts = len(downs)
    slots, hidden, _ = downs[0].shape
    lanes = wide - width

    def body(place_ref, even_ref, odd_ref, *refs):
        da_ref, dy_ref, gate_ref = refs[parts:]

        @pl.when(pl.program_id(0) == 0)
        def _():
            for c in range(count // own // 2):
                at = place_ref[0] ^ (first + c)
                for parity in range(2):

                    @pl.when(place_ref[1] == parity)
                    def _():
                        for b, ref in ((2 * c + parity, even_ref), (2 * c + 1 - parity, odd_ref)):
                            dy_ref[b * own : (b + 1) * own] = ref[at, :, 0:width]
                            gate_ref[b * own : (b + 1) * own] = ref[at, :, width:wide]

        for k in range(parts):
            da_ref[0, k] = dot(dy_ref[...], refs[k][0], 1, 1)

    return pl.pallas_call(
        body,
        grid_spec=pltpu.PrefetchScalarGridSpec(
            num_scalar_prefetch=1,
            grid=(slots,),
            in_specs=[whole(even.shape), whole(odd.shape)] + weight_specs(parts, hidden, width, 1),
            out_specs=[
                pl.BlockSpec((1, parts, count, hidden), lambda s, *_: (s, 0, 0, 0)),
                whole((count, width)),
                whole((count, lanes)),
            ],
        ),
        out_shape=(
            jax.ShapeDtypeStruct((slots, parts, count, hidden), F32),
            jax.ShapeDtypeStruct((count, width), BF),
            jax.ShapeDtypeStruct((count, lanes), BF),
        ),
        compiler_params=pltpu.CompilerParams(vmem_limit_bytes=VMEM_LIMIT),
        name="down_products",
    )(place, even, odd, *downs)


def pieces(x):
    high = lax.reduce_precision(x, 8, 7)
    middle = lax.reduce_precision(x - high, 8, 7)
    return [high, middle, x - high - middle]


def swish_parts(g, u, da):
    sig = jax.nn.sigmoid(g)
    swish = g * sig
    return swish * u, da * u * (sig * (1.0 + g * (1.0 - sig))), da * swish


def experts_first(place, rows_in, down_prod, gates, gate_ws, up_ws, experts):
    count, width = rows_in.shape
    parts = len(gate_ws)
    slots, hidden, _ = gate_ws[0].shape
    lanes = gates.shape[1]

    def body(place_ref, x_ref, da_ref, gate_ref, *refs):
        gate_w, up_w = refs[:parts], refs[parts : 2 * parts]
        act_ref, dg_ref, du_ref, gg_ref, dx_ref, acc_ref, sum_ref = refs[2 * parts :]
        s = pl.program_id(0)
        x = x_ref[...]
        lane = lax.broadcasted_iota(jnp.int32, (count, lanes), 1)
        slot = place_ref[3] * slots + s
        mine = lane % experts == slot
        gate = jnp.sum(jnp.where(mine, gate_ref[...].astype(F32), 0.0), axis=1, keepdims=True)
        total = jnp.zeros((count, 1), F32)

        @pl.when(s == 0)
        def _():
            acc_ref[...] = jnp.zeros(acc_ref.shape, F32)
            sum_ref[...] = jnp.zeros(sum_ref.shape, F32)

        for k in range(parts):
            g = dot(x, gate_w[k][0], 1, 1)
            u = dot(x, up_w[k][0], 1, 1)
            da = da_ref[0, k]
            act, dg, du = swish_parts(g, u, da * gate)
            total = total + jnp.sum(act * da, axis=1, keepdims=True)
            act_ref[0, k] = (act * gate).astype(BF)
            dg_ref[0, k] = dg.astype(BF)
            du_ref[0, k] = du.astype(BF)
            acc_ref[...] += dot(dg_ref[0, k], gate_w[k][0], 1, 0) + dot(du_ref[0, k], up_w[k][0], 1, 0)

        high = total.astype(BF).astype(F32)
        middle = (total - high).astype(BF).astype(F32)
        for n, piece in enumerate((high, middle, total - high - middle)):
            sum_ref[...] += jnp.where(lane == n * experts + slot, piece, 0.0)

        @pl.when(s == slots - 1)
        def _():
            dx_ref[...] = acc_ref[...].astype(BF)
            gg_ref[...] = sum_ref[...].astype(BF)

    hid = jax.ShapeDtypeStruct((slots, parts, count, hidden), BF)
    hid_spec = pl.BlockSpec((1, parts, count, hidden), lambda s, *_: (s, 0, 0, 0))
    return pl.pallas_call(
        body,
        grid_spec=pltpu.PrefetchScalarGridSpec(
            num_scalar_prefetch=1,
            grid=(slots,),
            in_specs=[whole(rows_in.shape), hid_spec, whole(gates.shape)]
            + weight_specs(parts, hidden, width, 2),
            out_specs=[hid_spec, hid_spec, hid_spec, whole((count, lanes)), whole((count, width))],
            scratch_shapes=[pltpu.VMEM((count, width), F32), pltpu.VMEM((count, lanes), F32)],
        ),
        out_shape=(
            hid,
            hid,
            hid,
            jax.ShapeDtypeStruct((count, lanes), BF),
            jax.ShapeDtypeStruct((count, width), BF),
        ),
        compiler_params=pltpu.CompilerParams(vmem_limit_bytes=VMEM_LIMIT),
        name="experts_first",
    )(place, rows_in, down_prod, gates, *gate_ws, *up_ws)


def experts_second(place, rows_in, grads_in, sums, act, dgate, dup, downs, own):
    count, width = rows_in.shape
    parts = len(downs)
    slots, hidden, _ = downs[0].shape
    wide = width + sums.shape[1]
    half = count // own // 2

    def body(place_ref, x_ref, dy_ref, sum_ref, act_ref, dg_ref, du_ref, *refs):
        down_w = refs[:parts]
        low_ref, high_ref = refs[parts : parts + 2]
        grads = refs[parts + 2 : -1]
        acc_ref = refs[-1]
        s = pl.program_id(0)

        @pl.when(s == 0)
        def _():
            acc_ref[...] = jnp.zeros(acc_ref.shape, F32)

        for k in range(parts):
            acc_ref[...] += dot(act_ref[0, k], down_w[k][0], 1, 0)
            for m, (left, right) in enumerate(((dg_ref, x_ref), (du_ref, x_ref), (act_ref, dy_ref))):
                grad = dot(left[0, k], right[...], 0, 0).astype(BF)
                if k < parts - 1:
                    grads[k][m, 0] = grad
                else:
                    grads[k + m][0] = grad

        @pl.when(s == slots - 1)
        def _():
            for c in range(half):
                at = (place_ref[0] % half) ^ c
                for parity in range(2):

                    @pl.when(place_ref[1] == parity)
                    def _():
                        for b, ref in ((2 * c + parity, low_ref), (2 * c + 1 - parity, high_ref)):
                            ref[at, :, 0:width] = acc_ref[b * own : (b + 1) * own].astype(BF)
                            ref[at, :, width:wide] = sum_ref[b * own : (b + 1) * own]

    hid_spec = pl.BlockSpec((1, parts, count, hidden), lambda s, *_: (s, 0, 0, 0))
    out_shape = (half, own, wide)
    return pl.pallas_call(
        body,
        grid_spec=pltpu.PrefetchScalarGridSpec(
            num_scalar_prefetch=1,
            grid=(slots,),
            in_specs=[whole(rows_in.shape), whole(grads_in.shape), whole(sums.shape)]
            + [hid_spec] * 3
            + weight_specs(parts, hidden, width, 1),
            out_specs=[whole(out_shape)] * 2
            + [pl.BlockSpec((3, 1, hidden, width), lambda s, *_: (0, s, 0, 0))] * (parts - 1)
            + [pl.BlockSpec((1, hidden, width), lambda s, *_: (s, 0, 0))] * 3,
            scratch_shapes=[pltpu.VMEM((count, width), F32)],
        ),
        out_shape=(jax.ShapeDtypeStruct(out_shape, BF),) * 2
        + (jax.ShapeDtypeStruct((3, slots, hidden, width), BF),) * (parts - 1)
        + (jax.ShapeDtypeStruct((slots, hidden, width), BF),) * 3,
        compiler_params=pltpu.CompilerParams(vmem_limit_bytes=VMEM_LIMIT),
        name="experts_second",
    )(place, rows_in, grads_in, sums, act, dgate, dup, *downs)


def shared_own(rows, grads, weights):
    parts = len(weights)

    def body(x_ref, dy_ref, *refs):
        out_ref, dx_ref = refs[parts:]
        for k in range(parts):
            gw, uw, dw = refs[k][0], refs[k][1], refs[k][2]
            act, dg, du = swish_parts(
                dot(x_ref[...], gw, 1, 1),
                dot(x_ref[...], uw, 1, 1),
                dot(dy_ref[...], dw, 1, 1),
            )
            out = dot(act.astype(BF), dw, 1, 0)
            dx = dot(dg.astype(BF), gw, 1, 0) + dot(du.astype(BF), uw, 1, 0)
            if k == 0:
                out_ref[...] = out
                dx_ref[...] = dx
            else:
                out_ref[...] += out
                dx_ref[...] += dx

    shape = jax.ShapeDtypeStruct(rows.shape, F32)
    return pl.pallas_call(
        body,
        out_shape=(shape, shape),
        compiler_params=pltpu.CompilerParams(vmem_limit_bytes=VMEM_LIMIT),
        name="shared_own",
    )(rows, grads, *weights)


def shared_grads(rows_in, grads_in, rows_cut, grads_cut, weights):
    parts = len(weights)
    hidden = weights[0].shape[1]
    cut = rows_cut.shape[1]

    def body(x_ref, dy_ref, xc_ref, dyc_ref, *refs):
        out_ref = refs[parts]
        for k in range(parts):
            act, dg, du = swish_parts(
                dot(x_ref[...], refs[k][0], 1, 1),
                dot(x_ref[...], refs[k][1], 1, 1),
                dot(dy_ref[...], refs[k][2], 1, 1),
            )
            out_ref[k, 0] = dot(dg.astype(BF), xc_ref[...], 0, 0).astype(BF)
            out_ref[k, 1] = dot(du.astype(BF), xc_ref[...], 0, 0).astype(BF)
            out_ref[k, 2] = dot(act.astype(BF), dyc_ref[...], 0, 0).astype(BF)

    return pl.pallas_call(
        body,
        out_shape=jax.ShapeDtypeStruct((parts, 3, hidden, cut), BF),
        compiler_params=pltpu.CompilerParams(vmem_limit_bytes=VMEM_LIMIT),
        name="shared_grads",
    )(rows_in, grads_in, rows_cut, grads_cut, *weights)


def store_chunks(place_ref, value, low_ref, high_ref):
    half, cut, _ = low_ref.shape
    for c in range(half):
        first = value[2 * c * cut : (2 * c + 1) * cut]
        second = value[(2 * c + 1) * cut : (2 * c + 2) * cut]
        at = place_ref[0] ^ c
        even = place_ref[1] == 0
        low_ref[at] = jnp.where(even, first, second).astype(BF)
        high_ref[at] = jnp.where(even, second, first).astype(BF)


def output_grads(place, attn_parts, att_parts, heads, hw, blocks):
    parts = len(attn_parts)
    own, width = attn_parts[0].shape
    span = heads * hw
    full = att_parts[0].shape[1]
    hd = full // heads

    def body(place_ref, *refs):
        low_ref, high_ref = refs[2 * parts :]
        attn = jnp.concatenate([r[...] for r in refs[:parts]], axis=0)
        att = jnp.concatenate([r[...] for r in refs[parts : 2 * parts]], axis=0)
        row = lax.broadcasted_iota(jnp.int32, (full, span), 0)
        col = lax.broadcasted_iota(jnp.int32, (full, span), 1)
        source = (col // hw) * hd + place_ref[2] * hw + col % hw
        pick = jnp.where(row == source, 1.0, 0.0).astype(BF)
        mine = dot(att, pick, 1, 0).astype(BF)
        store_chunks(place_ref, dot(attn, mine, 0, 0), low_ref, high_ref)

    shape = (blocks // 2, width // blocks, span)
    return pl.pallas_call(
        body,
        grid_spec=pltpu.PrefetchScalarGridSpec(
            num_scalar_prefetch=1,
            grid=(1,),
            in_specs=[whole((own, width))] * parts + [whole((own, full))] * parts,
            out_specs=[whole(shape)] * 2,
        ),
        out_shape=(jax.ShapeDtypeStruct(shape, BF),) * 2,
        compiler_params=pltpu.CompilerParams(vmem_limit_bytes=VMEM_LIMIT),
        name="output_grads",
    )(place, *attn_parts, *att_parts)


def project_back(place, back, cosine, sine, tokens, normed, wq, wk, wv, groups, blocks, quarters):
    heads = wq.shape[0]
    pw = wq.shape[2]
    hw = 2 * pw
    rows, width = normed.shape
    own = rows // quarters
    span = heads * hw

    def body(place_ref, back_ref, cos_ref, sin_ref, tok_ref, norm_ref, q_ref, k_ref, v_ref, *refs):
        dx_ref, gain_ref = refs[:2]
        chunk_refs = refs[2:-1]
        grad_ref = refs[-1]
        cos = cos_ref[...]
        sin = sin_ref[...]
        for h in range(heads):
            total = back_ref[h].astype(F32)
            for r in range(1, groups):
                total = total + back_ref[r * heads + h].astype(F32)
            for part in range(3):
                a = total[part * hw : part * hw + pw]
                b = total[part * hw + pw : (part + 1) * hw]
                if part < 2:
                    a, b = a * cos + b * sin, b * cos - a * sin
                at = part * span + h * hw
                grad_ref[at : at + hw] = jnp.concatenate([a, b], axis=0).astype(BF)
        for part in range(3):
            value = dot(norm_ref[...], grad_ref[part * span : (part + 1) * span], 0, 1)
            store_chunks(place_ref, value, chunk_refs[2 * part], chunk_refs[2 * part + 1])
        dx = dot(grad_ref[0:span], q_ref[...], 0, 0)
        dx = dx + dot(grad_ref[span : 2 * span], k_ref[...], 0, 0)
        dx = dx + dot(grad_ref[2 * span :], v_ref[...], 0, 0)
        for j in range(quarters):
            dx_ref[place_ref[2] ^ j] = dx[j * own : (j + 1) * own].astype(BF)
        x = tok_ref[...].astype(F32)
        gain_ref[...] = jnp.sum(dx * (x * rms_scale(x)), axis=0, keepdims=True)

    flat = (span, width)
    chunk = (blocks // 2, width // blocks, span)
    return pl.pallas_call(
        body,
        grid_spec=pltpu.PrefetchScalarGridSpec(
            num_scalar_prefetch=1,
            grid=(1,),
            in_specs=[
                whole(back.shape),
                whole(cosine.shape),
                whole(sine.shape),
                whole(tokens.shape),
                whole(normed.shape),
                whole(flat),
                whole(flat),
                whole(flat),
            ],
            out_specs=[whole((quarters, own, width)), whole((1, width))] + [whole(chunk)] * 6,
            scratch_shapes=[pltpu.VMEM((3 * span, rows), BF)],
        ),
        out_shape=(
            jax.ShapeDtypeStruct((quarters, own, width), BF),
            jax.ShapeDtypeStruct((1, width), F32),
        )
        + (jax.ShapeDtypeStruct(chunk, BF),) * 6,
        compiler_params=pltpu.CompilerParams(vmem_limit_bytes=VMEM_LIMIT),
        name="project_back",
    )(place, back, cosine, sine, tokens, normed, wq.reshape(flat), wk.reshape(flat), wv.reshape(flat))


def after(x, *others):
    return lax.optimization_barrier((x,) + others)[0]


def added(parts):
    total = parts[0].astype(F32)
    for p in parts[1:]:
        total = total + p.astype(F32)
    return total


def flip(x, by, axis):
    size = lax.axis_size(axis)
    return lax.ppermute(x, axis, [(i, i ^ by) for i in range(size)])


def exchange(x, axis):
    return lax.all_to_all(x, axis, 0, 0, tiled=True)


def spread(x, axis):
    size = lax.axis_size(axis)
    return exchange(jnp.broadcast_to(x[None], (size,) + x.shape), axis)


def even_blocks(x):
    size = lax.axis_size("expert")
    return [x] + [flip(x, m, "expert") for m in range(2, size, 2)]


def odd_blocks(evens):
    return flip(evens, 1, "expert")


def paired(evens, odds):
    return added([evens, flip(odds, 1, "expert")]).astype(BF)


def collected(sums):
    return added([sums[0]] + [flip(sums[j], 2 * j, "expert") for j in range(1, sums.shape[0])])


def of_quarters(x):
    quarters = lax.axis_size("tensor")
    return [x] + [flip(x, k, "tensor") for k in range(1, quarters)]


def in_order(place, parts):
    count = len(parts)
    rows, width = parts[0].shape

    def body(place_ref, *refs):
        for k in range(count):
            refs[count][place_ref[2] ^ k] = refs[k][...]

    return pl.pallas_call(
        body,
        grid_spec=pltpu.PrefetchScalarGridSpec(
            num_scalar_prefetch=1,
            grid=(1,),
            in_specs=[whole((rows, width))] * count,
            out_specs=whole((count, rows, width)),
        ),
        out_shape=jax.ShapeDtypeStruct((count, rows, width), parts[0].dtype),
        compiler_params=pltpu.CompilerParams(vmem_limit_bytes=VMEM_LIMIT),
        name="in_order",
    )(place, *parts).reshape(count * rows, width)


def on_device(
    tokens,
    segment_ids,
    expert_ids,
    gate_values,
    expert_slot,
    first_gain,
    second_gain,
    query_weight,
    key_weight,
    value_weight,
    output_weight,
    shared_gate,
    shared_up,
    shared_down,
    routed_gate,
    routed_up,
    routed_down,
    cotangent,
):
    rows, width = tokens.shape
    top = expert_ids.shape[1]
    experts_total = expert_slot.shape[0]
    slots_local = routed_gate.shape[0]
    blocks = lax.axis_size("expert")
    quarters = lax.axis_size("tensor")
    rank = lax.axis_index("expert")
    quarter = lax.axis_index("tensor")
    heads = query_weight.shape[0]
    pair_width = query_weight.shape[2]
    hw = 2 * pair_width
    hd = quarters * hw
    units = blocks * quarters
    groups = units // heads
    own = rows // quarters
    cut = width // blocks
    starts = query_groups(blocks, groups)
    most = max(starts[i + 1] - starts[i] for i in range(groups))
    unit_group = [min(j // heads, groups) for j in range(units)]
    unit = rank * quarters + quarter
    low_table = jnp.array([starts[g] for g in unit_group], jnp.int32)
    high_table = jnp.array([starts[g + 1] if g < groups else starts[g] for g in unit_group], jnp.int32)
    bounds = jnp.stack([low_table[unit], high_table[unit]])
    block_group = jnp.array(
        [max(g for g in range(groups) if starts[g] <= b) for b in range(blocks)], jnp.int32
    )[rank]

    seg_mine = lax.dynamic_slice_in_dim(segment_ids, rank * rows, rows)
    doc_start = jnp.sum((segment_ids[:, None] < seg_mine[None, :]).astype(jnp.int32), axis=0)
    positions = rank * rows + jnp.arange(rows, dtype=jnp.int32) - doc_start
    freq_index = quarter * pair_width + jnp.arange(pair_width, dtype=jnp.int32)
    inverse_freq = 10000.0 ** (-2.0 * freq_index.astype(F32) / HD)
    angles = inverse_freq[:, None] * positions.astype(F32)[None, :]
    cosine = jnp.cos(angles)
    sine = jnp.sin(angles)
    seg_row = segment_ids.reshape(blocks, 1, rows)
    seg_col = jnp.broadcast_to(segment_ids.reshape(blocks, rows, 1), (blocks, rows, 128))

    normed_one, send = project(
        tokens, first_gain, query_weight, key_weight, value_weight, cosine, sine, units, groups
    )
    arrived = exchange(send, BOTH).reshape(blocks, quarters, 3 * hw, rows)

    def across(x):
        return flip(x, 2, "tensor")

    def beside(x):
        return flip(x, 1, "tensor")

    def all_quarters(x, far):
        return (x, beside(x), far, beside(far))

    out_mine = after(output_weight.reshape(heads, hw, width), normed_one)
    out_far = across(out_mine)
    gate_mine = after(routed_gate, out_far)
    gate_far = across(gate_mine)
    arrived = after(arrived, out_far)
    up_mine = after(routed_up, arrived)
    up_far = across(up_mine)
    out_ws = all_quarters(out_mine, out_far)
    out_full = jnp.zeros((heads, quarters, hw, width), BF)
    for k in range(quarters):
        out_full = lax.dynamic_update_slice(out_full, out_ws[k][:, None], (0, quarter ^ k, 0, 0))
    out_full = out_full.reshape(heads * hd, width)

    half = blocks // 2
    place = jnp.stack([rank // 2, rank % 2, quarter, rank])
    own_tokens = lax.dynamic_slice_in_dim(tokens, quarter * own, own).astype(F32)
    own_grads = lax.dynamic_slice_in_dim(cotangent, quarter * own, own)
    own_ids = lax.dynamic_slice_in_dim(expert_ids, quarter * own, own)
    own_gates = lax.dynamic_slice_in_dim(gate_values, quarter * own, own)
    onehot = own_ids[:, :, None] == jnp.arange(experts_total, dtype=jnp.int32)
    own_slots = jnp.sum(jnp.where(onehot, expert_slot[None, None, :], 0), axis=2)
    slot_hot = own_slots[:, :, None] == jnp.arange(experts_total, dtype=jnp.int32)
    dense_gates = jnp.sum(jnp.where(slot_hot, own_gates[:, :, None], 0.0), axis=1)
    lanes = -(-3 * experts_total // 128) * 128
    spare = jnp.zeros((own, lanes - 3 * experts_total), BF)
    own_wide = jnp.concatenate(
        [own_grads] + [p.astype(BF) for p in pieces(dense_gates)] + [spare], axis=1
    )
    grads_even = even_blocks(after(own_wide, arrived))

    attended_units, lse = attend(bounds, arrived, seg_col, seg_row, most)
    attended_units, grads_even = lax.optimization_barrier((attended_units, tuple(grads_even)))
    grads_even = jnp.stack(grads_even)
    grads_odd = odd_blocks(grads_even)
    down_mine = after(routed_down, attended_units)
    down_far = across(down_mine)
    gate_ws = all_quarters(gate_mine, gate_far)
    up_ws = all_quarters(up_mine, up_far)
    down_ws = all_quarters(down_mine, down_far)
    back = exchange(attended_units.reshape(units, own, hd), BOTH)
    back, grads_odd = lax.optimization_barrier((back, grads_odd, out_full, gate_far))[:2]
    attended_heads = lax.dynamic_slice_in_dim(back, block_group * heads, heads)
    attended = attended_heads.transpose(1, 0, 2).reshape(own, heads * hd)
    hidden_state = own_tokens + jnp.dot(attended, out_full, preferred_element_type=F32)
    second_scale = rms_scale(hidden_state)
    normed_two = (hidden_state * second_scale * second_gain).astype(BF)

    rows_in = spread(normed_two, "expert").reshape(blocks * own, width)
    shared_mine = after(jnp.stack([shared_gate, shared_up, shared_down]), normed_two)
    shared_far = across(shared_mine)
    shared_near = beside(shared_mine)
    shared_ws = (shared_mine, shared_near, shared_far, beside(shared_far))

    total_rows = blocks * own
    step = min(total_rows, 512)
    spans = [slice(c, c + step) for c in range(0, total_rows, step)]
    prods = [
        down_products(place, grads_even, grads_odd, c.start // own // 2, step, width, down_ws)
        for c in spans
    ]
    firsts = [
        experts_first(place, rows_in[c], p[0], p[2], gate_ws, up_ws, experts_total)
        for c, p in zip(spans, prods)
    ]
    grads_in = jnp.concatenate([p[1] for p in prods], axis=0)
    grad_rows = jnp.concatenate([f[4] for f in firsts], axis=0)
    grad_home = exchange(grad_rows.reshape(blocks, own, width), "expert")

    seconds = []
    for c, f in zip(spans, firsts):
        act = lax.optimization_barrier((f[0], shared_far, shared_near))[0]
        seconds.append(
            experts_second(place, rows_in[c], grads_in[c], f[3], act, f[1], f[2], down_ws, own)
        )
    if len(seconds) == 1:
        out_low, out_high = seconds[0][:2]
        parts = seconds[0][2:]
    else:
        order = (rank // (step // own)) ^ jnp.arange(len(seconds), dtype=jnp.int32)
        out_low, out_high = (
            jnp.stack([s[i] for s in seconds])[order].reshape(half, own, width + lanes)
            for i in range(2)
        )
        parts = [added([s[2 + k] for s in seconds]).astype(BF) for k in range(quarters + 2)]
    shared_out, shared_dx = shared_own(after(normed_two, out_low), own_grads, shared_ws)
    att_parts = of_quarters(after(attended, shared_far))

    to_far = [added([parts[2][0], beside(parts[3])]).astype(BF)]
    grad_home, to_far[0], att_parts = lax.optimization_barrier(
        (grad_home, to_far[0], tuple(att_parts), shared_dx)
    )[:3]
    grad_norm_two = jnp.sum(grad_home.astype(F32), axis=0) + shared_dx
    grad_full = own_grads.astype(F32)
    grad_second, second_gain_local = norm_backward(
        grad_norm_two, hidden_state, second_scale, second_gain
    )
    grad_hidden = grad_full + grad_second
    grad_attn = grad_hidden.astype(BF)
    grad_attended = jnp.einsum(
        "td,hcd->htc", grad_attn, out_full.reshape(heads, hd, width), preferred_element_type=F32
    ).astype(BF)
    out_got = flip(out_high, 1, "expert")
    grad_attended, out_got = lax.optimization_barrier((grad_attended, out_got))
    do_send = jnp.concatenate([grad_attended] * groups + [grad_attended[: units - groups * heads]], axis=0)
    do_units = exchange(do_send, BOTH).reshape(blocks, rows, hd)

    grad_attn_sent = after(grad_attn, do_send)
    routed_far = [across(to_far[0])]
    proj_low, proj_high = output_grads(
        place, of_quarters(grad_attn_sent), att_parts, heads, hw, blocks
    )
    out_pairs = added([out_low, after(out_got, proj_low)]).astype(BF)
    do_units, out_pairs = lax.optimization_barrier(
        (do_units, out_pairs, proj_low, routed_far[0])
    )[:2]

    grad_units = attend_back(bounds, arrived, seg_col, seg_row, lse, do_units, most)
    out_home = collected(out_pairs)
    proj_pairs = paired(proj_low, proj_high)
    grad_units = lax.optimization_barrier((grad_units, out_home, proj_pairs, routed_far[0]))[0]
    back_grads = exchange(grad_units.reshape(units, 3 * hw, rows), BOTH)

    from_far = [beside(after(parts[3 + m], grad_units)) for m in (1, 2)]
    to_far += [added([parts[2][m], from_far[m - 1]]).astype(BF) for m in (1, 2)]
    rows_late, grads_late = lax.optimization_barrier((rows_in, grads_in, grad_units))[:2]
    rows_cut = lax.dynamic_slice_in_dim(rows_late, rank * cut, cut, axis=1)
    grads_cut = lax.dynamic_slice_in_dim(grads_late, rank * cut, cut, axis=1)
    shared_parts = [
        shared_grads(rows_late[c], grads_late[c], rows_cut[c], grads_cut[c], shared_ws) for c in spans
    ]
    shared_parts = shared_parts[0] if len(spans) == 1 else added(shared_parts).astype(BF)
    shared_gots = [flip(shared_parts[k], k, "tensor") for k in range(1, quarters)]
    near = beside(after(parts[1], grad_units))
    out_grad = collected(after(proj_pairs, grad_units))
    moe_out = out_home[:, :width] + shared_out
    slot_sums = out_home[:, width : width + 3 * experts_total].reshape(own, 3, experts_total)
    slot_sums = jnp.sum(slot_sums, axis=1)
    gate_grad = jnp.sum(jnp.where(slot_hot, slot_sums[:, None, :], 0.0), axis=2)
    final = [(hidden_state + moe_out).astype(BF)] + [p.astype(BF) for p in pieces(gate_grad)]
    final = jnp.concatenate(final + [jnp.zeros((own, 128 - 3 * top), BF)], axis=1)
    final = in_order(place, of_quarters(after(final, grad_units)))
    output = final[:, :width]
    gate_grad = jnp.sum(final[:, width : width + 3 * top].reshape(rows, 3, top).astype(F32), axis=1)
    back_grads, near = lax.optimization_barrier((back_grads, near, shared_parts, out_grad, output))[:2]

    back_out = project_back(
        place,
        back_grads,
        cosine,
        sine,
        tokens,
        normed_one,
        query_weight,
        key_weight,
        value_weight,
        groups,
        blocks,
        quarters,
    )
    gains = jnp.stack([back_out[1][0], second_gain_local]).reshape(2, blocks, cut).transpose(1, 0, 2)
    gains = jnp.broadcast_to(gains[:, None], (blocks, quarters, 2, cut)).reshape(units, 2, cut)
    gains = exchange(gains, BOTH)
    dx_parts = [back_out[0][0]] + [flip(back_out[0][k], k, "tensor") for k in range(1, quarters)]
    pair_q = paired(back_out[2], back_out[3])
    pair_k = paired(back_out[4], after(back_out[5], pair_q))
    far_one = across(lax.optimization_barrier((to_far[1], output, tuple(shared_gots)))[0])
    dx_parts, pair_q = lax.optimization_barrier((tuple(dx_parts), pair_q))
    grad_one = added(dx_parts)
    far_two = across(after(to_far[2], far_one))
    routed = [added([parts[0][0], near[0], after(routed_far[0], pair_q)])]
    shared_gots = lax.optimization_barrier((tuple(shared_gots), pair_q))[0]
    shared = added([shared_parts[0], *shared_gots])
    pair_v = paired(back_out[6], after(back_out[7], pair_k))
    routed.append(added([parts[0][1], near[1], after(far_one, pair_k)]))
    pair_v, routed, shared = lax.optimization_barrier((pair_v, routed, shared))
    routed.append(added([parts[0][2], near[2], after(far_two, pair_v)]))
    qkv_grads = [collected(p) for p in (pair_q, pair_k, pair_v)]
    first_scale = rms_scale(own_tokens)
    grad_first, _ = norm_backward(grad_one, own_tokens, first_scale, first_gain)
    input_mine = after((grad_hidden + grad_first).astype(BF), pair_k)
    input_parts, routed[2] = lax.optimization_barrier((tuple(of_quarters(input_mine)), routed[2]))
    input_grad = in_order(place, input_parts)
    gains = jnp.sum(after(gains, pair_v), axis=0)

    weight_shape = (heads, 2, pair_width, cut)
    return (
        output,
        input_grad,
        gate_grad,
        gains[0],
        gains[1],
        qkv_grads[0].T.reshape(weight_shape),
        qkv_grads[1].T.reshape(weight_shape),
        qkv_grads[2].T.reshape(weight_shape),
        out_grad.T.reshape(weight_shape),
        shared[0],
        shared[1],
        shared[2],
        routed[0],
        routed[1],
        routed[2],
    )


def solution(mesh):
    placed = (
        P("expert", None),
        P(),
        P("expert", None),
        P("expert", None),
        P(),
        P(),
        P(),
        P(None, None, "tensor", None),
        P(None, None, "tensor", None),
        P(None, None, "tensor", None),
        P(None, None, "tensor", None),
        P("tensor", None),
        P("tensor", None),
        P("tensor", None),
        P("expert", "tensor", None),
        P("expert", "tensor", None),
        P("expert", "tensor", None),
        P("expert", None),
    )
    return jax.shard_map(
        on_device,
        mesh=mesh,
        in_specs=placed,
        out_specs=(
            P("expert", None),
            P("expert", None),
            P("expert", None),
            P("expert"),
            P("expert"),
            P(None, None, "tensor", "expert"),
            P(None, None, "tensor", "expert"),
            P(None, None, "tensor", "expert"),
            P(None, None, "tensor", "expert"),
            P("tensor", "expert"),
            P("tensor", "expert"),
            P("tensor", "expert"),
            P("expert", "tensor", None),
            P("expert", "tensor", None),
            P("expert", "tensor", None),
        ),
        check_vma=False,
    )
```

```python
import jax
import jax.numpy as jnp
from jax import lax
from jax.experimental import pallas as pl
from jax.experimental.pallas import tpu as pltpu
from jax.sharding import PartitionSpec as P

HD = 128
REACH = 4
EPSILON = 1e-06
MASKED = -1e30
BF = jnp.bfloat16
F32 = jnp.float32
BOTH = ("expert", "tensor")
VMEM_LIMIT = 60 * 1024 * 1024


def dot(a, b, ca, cb):
    return lax.dot_general(a, b, (((ca,), (cb,)), ((), ())), preferred_element_type=F32)


def whole(shape):
    zeros = (0,) * len(shape)
    return pl.BlockSpec(shape, lambda *_: zeros)


def query_groups(blocks, groups):
    cost = [min(b, REACH) + 1 for b in range(blocks)]
    most = max(cost)
    while True:
        starts, load = [0], 0
        for b in range(blocks):
            if load + cost[b] > most:
                starts.append(b)
                load = 0
            load += cost[b]
        if len(starts) <= groups:
            break
        most += 1
    return starts + [blocks] * (groups + 2 - len(starts))


def rms_scale(values):
    return lax.rsqrt(jnp.mean(values * values, axis=-1, keepdims=True) + EPSILON)


def norm_backward(grad_out, values, inverse_rms, gain_vector):
    weighted = grad_out * gain_vector
    normal = values * inverse_rms
    gain_grad = jnp.sum(grad_out * normal, axis=0)
    grad_in = inverse_rms * (
        weighted - normal * jnp.mean(normal * weighted, axis=-1, keepdims=True)
    )
    return grad_in, gain_grad


def project(tokens, gain, wq, wk, wv, cosine, sine, units, groups):
    rows, width = tokens.shape
    heads = wq.shape[0]
    hw = wq.shape[1] * wq.shape[2]
    pw = wq.shape[2]

    def body(tok, gain_ref, q_ref, k_ref, v_ref, cos_ref, sin_ref, norm_ref, send_ref):
        x = tok[...].astype(F32)
        normed = (x * rms_scale(x) * gain_ref[...]).astype(BF)
        norm_ref[...] = normed
        cos = cos_ref[...]
        sin = sin_ref[...]
        for part, w_ref in enumerate((q_ref, k_ref, v_ref)):
            pre = dot(w_ref[...], normed, 1, 1)
            for h in range(heads):
                a = pre[h * hw : h * hw + pw]
                b = pre[h * hw + pw : (h + 1) * hw]
                if part < 2:
                    a, b = a * cos - b * sin, b * cos + a * sin
                chunk = jnp.concatenate([a, b], axis=0).astype(BF)
                for unit in range(h, units, heads):
                    send_ref[unit, part * hw : (part + 1) * hw] = chunk

    flat = (heads * hw, width)
    return pl.pallas_call(
        body,
        out_shape=(
            jax.ShapeDtypeStruct((rows, width), BF),
            jax.ShapeDtypeStruct((units, 3 * hw, rows), BF),
        ),
        compiler_params=pltpu.CompilerParams(vmem_limit_bytes=VMEM_LIMIT),
        name="project",
    )(tokens, gain[None], wq.reshape(flat), wk.reshape(flat), wv.reshape(flat), cosine, sine)


def allowed_pairs(seg_col, seg_row, query_block, key_block, rows):
    wide = jnp.concatenate([seg_col] * (rows // seg_col.shape[1]), axis=1)
    same = wide == seg_row
    ahead = lax.broadcasted_iota(jnp.int32, (rows, rows), 0) - lax.broadcasted_iota(
        jnp.int32, (rows, rows), 1
    )
    return same & (ahead + (query_block - key_block) * rows >= 0)


def attend(bounds, arrived, seg_col, seg_row, most):
    blocks, quarters, chunk, rows = arrived.shape
    hw = chunk // 3
    hd = quarters * hw
    scale = HD ** (-0.5)

    def part(ref, block, which):
        return ref[block, :, which * hw : (which + 1) * hw, :].reshape(hd, rows)

    def body(bounds_ref, arr_ref, col_ref, row_ref, out_ref, lse_ref, score_ref):
        query_block = bounds_ref[0] + pl.program_id(0)

        @pl.when(query_block < bounds_ref[1])
        def _():
            query = part(arr_ref, query_block, 0)
            col = col_ref[query_block]
            low = jnp.maximum(query_block - REACH, 0)

            def first(kb, best):
                s = dot(query, part(arr_ref, kb, 1), 0, 0) * scale
                s = jnp.where(allowed_pairs(col, row_ref[kb], query_block, kb, rows), s, MASKED)
                score_ref[kb - low] = s
                return jnp.maximum(best, jnp.max(s, axis=1, keepdims=True))

            best = lax.fori_loop(low, query_block + 1, first, jnp.full((rows, 1), MASKED, F32))

            def second(kb, carry):
                total, out = carry
                p = jnp.exp(score_ref[kb - low] - best)
                total = total + jnp.sum(p, axis=1, keepdims=True)
                return total, out + dot(p.astype(BF), part(arr_ref, kb, 2), 1, 1)

            total, out = lax.fori_loop(
                low, query_block + 1, second, (jnp.zeros((rows, 1), F32), jnp.zeros((rows, hd), F32))
            )
            out_ref[query_block] = (out / total).astype(BF)
            lse_ref[query_block] = jnp.broadcast_to(best + jnp.log(total), (rows, 128))

    grid_spec = pltpu.PrefetchScalarGridSpec(
        num_scalar_prefetch=1,
        grid=(most,),
        in_specs=[whole(arrived.shape), whole(seg_col.shape), whole(seg_row.shape)],
        out_specs=[whole((blocks, rows, hd)), whole((blocks, rows, 128))],
        scratch_shapes=[pltpu.VMEM((REACH + 1, rows, rows), F32)],
    )
    return pl.pallas_call(
        body,
        grid_spec=grid_spec,
        out_shape=(
            jax.ShapeDtypeStruct((blocks, rows, hd), BF),
            jax.ShapeDtypeStruct((blocks, rows, 128), F32),
        ),
        compiler_params=pltpu.CompilerParams(vmem_limit_bytes=VMEM_LIMIT),
        name="attend",
    )(bounds, arrived, seg_col, seg_row)


def attend_back(bounds, arrived, seg_col, seg_row, lse, grad_out, most):
    blocks, quarters, chunk, rows = arrived.shape
    hw = chunk // 3
    hd = quarters * hw
    scale = HD ** (-0.5)

    def part(ref, block, which):
        return ref[block, :, which * hw : (which + 1) * hw, :].reshape(hd, rows)

    def body(bounds_ref, arr_ref, col_ref, row_ref, lse_ref, do_ref, res_ref, prob_ref, dp_ref, dk_ref, dv_ref):
        step = pl.program_id(0)
        query_block = bounds_ref[0] + step

        @pl.when(step == 0)
        def _():
            res_ref[...] = jnp.zeros(res_ref.shape, BF)
            dk_ref[...] = jnp.zeros(dk_ref.shape, F32)
            dv_ref[...] = jnp.zeros(dv_ref.shape, F32)

        @pl.when(query_block < bounds_ref[1])
        def _():
            query = part(arr_ref, query_block, 0)
            col = col_ref[query_block]
            lse_now = jnp.concatenate([lse_ref[query_block]] * (rows // 128), axis=1)
            do = do_ref[query_block]
            low = jnp.maximum(query_block - REACH, 0)

            def first(kb, inner):
                s = dot(query, part(arr_ref, kb, 1), 0, 0) * scale
                ok = allowed_pairs(col, row_ref[kb], query_block, kb, rows)
                p = jnp.where(ok, jnp.exp(jnp.where(ok, s - lse_now, 0.0)), 0.0)
                dp = dot(do, part(arr_ref, kb, 2), 1, 0)
                prob_ref[kb - low] = p
                dp_ref[kb - low] = dp
                dv_ref[kb] += dot(do, p.astype(BF), 0, 0)
                return inner + jnp.sum(p * dp, axis=1, keepdims=True)

            inner = lax.fori_loop(low, query_block + 1, first, jnp.zeros((rows, 1), F32))

            def second(kb, dq):
                ds = (prob_ref[kb - low] * (dp_ref[kb - low] - inner)).astype(BF)
                dk_ref[kb] += dot(query, ds, 1, 0)
                return dq + dot(part(arr_ref, kb, 1), ds, 1, 1)

            dq = lax.fori_loop(low, query_block + 1, second, jnp.zeros((hd, rows), F32))
            res_ref[query_block, :, 0:hw, :] = (dq * scale).astype(BF).reshape(quarters, hw, rows)

        @pl.when(step == pl.num_programs(0) - 1)
        def _():
            for b in range(blocks):
                res_ref[b, :, hw : 2 * hw, :] = (dk_ref[b] * scale).astype(BF).reshape(quarters, hw, rows)
                res_ref[b, :, 2 * hw : 3 * hw, :] = dv_ref[b].astype(BF).reshape(quarters, hw, rows)

    grid_spec = pltpu.PrefetchScalarGridSpec(
        num_scalar_prefetch=1,
        grid=(most,),
        in_specs=[
            whole(arrived.shape),
            whole(seg_col.shape),
            whole(seg_row.shape),
            whole(lse.shape),
            whole(grad_out.shape),
        ],
        out_specs=whole(arrived.shape),
        scratch_shapes=[
            pltpu.VMEM((REACH + 1, rows, rows), F32),
            pltpu.VMEM((REACH + 1, rows, rows), F32),
            pltpu.VMEM((blocks, hd, rows), F32),
            pltpu.VMEM((blocks, hd, rows), F32),
        ],
    )
    return pl.pallas_call(
        body,
        grid_spec=grid_spec,
        out_shape=jax.ShapeDtypeStruct(arrived.shape, BF),
        compiler_params=pltpu.CompilerParams(vmem_limit_bytes=VMEM_LIMIT),
        name="attend_back",
    )(bounds, arrived, seg_col, seg_row, lse, grad_out)


def weight_specs(parts, hidden, width, mats):
    return [pl.BlockSpec((1, hidden, width), lambda s, *_: (s, 0, 0))] * (parts * mats)


def down_products(place, even, odd, first, count, width, downs):
    half, own, wide = even.shape
    parts = len(downs)
    slots, hidden, _ = downs[0].shape
    lanes = wide - width

    def body(place_ref, even_ref, odd_ref, *refs):
        da_ref, dy_ref, gate_ref = refs[parts:]

        @pl.when(pl.program_id(0) == 0)
        def _():
            for c in range(count // own // 2):
                at = place_ref[0] ^ (first + c)
                for parity in range(2):

                    @pl.when(place_ref[1] == parity)
                    def _():
                        for b, ref in ((2 * c + parity, even_ref), (2 * c + 1 - parity, odd_ref)):
                            dy_ref[b * own : (b + 1) * own] = ref[at, :, 0:width]
                            gate_ref[b * own : (b + 1) * own] = ref[at, :, width:wide]

        for k in range(parts):
            da_ref[0, k] = dot(dy_ref[...], refs[k][0], 1, 1)

    return pl.pallas_call(
        body,
        grid_spec=pltpu.PrefetchScalarGridSpec(
            num_scalar_prefetch=1,
            grid=(slots,),
            in_specs=[whole(even.shape), whole(odd.shape)] + weight_specs(parts, hidden, width, 1),
            out_specs=[
                pl.BlockSpec((1, parts, count, hidden), lambda s, *_: (s, 0, 0, 0)),
                whole((count, width)),
                whole((count, lanes)),
            ],
        ),
        out_shape=(
            jax.ShapeDtypeStruct((slots, parts, count, hidden), F32),
            jax.ShapeDtypeStruct((count, width), BF),
            jax.ShapeDtypeStruct((count, lanes), BF),
        ),
        compiler_params=pltpu.CompilerParams(vmem_limit_bytes=VMEM_LIMIT),
        name="down_products",
    )(place, even, odd, *downs)


def pieces(x):
    high = lax.reduce_precision(x, 8, 7)
    middle = lax.reduce_precision(x - high, 8, 7)
    return [high, middle, x - high - middle]


def swish_parts(g, u, da):
    sig = jax.nn.sigmoid(g)
    swish = g * sig
    return swish * u, da * u * (sig * (1.0 + g * (1.0 - sig))), da * swish


def experts_first(place, rows_in, down_prod, gates, gate_ws, up_ws, experts):
    count, width = rows_in.shape
    parts = len(gate_ws)
    slots, hidden, _ = gate_ws[0].shape
    lanes = gates.shape[1]

    def body(place_ref, x_ref, da_ref, gate_ref, *refs):
        gate_w, up_w = refs[:parts], refs[parts : 2 * parts]
        act_ref, dg_ref, du_ref, gg_ref, dx_ref, acc_ref, sum_ref = refs[2 * parts :]
        s = pl.program_id(0)
        x = x_ref[...]
        lane = lax.broadcasted_iota(jnp.int32, (count, lanes), 1)
        slot = place_ref[3] * slots + s
        mine = lane % experts == slot
        gate = jnp.sum(jnp.where(mine, gate_ref[...].astype(F32), 0.0), axis=1, keepdims=True)
        total = jnp.zeros((count, 1), F32)

        @pl.when(s == 0)
        def _():
            acc_ref[...] = jnp.zeros(acc_ref.shape, F32)
            sum_ref[...] = jnp.zeros(sum_ref.shape, F32)

        for k in range(parts):
            g = dot(x, gate_w[k][0], 1, 1)
            u = dot(x, up_w[k][0], 1, 1)
            da = da_ref[0, k]
            act, dg, du = swish_parts(g, u, da * gate)
            total = total + jnp.sum(act * da, axis=1, keepdims=True)
            act_ref[0, k] = (act * gate).astype(BF)
            dg_ref[0, k] = dg.astype(BF)
            du_ref[0, k] = du.astype(BF)
            acc_ref[...] += dot(dg_ref[0, k], gate_w[k][0], 1, 0) + dot(du_ref[0, k], up_w[k][0], 1, 0)

        high = total.astype(BF).astype(F32)
        middle = (total - high).astype(BF).astype(F32)
        for n, piece in enumerate((high, middle, total - high - middle)):
            sum_ref[...] += jnp.where(lane == n * experts + slot, piece, 0.0)

        @pl.when(s == slots - 1)
        def _():
            dx_ref[...] = acc_ref[...].astype(BF)
            gg_ref[...] = sum_ref[...].astype(BF)

    hid = jax.ShapeDtypeStruct((slots, parts, count, hidden), BF)
    hid_spec = pl.BlockSpec((1, parts, count, hidden), lambda s, *_: (s, 0, 0, 0))
    return pl.pallas_call(
        body,
        grid_spec=pltpu.PrefetchScalarGridSpec(
            num_scalar_prefetch=1,
            grid=(slots,),
            in_specs=[whole(rows_in.shape), hid_spec, whole(gates.shape)]
            + weight_specs(parts, hidden, width, 2),
            out_specs=[hid_spec, hid_spec, hid_spec, whole((count, lanes)), whole((count, width))],
            scratch_shapes=[pltpu.VMEM((count, width), F32), pltpu.VMEM((count, lanes), F32)],
        ),
        out_shape=(
            hid,
            hid,
            hid,
            jax.ShapeDtypeStruct((count, lanes), BF),
            jax.ShapeDtypeStruct((count, width), BF),
        ),
        compiler_params=pltpu.CompilerParams(vmem_limit_bytes=VMEM_LIMIT),
        name="experts_first",
    )(place, rows_in, down_prod, gates, *gate_ws, *up_ws)


def experts_second(place, rows_in, grads_in, sums, act, dgate, dup, downs, own):
    count, width = rows_in.shape
    parts = len(downs)
    slots, hidden, _ = downs[0].shape
    wide = width + sums.shape[1]
    half = count // own // 2

    def body(place_ref, x_ref, dy_ref, sum_ref, act_ref, dg_ref, du_ref, *refs):
        down_w = refs[:parts]
        low_ref, high_ref = refs[parts : parts + 2]
        grads = refs[parts + 2 : -1]
        acc_ref = refs[-1]
        s = pl.program_id(0)

        @pl.when(s == 0)
        def _():
            acc_ref[...] = jnp.zeros(acc_ref.shape, F32)

        for k in range(parts):
            acc_ref[...] += dot(act_ref[0, k], down_w[k][0], 1, 0)
            for m, (left, right) in enumerate(((dg_ref, x_ref), (du_ref, x_ref), (act_ref, dy_ref))):
                grad = dot(left[0, k], right[...], 0, 0).astype(BF)
                if k < parts - 1:
                    grads[k][m, 0] = grad
                else:
                    grads[k + m][0] = grad

        @pl.when(s == slots - 1)
        def _():
            for c in range(half):
                at = (place_ref[0] % half) ^ c
                for parity in range(2):

                    @pl.when(place_ref[1] == parity)
                    def _():
                        for b, ref in ((2 * c + parity, low_ref), (2 * c + 1 - parity, high_ref)):
                            ref[at, :, 0:width] = acc_ref[b * own : (b + 1) * own].astype(BF)
                            ref[at, :, width:wide] = sum_ref[b * own : (b + 1) * own]

    hid_spec = pl.BlockSpec((1, parts, count, hidden), lambda s, *_: (s, 0, 0, 0))
    out_shape = (half, own, wide)
    return pl.pallas_call(
        body,
        grid_spec=pltpu.PrefetchScalarGridSpec(
            num_scalar_prefetch=1,
            grid=(slots,),
            in_specs=[whole(rows_in.shape), whole(grads_in.shape), whole(sums.shape)]
            + [hid_spec] * 3
            + weight_specs(parts, hidden, width, 1),
            out_specs=[whole(out_shape)] * 2
            + [pl.BlockSpec((3, 1, hidden, width), lambda s, *_: (0, s, 0, 0))] * (parts - 1)
            + [pl.BlockSpec((1, hidden, width), lambda s, *_: (s, 0, 0))] * 3,
            scratch_shapes=[pltpu.VMEM((count, width), F32)],
        ),
        out_shape=(jax.ShapeDtypeStruct(out_shape, BF),) * 2
        + (jax.ShapeDtypeStruct((3, slots, hidden, width), BF),) * (parts - 1)
        + (jax.ShapeDtypeStruct((slots, hidden, width), BF),) * 3,
        compiler_params=pltpu.CompilerParams(vmem_limit_bytes=VMEM_LIMIT),
        name="experts_second",
    )(place, rows_in, grads_in, sums, act, dgate, dup, *downs)


def shared_own(rows, grads, weights):
    parts = len(weights)

    def body(x_ref, dy_ref, *refs):
        out_ref, dx_ref = refs[parts:]
        for k in range(parts):
            gw, uw, dw = refs[k][0], refs[k][1], refs[k][2]
            act, dg, du = swish_parts(
                dot(x_ref[...], gw, 1, 1),
                dot(x_ref[...], uw, 1, 1),
                dot(dy_ref[...], dw, 1, 1),
            )
            out = dot(act.astype(BF), dw, 1, 0)
            dx = dot(dg.astype(BF), gw, 1, 0) + dot(du.astype(BF), uw, 1, 0)
            if k == 0:
                out_ref[...] = out
                dx_ref[...] = dx
            else:
                out_ref[...] += out
                dx_ref[...] += dx

    shape = jax.ShapeDtypeStruct(rows.shape, F32)
    return pl.pallas_call(
        body,
        out_shape=(shape, shape),
        compiler_params=pltpu.CompilerParams(vmem_limit_bytes=VMEM_LIMIT),
        name="shared_own",
    )(rows, grads, *weights)


def shared_grads(rows_in, grads_in, rows_cut, grads_cut, weights):
    parts = len(weights)
    hidden = weights[0].shape[1]
    cut = rows_cut.shape[1]

    def body(x_ref, dy_ref, xc_ref, dyc_ref, *refs):
        out_ref = refs[parts]
        for k in range(parts):
            act, dg, du = swish_parts(
                dot(x_ref[...], refs[k][0], 1, 1),
                dot(x_ref[...], refs[k][1], 1, 1),
                dot(dy_ref[...], refs[k][2], 1, 1),
            )
            out_ref[k, 0] = dot(dg.astype(BF), xc_ref[...], 0, 0).astype(BF)
            out_ref[k, 1] = dot(du.astype(BF), xc_ref[...], 0, 0).astype(BF)
            out_ref[k, 2] = dot(act.astype(BF), dyc_ref[...], 0, 0).astype(BF)

    return pl.pallas_call(
        body,
        out_shape=jax.ShapeDtypeStruct((parts, 3, hidden, cut), BF),
        compiler_params=pltpu.CompilerParams(vmem_limit_bytes=VMEM_LIMIT),
        name="shared_grads",
    )(rows_in, grads_in, rows_cut, grads_cut, *weights)


def store_chunks(place_ref, value, low_ref, high_ref):
    half, cut, _ = low_ref.shape
    for c in range(half):
        first = value[2 * c * cut : (2 * c + 1) * cut]
        second = value[(2 * c + 1) * cut : (2 * c + 2) * cut]
        at = place_ref[0] ^ c
        even = place_ref[1] == 0
        low_ref[at] = jnp.where(even, first, second).astype(BF)
        high_ref[at] = jnp.where(even, second, first).astype(BF)


def output_grads(place, attn_parts, att_parts, heads, hw, blocks):
    parts = len(attn_parts)
    own, width = attn_parts[0].shape
    span = heads * hw
    full = att_parts[0].shape[1]
    hd = full // heads

    def body(place_ref, *refs):
        low_ref, high_ref = refs[2 * parts :]
        attn = jnp.concatenate([r[...] for r in refs[:parts]], axis=0)
        att = jnp.concatenate([r[...] for r in refs[parts : 2 * parts]], axis=0)
        row = lax.broadcasted_iota(jnp.int32, (full, span), 0)
        col = lax.broadcasted_iota(jnp.int32, (full, span), 1)
        source = (col // hw) * hd + place_ref[2] * hw + col % hw
        pick = jnp.where(row == source, 1.0, 0.0).astype(BF)
        mine = dot(att, pick, 1, 0).astype(BF)
        store_chunks(place_ref, dot(attn, mine, 0, 0), low_ref, high_ref)

    shape = (blocks // 2, width // blocks, span)
    return pl.pallas_call(
        body,
        grid_spec=pltpu.PrefetchScalarGridSpec(
            num_scalar_prefetch=1,
            grid=(1,),
            in_specs=[whole((own, width))] * parts + [whole((own, full))] * parts,
            out_specs=[whole(shape)] * 2,
        ),
        out_shape=(jax.ShapeDtypeStruct(shape, BF),) * 2,
        compiler_params=pltpu.CompilerParams(vmem_limit_bytes=VMEM_LIMIT),
        name="output_grads",
    )(place, *attn_parts, *att_parts)


def project_back(place, back, cosine, sine, tokens, normed, wq, wk, wv, groups, blocks, quarters):
    heads = wq.shape[0]
    pw = wq.shape[2]
    hw = 2 * pw
    rows, width = normed.shape
    own = rows // quarters
    span = heads * hw

    def body(place_ref, back_ref, cos_ref, sin_ref, tok_ref, norm_ref, q_ref, k_ref, v_ref, *refs):
        dx_ref, gain_ref = refs[:2]
        chunk_refs = refs[2:-1]
        grad_ref = refs[-1]
        cos = cos_ref[...]
        sin = sin_ref[...]
        for h in range(heads):
            total = back_ref[h].astype(F32)
            for r in range(1, groups):
                total = total + back_ref[r * heads + h].astype(F32)
            for part in range(3):
                a = total[part * hw : part * hw + pw]
                b = total[part * hw + pw : (part + 1) * hw]
                if part < 2:
                    a, b = a * cos + b * sin, b * cos - a * sin
                at = part * span + h * hw
                grad_ref[at : at + hw] = jnp.concatenate([a, b], axis=0).astype(BF)
        for part in range(3):
            value = dot(norm_ref[...], grad_ref[part * span : (part + 1) * span], 0, 1)
            store_chunks(place_ref, value, chunk_refs[2 * part], chunk_refs[2 * part + 1])
        dx = dot(grad_ref[0:span], q_ref[...], 0, 0)
        dx = dx + dot(grad_ref[span : 2 * span], k_ref[...], 0, 0)
        dx = dx + dot(grad_ref[2 * span :], v_ref[...], 0, 0)
        for j in range(quarters):
            dx_ref[place_ref[2] ^ j] = dx[j * own : (j + 1) * own].astype(BF)
        x = tok_ref[...].astype(F32)
        gain_ref[...] = jnp.sum(dx * (x * rms_scale(x)), axis=0, keepdims=True)

    flat = (span, width)
    chunk = (blocks // 2, width // blocks, span)
    return pl.pallas_call(
        body,
        grid_spec=pltpu.PrefetchScalarGridSpec(
            num_scalar_prefetch=1,
            grid=(1,),
            in_specs=[
                whole(back.shape),
                whole(cosine.shape),
                whole(sine.shape),
                whole(tokens.shape),
                whole(normed.shape),
                whole(flat),
                whole(flat),
                whole(flat),
            ],
            out_specs=[whole((quarters, own, width)), whole((1, width))] + [whole(chunk)] * 6,
            scratch_shapes=[pltpu.VMEM((3 * span, rows), BF)],
        ),
        out_shape=(
            jax.ShapeDtypeStruct((quarters, own, width), BF),
            jax.ShapeDtypeStruct((1, width), F32),
        )
        + (jax.ShapeDtypeStruct(chunk, BF),) * 6,
        compiler_params=pltpu.CompilerParams(vmem_limit_bytes=VMEM_LIMIT),
        name="project_back",
    )(place, back, cosine, sine, tokens, normed, wq.reshape(flat), wk.reshape(flat), wv.reshape(flat))


def after(x, *others):
    return lax.optimization_barrier((x,) + others)[0]


def added(parts):
    total = parts[0].astype(F32)
    for p in parts[1:]:
        total = total + p.astype(F32)
    return total


def flip(x, by, axis):
    size = lax.axis_size(axis)
    return lax.ppermute(x, axis, [(i, i ^ by) for i in range(size)])


def exchange(x, axis):
    return lax.all_to_all(x, axis, 0, 0, tiled=True)


def spread(x, axis):
    size = lax.axis_size(axis)
    return exchange(jnp.broadcast_to(x[None], (size,) + x.shape), axis)


def even_blocks(x):
    size = lax.axis_size("expert")
    return [x] + [flip(x, m, "expert") for m in range(2, size, 2)]


def odd_blocks(evens):
    return flip(evens, 1, "expert")


def paired(evens, odds):
    return added([evens, flip(odds, 1, "expert")]).astype(BF)


def collected(sums):
    return added([sums[0]] + [flip(sums[j], 2 * j, "expert") for j in range(1, sums.shape[0])])


def of_quarters(x):
    quarters = lax.axis_size("tensor")
    return [x] + [flip(x, k, "tensor") for k in range(1, quarters)]


def in_order(place, parts):
    count = len(parts)
    rows, width = parts[0].shape

    def body(place_ref, *refs):
        for k in range(count):
            refs[count][place_ref[2] ^ k] = refs[k][...]

    return pl.pallas_call(
        body,
        grid_spec=pltpu.PrefetchScalarGridSpec(
            num_scalar_prefetch=1,
            grid=(1,),
            in_specs=[whole((rows, width))] * count,
            out_specs=whole((count, rows, width)),
        ),
        out_shape=jax.ShapeDtypeStruct((count, rows, width), parts[0].dtype),
        compiler_params=pltpu.CompilerParams(vmem_limit_bytes=VMEM_LIMIT),
        name="in_order",
    )(place, *parts).reshape(count * rows, width)


def on_device(
    tokens,
    segment_ids,
    expert_ids,
    gate_values,
    expert_slot,
    first_gain,
    second_gain,
    query_weight,
    key_weight,
    value_weight,
    output_weight,
    shared_gate,
    shared_up,
    shared_down,
    routed_gate,
    routed_up,
    routed_down,
    cotangent,
):
    rows, width = tokens.shape
    top = expert_ids.shape[1]
    experts_total = expert_slot.shape[0]
    slots_local = routed_gate.shape[0]
    blocks = lax.axis_size("expert")
    quarters = lax.axis_size("tensor")
    rank = lax.axis_index("expert")
    quarter = lax.axis_index("tensor")
    heads = query_weight.shape[0]
    pair_width = query_weight.shape[2]
    hw = 2 * pair_width
    hd = quarters * hw
    units = blocks * quarters
    groups = units // heads
    own = rows // quarters
    cut = width // blocks
    starts = query_groups(blocks, groups)
    most = max(starts[i + 1] - starts[i] for i in range(groups))
    unit_group = [min(j // heads, groups) for j in range(units)]
    unit = rank * quarters + quarter
    low_table = jnp.array([starts[g] for g in unit_group], jnp.int32)
    high_table = jnp.array([starts[g + 1] if g < groups else starts[g] for g in unit_group], jnp.int32)
    bounds = jnp.stack([low_table[unit], high_table[unit]])
    block_group = jnp.array(
        [max(g for g in range(groups) if starts[g] <= b) for b in range(blocks)], jnp.int32
    )[rank]

    seg_mine = lax.dynamic_slice_in_dim(segment_ids, rank * rows, rows)
    doc_start = jnp.sum((segment_ids[:, None] < seg_mine[None, :]).astype(jnp.int32), axis=0)
    positions = rank * rows + jnp.arange(rows, dtype=jnp.int32) - doc_start
    freq_index = quarter * pair_width + jnp.arange(pair_width, dtype=jnp.int32)
    inverse_freq = 10000.0 ** (-2.0 * freq_index.astype(F32) / HD)
    angles = inverse_freq[:, None] * positions.astype(F32)[None, :]
    cosine = jnp.cos(angles)
    sine = jnp.sin(angles)
    seg_row = segment_ids.reshape(blocks, 1, rows)
    seg_col = jnp.broadcast_to(segment_ids.reshape(blocks, rows, 1), (blocks, rows, 128))

    normed_one, send = project(
        tokens, first_gain, query_weight, key_weight, value_weight, cosine, sine, units, groups
    )
    arrived = exchange(send, BOTH).reshape(blocks, quarters, 3 * hw, rows)

    def across(x):
        return flip(x, 2, "tensor")

    def beside(x):
        return flip(x, 1, "tensor")

    def all_quarters(x, far):
        return (x, beside(x), far, beside(far))

    out_mine = after(output_weight.reshape(heads, hw, width), normed_one)
    out_far = across(out_mine)
    gate_mine = after(routed_gate, out_far)
    gate_far = across(gate_mine)
    arrived = after(arrived, out_far)
    up_mine = after(routed_up, arrived)
    up_far = across(up_mine)
    out_ws = all_quarters(out_mine, out_far)
    out_full = jnp.zeros((heads, quarters, hw, width), BF)
    for k in range(quarters):
        out_full = lax.dynamic_update_slice(out_full, out_ws[k][:, None], (0, quarter ^ k, 0, 0))
    out_full = out_full.reshape(heads * hd, width)

    half = blocks // 2
    place = jnp.stack([rank // 2, rank % 2, quarter, rank])
    own_tokens = lax.dynamic_slice_in_dim(tokens, quarter * own, own).astype(F32)
    own_grads = lax.dynamic_slice_in_dim(cotangent, quarter * own, own)
    own_ids = lax.dynamic_slice_in_dim(expert_ids, quarter * own, own)
    own_gates = lax.dynamic_slice_in_dim(gate_values, quarter * own, own)
    onehot = own_ids[:, :, None] == jnp.arange(experts_total, dtype=jnp.int32)
    own_slots = jnp.sum(jnp.where(onehot, expert_slot[None, None, :], 0), axis=2)
    slot_hot = own_slots[:, :, None] == jnp.arange(experts_total, dtype=jnp.int32)
    dense_gates = jnp.sum(jnp.where(slot_hot, own_gates[:, :, None], 0.0), axis=1)
    lanes = -(-3 * experts_total // 128) * 128
    spare = jnp.zeros((own, lanes - 3 * experts_total), BF)
    own_wide = jnp.concatenate(
        [own_grads] + [p.astype(BF) for p in pieces(dense_gates)] + [spare], axis=1
    )
    grads_even = even_blocks(after(own_wide, arrived))

    attended_units, lse = attend(bounds, arrived, seg_col, seg_row, most)
    attended_units, grads_even = lax.optimization_barrier((attended_units, tuple(grads_even)))
    grads_even = jnp.stack(grads_even)
    grads_odd = odd_blocks(grads_even)
    down_mine = after(routed_down, attended_units)
    down_far = across(down_mine)
    gate_ws = all_quarters(gate_mine, gate_far)
    up_ws = all_quarters(up_mine, up_far)
    down_ws = all_quarters(down_mine, down_far)
    back = exchange(attended_units.reshape(units, own, hd), BOTH)
    back, grads_odd = lax.optimization_barrier((back, grads_odd, out_full, gate_far))[:2]
    attended_heads = lax.dynamic_slice_in_dim(back, block_group * heads, heads)
    attended = attended_heads.transpose(1, 0, 2).reshape(own, heads * hd)
    hidden_state = own_tokens + jnp.dot(attended, out_full, preferred_element_type=F32)
    second_scale = rms_scale(hidden_state)
    normed_two = (hidden_state * second_scale * second_gain).astype(BF)

    rows_in = spread(normed_two, "expert").reshape(blocks * own, width)
    shared_mine = after(jnp.stack([shared_gate, shared_up, shared_down]), normed_two)
    shared_far = across(shared_mine)
    shared_near = beside(shared_mine)
    shared_ws = (shared_mine, shared_near, shared_far, beside(shared_far))

    total_rows = blocks * own
    step = min(total_rows, 512)
    spans = [slice(c, c + step) for c in range(0, total_rows, step)]
    prods = [
        down_products(place, grads_even, grads_odd, c.start // own // 2, step, width, down_ws)
        for c in spans
    ]
    firsts = [
        experts_first(place, rows_in[c], p[0], p[2], gate_ws, up_ws, experts_total)
        for c, p in zip(spans, prods)
    ]
    grads_in = jnp.concatenate([p[1] for p in prods], axis=0)
    grad_rows = jnp.concatenate([f[4] for f in firsts], axis=0)
    grad_home = exchange(grad_rows.reshape(blocks, own, width), "expert")

    seconds = []
    for c, f in zip(spans, firsts):
        act = lax.optimization_barrier((f[0], shared_far, shared_near))[0]
        seconds.append(
            experts_second(place, rows_in[c], grads_in[c], f[3], act, f[1], f[2], down_ws, own)
        )
    if len(seconds) == 1:
        out_low, out_high = seconds[0][:2]
        parts = seconds[0][2:]
    else:
        order = (rank // (step // own)) ^ jnp.arange(len(seconds), dtype=jnp.int32)
        out_low, out_high = (
            jnp.stack([s[i] for s in seconds])[order].reshape(half, own, width + lanes)
            for i in range(2)
        )
        parts = [added([s[2 + k] for s in seconds]).astype(BF) for k in range(quarters + 2)]
    shared_out, shared_dx = shared_own(after(normed_two, out_low), own_grads, shared_ws)
    att_parts = of_quarters(after(attended, shared_far))

    to_far = [added([parts[2][0], beside(parts[3])]).astype(BF)]
    grad_home, to_far[0], att_parts = lax.optimization_barrier(
        (grad_home, to_far[0], tuple(att_parts), shared_dx)
    )[:3]
    grad_norm_two = jnp.sum(grad_home.astype(F32), axis=0) + shared_dx
    grad_full = own_grads.astype(F32)
    grad_second, second_gain_local = norm_backward(
        grad_norm_two, hidden_state, second_scale, second_gain
    )
    grad_hidden = grad_full + grad_second
    grad_attn = grad_hidden.astype(BF)
    grad_attended = jnp.einsum(
        "td,hcd->htc", grad_attn, out_full.reshape(heads, hd, width), preferred_element_type=F32
    ).astype(BF)
    out_got = flip(out_high, 1, "expert")
    grad_attended, out_got = lax.optimization_barrier((grad_attended, out_got))
    do_send = jnp.concatenate([grad_attended] * groups + [grad_attended[: units - groups * heads]], axis=0)
    do_units = exchange(do_send, BOTH).reshape(blocks, rows, hd)

    grad_attn_sent = after(grad_attn, do_send)
    attn_parts = of_quarters(grad_attn_sent)
    from_near = beside(after(parts[4], do_send))
    proj_low, proj_high = output_grads(
        place, attn_parts, att_parts, heads, hw, blocks
    )
    out_pairs = added([out_low, after(out_got, proj_low)]).astype(BF)
    routed_far = [across(lax.optimization_barrier((to_far[0], tuple(attn_parts)))[0])]
    to_far.append(added([parts[2][1], after(from_near, proj_low)]).astype(BF))
    do_units, out_pairs, to_far[1] = lax.optimization_barrier(
        (do_units, out_pairs, to_far[1], proj_low)
    )[:3]

    grad_units = attend_back(bounds, arrived, seg_col, seg_row, lse, do_units, most)
    out_home = collected(out_pairs)
    proj_pairs = paired(proj_low, proj_high)
    grad_units, routed_far[0] = lax.optimization_barrier(
        (grad_units, routed_far[0], out_home, proj_pairs)
    )[:2]
    far_one = across(after(to_far[1], routed_far[0]))
    back_grads = exchange(grad_units.reshape(units, 3 * hw, rows), BOTH)

    to_far.append(added([parts[2][2], beside(after(parts[5], grad_units))]).astype(BF))
    rows_late, grads_late = lax.optimization_barrier((rows_in, grads_in, grad_units))[:2]
    rows_cut = lax.dynamic_slice_in_dim(rows_late, rank * cut, cut, axis=1)
    grads_cut = lax.dynamic_slice_in_dim(grads_late, rank * cut, cut, axis=1)
    shared_parts = [
        shared_grads(rows_late[c], grads_late[c], rows_cut[c], grads_cut[c], shared_ws) for c in spans
    ]
    shared_parts = shared_parts[0] if len(spans) == 1 else added(shared_parts).astype(BF)
    shared_sent, far_one = lax.optimization_barrier((shared_parts, far_one))
    shared_gots = [flip(shared_sent[k], k, "tensor") for k in range(1, quarters)]
    near = beside(after(parts[1], grad_units))
    out_grad = collected(after(proj_pairs, grad_units))
    moe_out = out_home[:, :width] + shared_out
    slot_sums = out_home[:, width : width + 3 * experts_total].reshape(own, 3, experts_total)
    slot_sums = jnp.sum(slot_sums, axis=1)
    gate_grad = jnp.sum(jnp.where(slot_hot, slot_sums[:, None, :], 0.0), axis=2)
    final = [(hidden_state + moe_out).astype(BF)] + [p.astype(BF) for p in pieces(gate_grad)]
    final = jnp.concatenate(final + [jnp.zeros((own, 128 - 3 * top), BF)], axis=1)
    final = in_order(place, of_quarters(after(final, grad_units)))
    output = final[:, :width]
    gate_grad = jnp.sum(final[:, width : width + 3 * top].reshape(rows, 3, top).astype(F32), axis=1)
    back_grads, near = lax.optimization_barrier((back_grads, near, shared_parts, out_grad, output))[:2]

    back_out = project_back(
        place,
        back_grads,
        cosine,
        sine,
        tokens,
        normed_one,
        query_weight,
        key_weight,
        value_weight,
        groups,
        blocks,
        quarters,
    )
    gains = jnp.stack([back_out[1][0], second_gain_local]).reshape(2, blocks, cut).transpose(1, 0, 2)
    gains = jnp.broadcast_to(gains[:, None], (blocks, quarters, 2, cut)).reshape(units, 2, cut)
    gains = exchange(gains, BOTH)
    dx_parts = [back_out[0][0]] + [flip(back_out[0][k], k, "tensor") for k in range(1, quarters)]
    pair_q = paired(back_out[2], back_out[3])
    pair_k = paired(back_out[4], after(back_out[5], pair_q))
    dx_parts, pair_q = lax.optimization_barrier((tuple(dx_parts), pair_q))
    grad_one = added(dx_parts)
    far_two = across(after(to_far[2], dx_parts[1]))
    routed = [added([parts[0][0], near[0], after(routed_far[0], pair_q)])]
    shared_gots = lax.optimization_barrier((tuple(shared_gots), pair_k))[0]
    shared = added([shared_parts[0], *shared_gots])
    pair_v = paired(back_out[6], after(back_out[7], pair_k))
    routed.append(added([parts[0][1], near[1], after(far_one, pair_k)]))
    pair_v, routed, shared = lax.optimization_barrier((pair_v, routed, shared))
    routed.append(added([parts[0][2], near[2], after(far_two, pair_v)]))
    qkv_grads = [collected(p) for p in (pair_q, pair_k, pair_v)]
    first_scale = rms_scale(own_tokens)
    grad_first, _ = norm_backward(grad_one, own_tokens, first_scale, first_gain)
    input_mine = after((grad_hidden + grad_first).astype(BF), pair_k)
    input_parts, routed[2] = lax.optimization_barrier((tuple(of_quarters(input_mine)), routed[2]))
    input_grad = in_order(place, input_parts)
    gains = jnp.sum(after(gains, pair_v), axis=0)

    weight_shape = (heads, 2, pair_width, cut)
    return (
        output,
        input_grad,
        gate_grad,
        gains[0],
        gains[1],
        qkv_grads[0].T.reshape(weight_shape),
        qkv_grads[1].T.reshape(weight_shape),
        qkv_grads[2].T.reshape(weight_shape),
        out_grad.T.reshape(weight_shape),
        shared[0],
        shared[1],
        shared[2],
        routed[0],
        routed[1],
        routed[2],
    )


def solution(mesh):
    placed = (
        P("expert", None),
        P(),
        P("expert", None),
        P("expert", None),
        P(),
        P(),
        P(),
        P(None, None, "tensor", None),
        P(None, None, "tensor", None),
        P(None, None, "tensor", None),
        P(None, None, "tensor", None),
        P("tensor", None),
        P("tensor", None),
        P("tensor", None),
        P("expert", "tensor", None),
        P("expert", "tensor", None),
        P("expert", "tensor", None),
        P("expert", None),
    )
    return jax.shard_map(
        on_device,
        mesh=mesh,
        in_specs=placed,
        out_specs=(
            P("expert", None),
            P("expert", None),
            P("expert", None),
            P("expert"),
            P("expert"),
            P(None, None, "tensor", "expert"),
            P(None, None, "tensor", "expert"),
            P(None, None, "tensor", "expert"),
            P(None, None, "tensor", "expert"),
            P("tensor", "expert"),
            P("tensor", "expert"),
            P("tensor", "expert"),
            P("expert", "tensor", None),
            P("expert", "tensor", None),
            P("expert", "tensor", None),
        ),
        check_vma=False,
    )
```

```python
import jax
import jax.numpy as jnp
from jax import lax
from jax.experimental import pallas as pl
from jax.experimental.pallas import tpu as pltpu
from jax.sharding import PartitionSpec as P

HD = 128
REACH = 4
EPSILON = 1e-06
MASKED = -1e30
BF = jnp.bfloat16
F32 = jnp.float32
BOTH = ("expert", "tensor")
VMEM_LIMIT = 60 * 1024 * 1024


def dot(a, b, ca, cb):
    return lax.dot_general(a, b, (((ca,), (cb,)), ((), ())), preferred_element_type=F32)


def whole(shape):
    zeros = (0,) * len(shape)
    return pl.BlockSpec(shape, lambda *_: zeros)


def query_groups(blocks, groups):
    cost = [min(b, REACH) + 1 for b in range(blocks)]
    most = max(cost)
    while True:
        starts, load = [0], 0
        for b in range(blocks):
            if load + cost[b] > most:
                starts.append(b)
                load = 0
            load += cost[b]
        if len(starts) <= groups:
            break
        most += 1
    return starts + [blocks] * (groups + 2 - len(starts))


def rms_scale(values):
    return lax.rsqrt(jnp.mean(values * values, axis=-1, keepdims=True) + EPSILON)


def norm_backward(grad_out, values, inverse_rms, gain_vector):
    weighted = grad_out * gain_vector
    normal = values * inverse_rms
    gain_grad = jnp.sum(grad_out * normal, axis=0)
    grad_in = inverse_rms * (
        weighted - normal * jnp.mean(normal * weighted, axis=-1, keepdims=True)
    )
    return grad_in, gain_grad


def project(tokens, gain, wq, wk, wv, cosine, sine, units, groups):
    rows, width = tokens.shape
    heads = wq.shape[0]
    hw = wq.shape[1] * wq.shape[2]
    pw = wq.shape[2]

    def body(tok, gain_ref, q_ref, k_ref, v_ref, cos_ref, sin_ref, norm_ref, send_ref):
        x = tok[...].astype(F32)
        normed = (x * rms_scale(x) * gain_ref[...]).astype(BF)
        norm_ref[...] = normed
        cos = cos_ref[...]
        sin = sin_ref[...]
        for part, w_ref in enumerate((q_ref, k_ref, v_ref)):
            pre = dot(w_ref[...], normed, 1, 1)
            for h in range(heads):
                a = pre[h * hw : h * hw + pw]
                b = pre[h * hw + pw : (h + 1) * hw]
                if part < 2:
                    a, b = a * cos - b * sin, b * cos + a * sin
                chunk = jnp.concatenate([a, b], axis=0).astype(BF)
                for unit in range(h, units, heads):
                    send_ref[unit, part * hw : (part + 1) * hw] = chunk

    flat = (heads * hw, width)
    return pl.pallas_call(
        body,
        out_shape=(
            jax.ShapeDtypeStruct((rows, width), BF),
            jax.ShapeDtypeStruct((units, 3 * hw, rows), BF),
        ),
        compiler_params=pltpu.CompilerParams(vmem_limit_bytes=VMEM_LIMIT),
        name="project",
    )(tokens, gain[None], wq.reshape(flat), wk.reshape(flat), wv.reshape(flat), cosine, sine)


def allowed_pairs(seg_col, seg_row, query_block, key_block, rows):
    wide = jnp.concatenate([seg_col] * (rows // seg_col.shape[1]), axis=1)
    same = wide == seg_row
    ahead = lax.broadcasted_iota(jnp.int32, (rows, rows), 0) - lax.broadcasted_iota(
        jnp.int32, (rows, rows), 1
    )
    return same & (ahead + (query_block - key_block) * rows >= 0)


def attend(bounds, arrived, seg_col, seg_row, most):
    blocks, quarters, chunk, rows = arrived.shape
    hw = chunk // 3
    hd = quarters * hw
    scale = HD ** (-0.5)

    def part(ref, block, which):
        return ref[block, :, which * hw : (which + 1) * hw, :].reshape(hd, rows)

    def body(bounds_ref, arr_ref, col_ref, row_ref, out_ref, lse_ref, score_ref):
        query_block = bounds_ref[0] + pl.program_id(0)

        @pl.when(query_block < bounds_ref[1])
        def _():
            query = part(arr_ref, query_block, 0)
            col = col_ref[query_block]
            low = jnp.maximum(query_block - REACH, 0)

            def first(kb, best):
                s = dot(query, part(arr_ref, kb, 1), 0, 0) * scale
                s = jnp.where(allowed_pairs(col, row_ref[kb], query_block, kb, rows), s, MASKED)
                score_ref[kb - low] = s
                return jnp.maximum(best, jnp.max(s, axis=1, keepdims=True))

            best = lax.fori_loop(low, query_block + 1, first, jnp.full((rows, 1), MASKED, F32))

            def second(kb, carry):
                total, out = carry
                p = jnp.exp(score_ref[kb - low] - best)
                total = total + jnp.sum(p, axis=1, keepdims=True)
                return total, out + dot(p.astype(BF), part(arr_ref, kb, 2), 1, 1)

            total, out = lax.fori_loop(
                low, query_block + 1, second, (jnp.zeros((rows, 1), F32), jnp.zeros((rows, hd), F32))
            )
            out_ref[query_block] = (out / total).astype(BF)
            lse_ref[query_block] = jnp.broadcast_to(best + jnp.log(total), (rows, 128))

    grid_spec = pltpu.PrefetchScalarGridSpec(
        num_scalar_prefetch=1,
        grid=(most,),
        in_specs=[whole(arrived.shape), whole(seg_col.shape), whole(seg_row.shape)],
        out_specs=[whole((blocks, rows, hd)), whole((blocks, rows, 128))],
        scratch_shapes=[pltpu.VMEM((REACH + 1, rows, rows), F32)],
    )
    return pl.pallas_call(
        body,
        grid_spec=grid_spec,
        out_shape=(
            jax.ShapeDtypeStruct((blocks, rows, hd), BF),
            jax.ShapeDtypeStruct((blocks, rows, 128), F32),
        ),
        compiler_params=pltpu.CompilerParams(vmem_limit_bytes=VMEM_LIMIT),
        name="attend",
    )(bounds, arrived, seg_col, seg_row)


def attend_back(bounds, arrived, seg_col, seg_row, lse, grad_out, most):
    blocks, quarters, chunk, rows = arrived.shape
    hw = chunk // 3
    hd = quarters * hw
    scale = HD ** (-0.5)

    def part(ref, block, which):
        return ref[block, :, which * hw : (which + 1) * hw, :].reshape(hd, rows)

    def body(bounds_ref, arr_ref, col_ref, row_ref, lse_ref, do_ref, res_ref, prob_ref, dp_ref, dk_ref, dv_ref):
        step = pl.program_id(0)
        query_block = bounds_ref[0] + step

        @pl.when(step == 0)
        def _():
            res_ref[...] = jnp.zeros(res_ref.shape, BF)
            dk_ref[...] = jnp.zeros(dk_ref.shape, F32)
            dv_ref[...] = jnp.zeros(dv_ref.shape, F32)

        @pl.when(query_block < bounds_ref[1])
        def _():
            query = part(arr_ref, query_block, 0)
            col = col_ref[query_block]
            lse_now = jnp.concatenate([lse_ref[query_block]] * (rows // 128), axis=1)
            do = do_ref[query_block]
            low = jnp.maximum(query_block - REACH, 0)

            def first(kb, inner):
                s = dot(query, part(arr_ref, kb, 1), 0, 0) * scale
                ok = allowed_pairs(col, row_ref[kb], query_block, kb, rows)
                p = jnp.where(ok, jnp.exp(jnp.where(ok, s - lse_now, 0.0)), 0.0)
                dp = dot(do, part(arr_ref, kb, 2), 1, 0)
                prob_ref[kb - low] = p
                dp_ref[kb - low] = dp
                dv_ref[kb] += dot(do, p.astype(BF), 0, 0)
                return inner + jnp.sum(p * dp, axis=1, keepdims=True)

            inner = lax.fori_loop(low, query_block + 1, first, jnp.zeros((rows, 1), F32))

            def second(kb, dq):
                ds = (prob_ref[kb - low] * (dp_ref[kb - low] - inner)).astype(BF)
                dk_ref[kb] += dot(query, ds, 1, 0)
                return dq + dot(part(arr_ref, kb, 1), ds, 1, 1)

            dq = lax.fori_loop(low, query_block + 1, second, jnp.zeros((hd, rows), F32))
            res_ref[query_block, :, 0:hw, :] = (dq * scale).astype(BF).reshape(quarters, hw, rows)

        @pl.when(step == pl.num_programs(0) - 1)
        def _():
            for b in range(blocks):
                res_ref[b, :, hw : 2 * hw, :] = (dk_ref[b] * scale).astype(BF).reshape(quarters, hw, rows)
                res_ref[b, :, 2 * hw : 3 * hw, :] = dv_ref[b].astype(BF).reshape(quarters, hw, rows)

    grid_spec = pltpu.PrefetchScalarGridSpec(
        num_scalar_prefetch=1,
        grid=(most,),
        in_specs=[
            whole(arrived.shape),
            whole(seg_col.shape),
            whole(seg_row.shape),
            whole(lse.shape),
            whole(grad_out.shape),
        ],
        out_specs=whole(arrived.shape),
        scratch_shapes=[
            pltpu.VMEM((REACH + 1, rows, rows), F32),
            pltpu.VMEM((REACH + 1, rows, rows), F32),
            pltpu.VMEM((blocks, hd, rows), F32),
            pltpu.VMEM((blocks, hd, rows), F32),
        ],
    )
    return pl.pallas_call(
        body,
        grid_spec=grid_spec,
        out_shape=jax.ShapeDtypeStruct(arrived.shape, BF),
        compiler_params=pltpu.CompilerParams(vmem_limit_bytes=VMEM_LIMIT),
        name="attend_back",
    )(bounds, arrived, seg_col, seg_row, lse, grad_out)


def weight_specs(parts, hidden, width, mats):
    return [pl.BlockSpec((1, hidden, width), lambda s, *_: (s, 0, 0))] * (parts * mats)


def down_products(place, even, odd, first, count, width, downs):
    half, own, wide = even.shape
    parts = len(downs)
    slots, hidden, _ = downs[0].shape
    lanes = wide - width

    def body(place_ref, even_ref, odd_ref, *refs):
        da_ref, dy_ref, gate_ref = refs[parts:]

        @pl.when(pl.program_id(0) == 0)
        def _():
            for c in range(count // own // 2):
                at = place_ref[0] ^ (first + c)
                for parity in range(2):

                    @pl.when(place_ref[1] == parity)
                    def _():
                        for b, ref in ((2 * c + parity, even_ref), (2 * c + 1 - parity, odd_ref)):
                            dy_ref[b * own : (b + 1) * own] = ref[at, :, 0:width]
                            gate_ref[b * own : (b + 1) * own] = ref[at, :, width:wide]

        for k in range(parts):
            da_ref[0, k] = dot(dy_ref[...], refs[k][0], 1, 1)

    return pl.pallas_call(
        body,
        grid_spec=pltpu.PrefetchScalarGridSpec(
            num_scalar_prefetch=1,
            grid=(slots,),
            in_specs=[whole(even.shape), whole(odd.shape)] + weight_specs(parts, hidden, width, 1),
            out_specs=[
                pl.BlockSpec((1, parts, count, hidden), lambda s, *_: (s, 0, 0, 0)),
                whole((count, width)),
                whole((count, lanes)),
            ],
        ),
        out_shape=(
            jax.ShapeDtypeStruct((slots, parts, count, hidden), F32),
            jax.ShapeDtypeStruct((count, width), BF),
            jax.ShapeDtypeStruct((count, lanes), BF),
        ),
        compiler_params=pltpu.CompilerParams(vmem_limit_bytes=VMEM_LIMIT),
        name="down_products",
    )(place, even, odd, *downs)


def pieces(x):
    high = lax.reduce_precision(x, 8, 7)
    middle = lax.reduce_precision(x - high, 8, 7)
    return [high, middle, x - high - middle]


def swish_parts(g, u, da):
    sig = jax.nn.sigmoid(g)
    swish = g * sig
    return swish * u, da * u * (sig * (1.0 + g * (1.0 - sig))), da * swish


def experts_first(place, rows_in, down_prod, gates, gate_ws, up_ws, experts):
    count, width = rows_in.shape
    parts = len(gate_ws)
    slots, hidden, _ = gate_ws[0].shape
    lanes = gates.shape[1]

    def body(place_ref, x_ref, da_ref, gate_ref, *refs):
        gate_w, up_w = refs[:parts], refs[parts : 2 * parts]
        act_ref, dg_ref, du_ref, gg_ref, dx_ref, acc_ref, sum_ref = refs[2 * parts :]
        s = pl.program_id(0)
        x = x_ref[...]
        lane = lax.broadcasted_iota(jnp.int32, (count, lanes), 1)
        slot = place_ref[3] * slots + s
        mine = lane % experts == slot
        gate = jnp.sum(jnp.where(mine, gate_ref[...].astype(F32), 0.0), axis=1, keepdims=True)
        total = jnp.zeros((count, 1), F32)

        @pl.when(s == 0)
        def _():
            acc_ref[...] = jnp.zeros(acc_ref.shape, F32)
            sum_ref[...] = jnp.zeros(sum_ref.shape, F32)

        for k in range(parts):
            g = dot(x, gate_w[k][0], 1, 1)
            u = dot(x, up_w[k][0], 1, 1)
            da = da_ref[0, k]
            act, dg, du = swish_parts(g, u, da * gate)
            total = total + jnp.sum(act * da, axis=1, keepdims=True)
            act_ref[0, k] = (act * gate).astype(BF)
            dg_ref[0, k] = dg.astype(BF)
            du_ref[0, k] = du.astype(BF)
            acc_ref[...] += dot(dg_ref[0, k], gate_w[k][0], 1, 0) + dot(du_ref[0, k], up_w[k][0], 1, 0)

        high = total.astype(BF).astype(F32)
        middle = (total - high).astype(BF).astype(F32)
        for n, piece in enumerate((high, middle, total - high - middle)):
            sum_ref[...] += jnp.where(lane == n * experts + slot, piece, 0.0)

        @pl.when(s == slots - 1)
        def _():
            dx_ref[...] = acc_ref[...].astype(BF)
            gg_ref[...] = sum_ref[...].astype(BF)

    hid = jax.ShapeDtypeStruct((slots, parts, count, hidden), BF)
    hid_spec = pl.BlockSpec((1, parts, count, hidden), lambda s, *_: (s, 0, 0, 0))
    return pl.pallas_call(
        body,
        grid_spec=pltpu.PrefetchScalarGridSpec(
            num_scalar_prefetch=1,
            grid=(slots,),
            in_specs=[whole(rows_in.shape), hid_spec, whole(gates.shape)]
            + weight_specs(parts, hidden, width, 2),
            out_specs=[hid_spec, hid_spec, hid_spec, whole((count, lanes)), whole((count, width))],
            scratch_shapes=[pltpu.VMEM((count, width), F32), pltpu.VMEM((count, lanes), F32)],
        ),
        out_shape=(
            hid,
            hid,
            hid,
            jax.ShapeDtypeStruct((count, lanes), BF),
            jax.ShapeDtypeStruct((count, width), BF),
        ),
        compiler_params=pltpu.CompilerParams(vmem_limit_bytes=VMEM_LIMIT),
        name="experts_first",
    )(place, rows_in, down_prod, gates, *gate_ws, *up_ws)


def experts_second(place, rows_in, grads_in, sums, act, dgate, dup, downs, own):
    count, width = rows_in.shape
    parts = len(downs)
    slots, hidden, _ = downs[0].shape
    wide = width + sums.shape[1]
    half = count // own // 2

    def body(place_ref, x_ref, dy_ref, sum_ref, act_ref, dg_ref, du_ref, *refs):
        down_w = refs[:parts]
        low_ref, high_ref = refs[parts : parts + 2]
        grads = refs[parts + 2 : -1]
        acc_ref = refs[-1]
        s = pl.program_id(0)

        @pl.when(s == 0)
        def _():
            acc_ref[...] = jnp.zeros(acc_ref.shape, F32)

        for k in range(parts):
            acc_ref[...] += dot(act_ref[0, k], down_w[k][0], 1, 0)
            for m, (left, right) in enumerate(((dg_ref, x_ref), (du_ref, x_ref), (act_ref, dy_ref))):
                grad = dot(left[0, k], right[...], 0, 0).astype(BF)
                if k < parts - 1:
                    grads[k][m, 0] = grad
                else:
                    grads[k + m][0] = grad

        @pl.when(s == slots - 1)
        def _():
            for c in range(half):
                at = (place_ref[0] % half) ^ c
                for parity in range(2):

                    @pl.when(place_ref[1] == parity)
                    def _():
                        for b, ref in ((2 * c + parity, low_ref), (2 * c + 1 - parity, high_ref)):
                            ref[at, :, 0:width] = acc_ref[b * own : (b + 1) * own].astype(BF)
                            ref[at, :, width:wide] = sum_ref[b * own : (b + 1) * own]

    hid_spec = pl.BlockSpec((1, parts, count, hidden), lambda s, *_: (s, 0, 0, 0))
    out_shape = (half, own, wide)
    return pl.pallas_call(
        body,
        grid_spec=pltpu.PrefetchScalarGridSpec(
            num_scalar_prefetch=1,
            grid=(slots,),
            in_specs=[whole(rows_in.shape), whole(grads_in.shape), whole(sums.shape)]
            + [hid_spec] * 3
            + weight_specs(parts, hidden, width, 1),
            out_specs=[whole(out_shape)] * 2
            + [pl.BlockSpec((3, 1, hidden, width), lambda s, *_: (0, s, 0, 0))] * (parts - 1)
            + [pl.BlockSpec((1, hidden, width), lambda s, *_: (s, 0, 0))] * 3,
            scratch_shapes=[pltpu.VMEM((count, width), F32)],
        ),
        out_shape=(jax.ShapeDtypeStruct(out_shape, BF),) * 2
        + (jax.ShapeDtypeStruct((3, slots, hidden, width), BF),) * (parts - 1)
        + (jax.ShapeDtypeStruct((slots, hidden, width), BF),) * 3,
        compiler_params=pltpu.CompilerParams(vmem_limit_bytes=VMEM_LIMIT),
        name="experts_second",
    )(place, rows_in, grads_in, sums, act, dgate, dup, *downs)


def shared_own(rows, grads, weights):
    parts = len(weights)

    def body(x_ref, dy_ref, *refs):
        out_ref, dx_ref = refs[parts:]
        for k in range(parts):
            gw, uw, dw = refs[k][0], refs[k][1], refs[k][2]
            act, dg, du = swish_parts(
                dot(x_ref[...], gw, 1, 1),
                dot(x_ref[...], uw, 1, 1),
                dot(dy_ref[...], dw, 1, 1),
            )
            out = dot(act.astype(BF), dw, 1, 0)
            dx = dot(dg.astype(BF), gw, 1, 0) + dot(du.astype(BF), uw, 1, 0)
            if k == 0:
                out_ref[...] = out
                dx_ref[...] = dx
            else:
                out_ref[...] += out
                dx_ref[...] += dx

    shape = jax.ShapeDtypeStruct(rows.shape, F32)
    return pl.pallas_call(
        body,
        out_shape=(shape, shape),
        compiler_params=pltpu.CompilerParams(vmem_limit_bytes=VMEM_LIMIT),
        name="shared_own",
    )(rows, grads, *weights)


def shared_grads(rows_in, grads_in, rows_cut, grads_cut, weights):
    parts = len(weights)
    hidden = weights[0].shape[1]
    cut = rows_cut.shape[1]

    def body(x_ref, dy_ref, xc_ref, dyc_ref, *refs):
        out_ref = refs[parts]
        for k in range(parts):
            act, dg, du = swish_parts(
                dot(x_ref[...], refs[k][0], 1, 1),
                dot(x_ref[...], refs[k][1], 1, 1),
                dot(dy_ref[...], refs[k][2], 1, 1),
            )
            out_ref[k, 0] = dot(dg.astype(BF), xc_ref[...], 0, 0).astype(BF)
            out_ref[k, 1] = dot(du.astype(BF), xc_ref[...], 0, 0).astype(BF)
            out_ref[k, 2] = dot(act.astype(BF), dyc_ref[...], 0, 0).astype(BF)

    return pl.pallas_call(
        body,
        out_shape=jax.ShapeDtypeStruct((parts, 3, hidden, cut), BF),
        compiler_params=pltpu.CompilerParams(vmem_limit_bytes=VMEM_LIMIT),
        name="shared_grads",
    )(rows_in, grads_in, rows_cut, grads_cut, *weights)


def store_chunks(place_ref, value, low_ref, high_ref):
    half, cut, _ = low_ref.shape
    for c in range(half):
        first = value[2 * c * cut : (2 * c + 1) * cut]
        second = value[(2 * c + 1) * cut : (2 * c + 2) * cut]
        at = place_ref[0] ^ c
        even = place_ref[1] == 0
        low_ref[at] = jnp.where(even, first, second).astype(BF)
        high_ref[at] = jnp.where(even, second, first).astype(BF)


def output_grads(place, attn_parts, att_parts, heads, hw, blocks):
    parts = len(attn_parts)
    own, width = attn_parts[0].shape
    span = heads * hw
    full = att_parts[0].shape[1]
    hd = full // heads

    def body(place_ref, *refs):
        low_ref, high_ref = refs[2 * parts :]
        attn = jnp.concatenate([r[...] for r in refs[:parts]], axis=0)
        att = jnp.concatenate([r[...] for r in refs[parts : 2 * parts]], axis=0)
        row = lax.broadcasted_iota(jnp.int32, (full, span), 0)
        col = lax.broadcasted_iota(jnp.int32, (full, span), 1)
        source = (col // hw) * hd + place_ref[2] * hw + col % hw
        pick = jnp.where(row == source, 1.0, 0.0).astype(BF)
        mine = dot(att, pick, 1, 0).astype(BF)
        store_chunks(place_ref, dot(attn, mine, 0, 0), low_ref, high_ref)

    shape = (blocks // 2, width // blocks, span)
    return pl.pallas_call(
        body,
        grid_spec=pltpu.PrefetchScalarGridSpec(
            num_scalar_prefetch=1,
            grid=(1,),
            in_specs=[whole((own, width))] * parts + [whole((own, full))] * parts,
            out_specs=[whole(shape)] * 2,
        ),
        out_shape=(jax.ShapeDtypeStruct(shape, BF),) * 2,
        compiler_params=pltpu.CompilerParams(vmem_limit_bytes=VMEM_LIMIT),
        name="output_grads",
    )(place, *attn_parts, *att_parts)


def project_back(place, back, cosine, sine, tokens, normed, wq, wk, wv, groups, blocks, quarters):
    heads = wq.shape[0]
    pw = wq.shape[2]
    hw = 2 * pw
    rows, width = normed.shape
    own = rows // quarters
    span = heads * hw

    def body(place_ref, back_ref, cos_ref, sin_ref, tok_ref, norm_ref, q_ref, k_ref, v_ref, *refs):
        dx_ref, gain_ref = refs[:2]
        chunk_refs = refs[2:-1]
        grad_ref = refs[-1]
        cos = cos_ref[...]
        sin = sin_ref[...]
        for h in range(heads):
            total = back_ref[h].astype(F32)
            for r in range(1, groups):
                total = total + back_ref[r * heads + h].astype(F32)
            for part in range(3):
                a = total[part * hw : part * hw + pw]
                b = total[part * hw + pw : (part + 1) * hw]
                if part < 2:
                    a, b = a * cos + b * sin, b * cos - a * sin
                at = part * span + h * hw
                grad_ref[at : at + hw] = jnp.concatenate([a, b], axis=0).astype(BF)
        for part in range(3):
            value = dot(norm_ref[...], grad_ref[part * span : (part + 1) * span], 0, 1)
            store_chunks(place_ref, value, chunk_refs[2 * part], chunk_refs[2 * part + 1])
        dx = dot(grad_ref[0:span], q_ref[...], 0, 0)
        dx = dx + dot(grad_ref[span : 2 * span], k_ref[...], 0, 0)
        dx = dx + dot(grad_ref[2 * span :], v_ref[...], 0, 0)
        for j in range(quarters):
            dx_ref[place_ref[2] ^ j] = dx[j * own : (j + 1) * own].astype(BF)
        x = tok_ref[...].astype(F32)
        gain_ref[...] = jnp.sum(dx * (x * rms_scale(x)), axis=0, keepdims=True)

    flat = (span, width)
    chunk = (blocks // 2, width // blocks, span)
    return pl.pallas_call(
        body,
        grid_spec=pltpu.PrefetchScalarGridSpec(
            num_scalar_prefetch=1,
            grid=(1,),
            in_specs=[
                whole(back.shape),
                whole(cosine.shape),
                whole(sine.shape),
                whole(tokens.shape),
                whole(normed.shape),
                whole(flat),
                whole(flat),
                whole(flat),
            ],
            out_specs=[whole((quarters, own, width)), whole((1, width))] + [whole(chunk)] * 6,
            scratch_shapes=[pltpu.VMEM((3 * span, rows), BF)],
        ),
        out_shape=(
            jax.ShapeDtypeStruct((quarters, own, width), BF),
            jax.ShapeDtypeStruct((1, width), F32),
        )
        + (jax.ShapeDtypeStruct(chunk, BF),) * 6,
        compiler_params=pltpu.CompilerParams(vmem_limit_bytes=VMEM_LIMIT),
        name="project_back",
    )(place, back, cosine, sine, tokens, normed, wq.reshape(flat), wk.reshape(flat), wv.reshape(flat))


def after(x, *others):
    return lax.optimization_barrier((x,) + others)[0]


def added(parts):
    total = parts[0].astype(F32)
    for p in parts[1:]:
        total = total + p.astype(F32)
    return total


def flip(x, by, axis):
    size = lax.axis_size(axis)
    return lax.ppermute(x, axis, [(i, i ^ by) for i in range(size)])


def exchange(x, axis):
    return lax.all_to_all(x, axis, 0, 0, tiled=True)


def spread(x, axis):
    size = lax.axis_size(axis)
    return exchange(jnp.broadcast_to(x[None], (size,) + x.shape), axis)


def even_blocks(x):
    size = lax.axis_size("expert")
    return [x] + [flip(x, m, "expert") for m in range(2, size, 2)]


def odd_blocks(evens):
    return flip(evens, 1, "expert")


def paired(evens, odds):
    return added([evens, flip(odds, 1, "expert")]).astype(BF)


def collected(sums):
    return added([sums[0]] + [flip(sums[j], 2 * j, "expert") for j in range(1, sums.shape[0])])


def of_quarters(x):
    quarters = lax.axis_size("tensor")
    return [x] + [flip(x, k, "tensor") for k in range(1, quarters)]


def in_order(place, parts):
    count = len(parts)
    rows, width = parts[0].shape

    def body(place_ref, *refs):
        for k in range(count):
            refs[count][place_ref[2] ^ k] = refs[k][...]

    return pl.pallas_call(
        body,
        grid_spec=pltpu.PrefetchScalarGridSpec(
            num_scalar_prefetch=1,
            grid=(1,),
            in_specs=[whole((rows, width))] * count,
            out_specs=whole((count, rows, width)),
        ),
        out_shape=jax.ShapeDtypeStruct((count, rows, width), parts[0].dtype),
        compiler_params=pltpu.CompilerParams(vmem_limit_bytes=VMEM_LIMIT),
        name="in_order",
    )(place, *parts).reshape(count * rows, width)


def on_device(
    tokens,
    segment_ids,
    expert_ids,
    gate_values,
    expert_slot,
    first_gain,
    second_gain,
    query_weight,
    key_weight,
    value_weight,
    output_weight,
    shared_gate,
    shared_up,
    shared_down,
    routed_gate,
    routed_up,
    routed_down,
    cotangent,
):
    rows, width = tokens.shape
    top = expert_ids.shape[1]
    experts_total = expert_slot.shape[0]
    slots_local = routed_gate.shape[0]
    blocks = lax.axis_size("expert")
    quarters = lax.axis_size("tensor")
    rank = lax.axis_index("expert")
    quarter = lax.axis_index("tensor")
    heads = query_weight.shape[0]
    pair_width = query_weight.shape[2]
    hw = 2 * pair_width
    hd = quarters * hw
    units = blocks * quarters
    groups = units // heads
    own = rows // quarters
    cut = width // blocks
    starts = query_groups(blocks, groups)
    most = max(starts[i + 1] - starts[i] for i in range(groups))
    unit_group = [min(j // heads, groups) for j in range(units)]
    unit = rank * quarters + quarter
    low_table = jnp.array([starts[g] for g in unit_group], jnp.int32)
    high_table = jnp.array([starts[g + 1] if g < groups else starts[g] for g in unit_group], jnp.int32)
    bounds = jnp.stack([low_table[unit], high_table[unit]])
    block_group = jnp.array(
        [max(g for g in range(groups) if starts[g] <= b) for b in range(blocks)], jnp.int32
    )[rank]

    seg_mine = lax.dynamic_slice_in_dim(segment_ids, rank * rows, rows)
    doc_start = jnp.sum((segment_ids[:, None] < seg_mine[None, :]).astype(jnp.int32), axis=0)
    positions = rank * rows + jnp.arange(rows, dtype=jnp.int32) - doc_start
    freq_index = quarter * pair_width + jnp.arange(pair_width, dtype=jnp.int32)
    inverse_freq = 10000.0 ** (-2.0 * freq_index.astype(F32) / HD)
    angles = inverse_freq[:, None] * positions.astype(F32)[None, :]
    cosine = jnp.cos(angles)
    sine = jnp.sin(angles)
    seg_row = segment_ids.reshape(blocks, 1, rows)
    seg_col = jnp.broadcast_to(segment_ids.reshape(blocks, rows, 1), (blocks, rows, 128))

    normed_one, send = project(
        tokens, first_gain, query_weight, key_weight, value_weight, cosine, sine, units, groups
    )
    arrived = exchange(send, BOTH).reshape(blocks, quarters, 3 * hw, rows)

    def across(x):
        return flip(x, 2, "tensor")

    def beside(x):
        return flip(x, 1, "tensor")

    def all_quarters(x, far):
        return (x, beside(x), far, beside(far))

    out_mine = after(output_weight.reshape(heads, hw, width), normed_one)
    out_far = across(out_mine)
    gate_mine = after(routed_gate, out_far)
    gate_far = across(gate_mine)
    arrived = after(arrived, out_far)
    up_mine = after(routed_up, arrived)
    up_far = across(up_mine)
    out_ws = all_quarters(out_mine, out_far)
    out_full = jnp.zeros((heads, quarters, hw, width), BF)
    for k in range(quarters):
        out_full = lax.dynamic_update_slice(out_full, out_ws[k][:, None], (0, quarter ^ k, 0, 0))
    out_full = out_full.reshape(heads * hd, width)

    half = blocks // 2
    place = jnp.stack([rank // 2, rank % 2, quarter, rank])
    own_tokens = lax.dynamic_slice_in_dim(tokens, quarter * own, own).astype(F32)
    own_grads = lax.dynamic_slice_in_dim(cotangent, quarter * own, own)
    own_ids = lax.dynamic_slice_in_dim(expert_ids, quarter * own, own)
    own_gates = lax.dynamic_slice_in_dim(gate_values, quarter * own, own)
    onehot = own_ids[:, :, None] == jnp.arange(experts_total, dtype=jnp.int32)
    own_slots = jnp.sum(jnp.where(onehot, expert_slot[None, None, :], 0), axis=2)
    slot_hot = own_slots[:, :, None] == jnp.arange(experts_total, dtype=jnp.int32)
    dense_gates = jnp.sum(jnp.where(slot_hot, own_gates[:, :, None], 0.0), axis=1)
    lanes = -(-3 * experts_total // 128) * 128
    spare = jnp.zeros((own, lanes - 3 * experts_total), BF)
    own_wide = jnp.concatenate(
        [own_grads] + [p.astype(BF) for p in pieces(dense_gates)] + [spare], axis=1
    )
    grads_even = even_blocks(after(own_wide, arrived))

    attended_units, lse = attend(bounds, arrived, seg_col, seg_row, most)
    attended_units, grads_even = lax.optimization_barrier((attended_units, tuple(grads_even)))
    grads_even = jnp.stack(grads_even)
    grads_odd = odd_blocks(grads_even)
    down_mine = after(routed_down, attended_units)
    down_far = across(down_mine)
    gate_ws = all_quarters(gate_mine, gate_far)
    up_ws = all_quarters(up_mine, up_far)
    down_ws = all_quarters(down_mine, down_far)
    back = exchange(attended_units.reshape(units, own, hd), BOTH)
    back, grads_odd = lax.optimization_barrier((back, grads_odd, out_full, gate_far))[:2]
    attended_heads = lax.dynamic_slice_in_dim(back, block_group * heads, heads)
    attended = attended_heads.transpose(1, 0, 2).reshape(own, heads * hd)
    hidden_state = own_tokens + jnp.dot(attended, out_full, preferred_element_type=F32)
    second_scale = rms_scale(hidden_state)
    normed_two = (hidden_state * second_scale * second_gain).astype(BF)

    rows_in = spread(normed_two, "expert").reshape(blocks * own, width)
    shared_mine = after(jnp.stack([shared_gate, shared_up, shared_down]), normed_two)
    shared_far = across(shared_mine)
    shared_near = beside(shared_mine)
    shared_ws = (shared_mine, shared_near, shared_far, beside(shared_far))

    total_rows = blocks * own
    step = min(total_rows, 512)
    spans = [slice(c, c + step) for c in range(0, total_rows, step)]
    prods = [
        down_products(place, grads_even, grads_odd, c.start // own // 2, step, width, down_ws)
        for c in spans
    ]
    firsts = [
        experts_first(place, rows_in[c], p[0], p[2], gate_ws, up_ws, experts_total)
        for c, p in zip(spans, prods)
    ]
    grads_in = jnp.concatenate([p[1] for p in prods], axis=0)
    grad_rows = jnp.concatenate([f[4] for f in firsts], axis=0)
    grad_home = exchange(grad_rows.reshape(blocks, own, width), "expert")

    seconds = []
    for c, f in zip(spans, firsts):
        act = lax.optimization_barrier((f[0], shared_far, shared_near))[0]
        seconds.append(
            experts_second(place, rows_in[c], grads_in[c], f[3], act, f[1], f[2], down_ws, own)
        )
    if len(seconds) == 1:
        out_low, out_high = seconds[0][:2]
        parts = seconds[0][2:]
    else:
        order = (rank // (step // own)) ^ jnp.arange(len(seconds), dtype=jnp.int32)
        out_low, out_high = (
            jnp.stack([s[i] for s in seconds])[order].reshape(half, own, width + lanes)
            for i in range(2)
        )
        parts = [added([s[2 + k] for s in seconds]).astype(BF) for k in range(quarters + 2)]
    shared_out, shared_dx = shared_own(after(normed_two, out_low), own_grads, shared_ws)
    att_parts = of_quarters(after(attended, shared_far))

    to_far = [added([parts[2][0], beside(parts[3])]).astype(BF)]
    grad_home, to_far[0], att_parts = lax.optimization_barrier(
        (grad_home, to_far[0], tuple(att_parts), shared_dx)
    )[:3]
    grad_norm_two = jnp.sum(grad_home.astype(F32), axis=0) + shared_dx
    grad_full = own_grads.astype(F32)
    grad_second, second_gain_local = norm_backward(
        grad_norm_two, hidden_state, second_scale, second_gain
    )
    grad_hidden = grad_full + grad_second
    grad_attn = grad_hidden.astype(BF)
    grad_attended = jnp.einsum(
        "td,hcd->htc", grad_attn, out_full.reshape(heads, hd, width), preferred_element_type=F32
    ).astype(BF)
    out_got = flip(out_high, 1, "expert")
    grad_attended, out_got = lax.optimization_barrier((grad_attended, out_got))
    do_send = jnp.concatenate([grad_attended] * groups + [grad_attended[: units - groups * heads]], axis=0)
    do_units = exchange(do_send, BOTH).reshape(blocks, rows, hd)

    grad_attn_sent = after(grad_attn, do_send)
    attn_parts = of_quarters(grad_attn_sent)
    from_near = beside(after(parts[4], do_send))
    proj_low, proj_high = output_grads(
        place, attn_parts, att_parts, heads, hw, blocks
    )
    out_pairs = added([out_low, after(out_got, proj_low)]).astype(BF)
    routed_far = [across(lax.optimization_barrier((to_far[0], tuple(attn_parts)))[0])]
    to_far.append(added([parts[2][1], after(from_near, proj_low)]).astype(BF))
    do_units, out_pairs, to_far[1] = lax.optimization_barrier(
        (do_units, out_pairs, to_far[1], proj_low)
    )[:3]

    grad_units = attend_back(bounds, arrived, seg_col, seg_row, lse, do_units, most)
    out_home = collected(out_pairs)
    proj_pairs = paired(proj_low, proj_high)
    grad_units, routed_far[0] = lax.optimization_barrier(
        (grad_units, routed_far[0], out_home, proj_pairs)
    )[:2]
    far_one = across(after(to_far[1], routed_far[0]))
    back_grads = exchange(grad_units.reshape(units, 3 * hw, rows), BOTH)

    to_far.append(added([parts[2][2], beside(after(parts[5], grad_units))]).astype(BF))
    rows_late, grads_late = lax.optimization_barrier((rows_in, grads_in, grad_units))[:2]
    rows_cut = lax.dynamic_slice_in_dim(rows_late, rank * cut, cut, axis=1)
    grads_cut = lax.dynamic_slice_in_dim(grads_late, rank * cut, cut, axis=1)
    shared_parts = [
        shared_grads(rows_late[c], grads_late[c], rows_cut[c], grads_cut[c], shared_ws) for c in spans
    ]
    shared_parts = shared_parts[0] if len(spans) == 1 else added(shared_parts).astype(BF)
    shared_sent, far_one = lax.optimization_barrier((shared_parts, far_one))
    shared_gots = [flip(shared_sent[k], k, "tensor") for k in range(1, quarters)]
    near = beside(after(parts[1], grad_units))
    out_parts = [flip(after(proj_pairs[j], shared_parts), 2 * j, "expert") for j in range(1, half)]
    moe_out = out_home[:, :width] + shared_out
    slot_sums = out_home[:, width : width + 3 * experts_total].reshape(own, 3, experts_total)
    slot_sums = jnp.sum(slot_sums, axis=1)
    gate_grad = jnp.sum(jnp.where(slot_hot, slot_sums[:, None, :], 0.0), axis=2)
    final = [(hidden_state + moe_out).astype(BF)] + [p.astype(BF) for p in pieces(gate_grad)]
    final = jnp.concatenate(final + [jnp.zeros((own, 128 - 3 * top), BF)], axis=1)
    final = in_order(place, of_quarters(after(final, grad_units)))
    output = final[:, :width]
    gate_grad = jnp.sum(final[:, width : width + 3 * top].reshape(rows, 3, top).astype(F32), axis=1)
    back_grads, near, out_parts = lax.optimization_barrier((back_grads, near, tuple(out_parts), shared_parts, output))[:3]

    back_out = project_back(
        place,
        back_grads,
        cosine,
        sine,
        tokens,
        normed_one,
        query_weight,
        key_weight,
        value_weight,
        groups,
        blocks,
        quarters,
    )
    gains = jnp.stack([back_out[1][0], second_gain_local]).reshape(2, blocks, cut).transpose(1, 0, 2)
    gains = jnp.broadcast_to(gains[:, None], (blocks, quarters, 2, cut)).reshape(units, 2, cut)
    gains = exchange(gains, BOTH)
    dx_parts = [back_out[0][0]] + [flip(back_out[0][k], k, "tensor") for k in range(1, quarters)]
    pair_q = paired(back_out[2], back_out[3])
    pair_k = paired(back_out[4], after(back_out[5], pair_q))
    dx_parts, pair_q = lax.optimization_barrier((tuple(dx_parts), pair_q))
    grad_one = added(dx_parts)
    far_two = across(after(to_far[2], dx_parts[1]))
    out_grad = added([proj_pairs[0], *lax.optimization_barrier((out_parts, pair_q))[0]])
    routed = [added([parts[0][0], near[0], after(routed_far[0], pair_q)])]
    shared_gots = lax.optimization_barrier((tuple(shared_gots), pair_k))[0]
    shared = added([shared_parts[0], *shared_gots])
    pair_v = paired(back_out[6], after(back_out[7], pair_k))
    routed.append(added([parts[0][1], near[1], after(far_one, pair_k)]))
    pair_v, routed, shared = lax.optimization_barrier((pair_v, routed, shared))
    routed.append(added([parts[0][2], near[2], after(far_two, pair_v)]))
    qkv_grads = [collected(p) for p in (pair_q, pair_k, pair_v)]
    first_scale = rms_scale(own_tokens)
    grad_first, _ = norm_backward(grad_one, own_tokens, first_scale, first_gain)
    input_mine = after((grad_hidden + grad_first).astype(BF), pair_k)
    input_parts, routed[2] = lax.optimization_barrier((tuple(of_quarters(input_mine)), routed[2]))
    input_grad = in_order(place, input_parts)
    gains = jnp.sum(after(gains, pair_v), axis=0)

    weight_shape = (heads, 2, pair_width, cut)
    return (
        output,
        input_grad,
        gate_grad,
        gains[0],
        gains[1],
        qkv_grads[0].T.reshape(weight_shape),
        qkv_grads[1].T.reshape(weight_shape),
        qkv_grads[2].T.reshape(weight_shape),
        out_grad.T.reshape(weight_shape),
        shared[0],
        shared[1],
        shared[2],
        routed[0],
        routed[1],
        routed[2],
    )


def solution(mesh):
    placed = (
        P("expert", None),
        P(),
        P("expert", None),
        P("expert", None),
        P(),
        P(),
        P(),
        P(None, None, "tensor", None),
        P(None, None, "tensor", None),
        P(None, None, "tensor", None),
        P(None, None, "tensor", None),
        P("tensor", None),
        P("tensor", None),
        P("tensor", None),
        P("expert", "tensor", None),
        P("expert", "tensor", None),
        P("expert", "tensor", None),
        P("expert", None),
    )
    return jax.shard_map(
        on_device,
        mesh=mesh,
        in_specs=placed,
        out_specs=(
            P("expert", None),
            P("expert", None),
            P("expert", None),
            P("expert"),
            P("expert"),
            P(None, None, "tensor", "expert"),
            P(None, None, "tensor", "expert"),
            P(None, None, "tensor", "expert"),
            P(None, None, "tensor", "expert"),
            P("tensor", "expert"),
            P("tensor", "expert"),
            P("tensor", "expert"),
            P("expert", "tensor", None),
            P("expert", "tensor", None),
            P("expert", "tensor", None),
        ),
        check_vma=False,
    )
```
